32 devices in a mesh: grp: 2 (over x), mode: 4 (over y, core), space: 4 (over z).
Axes of the slice: x: 2, y: 2, z: 4, core: 2. Of those that a mesh axis runs over, the one named last changes fastest.
Arguments:
- electrons: bfloat16 [1024, 64, 128], P('mode', ('grp', 'space')), parts along dimension 1, may hold values from -6 to 6
- phonons: bfloat16 [2048, 64, 128], P('mode', ('grp', 'space')), parts along dimension 1, may hold values from -6 to 6
- emission: bfloat16 [2048, 1024], P('mode'), may hold values from -0.1875 to 0.1875
- absorption: bfloat16 [1024, 2048], P('mode'), may hold values from -0.125 to 0.125
- block_coupling: bfloat16 [2048, 12, 128], P('mode'), may hold values from -0.15625 to 0.15625
- block_cols: int32 [16, 12], P('mode'), may hold values from -1 to 15, as said below
- upwind: int32 [64, 128], P(('grp', 'space')), parts along dimension 0, may hold values from 0 to 1
- speed: float32 [1024], P('mode'), may hold values from 0.1 to 0.9
- diffusion: float32 [2048], P('mode'), may hold values from 0.02 to 0.24
- electron_rate: float32 [1024], P('mode'), may hold values from 0.2 to 2
- phonon_rate: float32 [2048], P('mode'), may hold values from 0.2 to 2
Outputs:
- electrons_out: bfloat16 [1024, 64, 128], P('mode', ('grp', 'space')), parts along dimension 1
- phonons_out: bfloat16 [2048, 64, 128], P('mode', ('grp', 'space')), parts along dimension 1
The draws below stay inside these ranges and needn't reach their ends.
There are 2 independent parts, one for each index of `grp`. The reference program is written for one: setup_inputs(seed, part) draws one part's arguments, and reference() takes and returns one part's arrays. A program takes and returns all parts, laid end to end along the dimension named above; an argument that names none is the same for every part. Nothing has to cross between parts.
Inputs may be any that keep to these rules, and one draw needn't show every extreme that they name: `block_cols`: each row lists distinct block indices in its first slots and -1 in all later slots; every row has at least one block, one row fills all 12 slots, one of them naming block 15, and one row has a single block.
All inputs are finite; a program needn't handle non-finite values.
Results may differ from the reference program's by a relative error of at most 0.0065.
Values may be sent and summed in bfloat16 or wider, within the bound.
No kernel may reach another device: no remote copies, remote signals or barrier semaphores. Data moves between devices by JAX's collectives and lax.ppermute only.
A program may use at most 64 MiB of HBM per device.

```python
import math
import jax
import jax.numpy as jnp
from jax import lax

NE = 1024
NM = 2048
BLK = 128
S = 12
ITERS = 2
NY = 128
NX = 32
NB = 16


def draw_block_cols(key, part):
    base = jax.random.fold_in(key, 7)
    first, second, third, fourth = jax.random.split(base, 4)
    counts = jax.random.randint(first, (NB,), 1, S + 1)
    full_row = jax.random.randint(second, (), 0, NB)
    single_row = (full_row + 1 + jax.random.randint(fourth, (), 0, NB - 1)) % NB
    rows = jnp.arange(NB)
    counts = jnp.where(rows == full_row, S, counts)
    counts = jnp.where(rows == single_row, 1, counts)
    orders = jax.vmap(lambda k: jax.random.permutation(k, NB))(jax.random.split(third, NB))
    full_order = orders[full_row]
    where_last = jnp.argmax(full_order == NB - 1)
    rolled = jnp.roll(full_order, -where_last)
    orders = jnp.where((rows == full_row)[:, None], rolled[None, :], orders)[:, :S]
    slots = jnp.arange(S)[None, :]
    return jnp.where(slots < counts[:, None], orders, -1).astype(jnp.int32)


def with_ends(entries, own_key, low, largest):
    longest = entries.shape.index(max(entries.shape))
    spots = []
    for shift in (0, 1):
        where = [jax.random.randint(jax.random.fold_in(own_key, axis), (), 0, length) for axis, length in enumerate(entries.shape)]
        where[longest] = (where[longest] + shift) % entries.shape[longest]
        spots.append(tuple(where))
    return entries.at[spots[0]].set(low).at[spots[1]].set(largest)


def block_scale(rng, shape, pieces, least, largest):
    level = 1.0
    for axis_at, blocks in pieces:
        draws = jax.random.uniform(jax.random.fold_in(jax.random.fold_in(rng, 6), axis_at), (blocks,), jnp.float32, least / len(pieces), largest / len(pieces))
        level = level * jnp.repeat(jnp.exp(draws), shape[axis_at] // blocks).reshape((-1,) + (1,) * (len(shape) - 1 - axis_at))
    return level


def gaussian(own_key, shape, deviation, most, cuts=(), kind=jnp.bfloat16):
    array = jax.random.normal(own_key, shape, jnp.float32) * deviation
    if len(cuts) > 0:
        array = block_scale(own_key, shape, cuts, -0.22, 0.18) * array
    return jnp.clip(array, min=-most, max=most).astype(kind)


def setup_inputs(seed: int = 0, part: int = 0) -> dict:
    seeds = jax.random.split(jax.random.key(seed), 12)
    part_keys = jax.random.split(jax.random.fold_in(seeds[11], part), 12)
    electrons = gaussian(part_keys[0], (NE, NX, NY), 1.0, 6.0, ((0, 4), (1, 4)))
    phonons = gaussian(part_keys[1], (NM, NX, NY), 1.0, 6.0, ((0, 4), (1, 4)))
    emission = gaussian(seeds[2], (NM, NE), NE ** -0.5, 0.1875, ((0, 4),))
    absorption = gaussian(seeds[3], (NE, NM), NM ** -0.5, 0.125, ((0, 4),))
    block_coupling = gaussian(seeds[4], (NM, S, BLK), (S * BLK) ** -0.5, 0.15625, ((0, 4),))
    block_cols = draw_block_cols(jax.random.fold_in(seeds[11], 71), part)
    upwind = with_ends(jax.random.randint(part_keys[6], (NX, NY), 0, 2), jax.random.fold_in(part_keys[6], 1), 0, 1).astype(jnp.int32)
    speed = jnp.clip(0.1 + 0.79999997 * jax.random.uniform(seeds[7], (NE,), jnp.float32) ** block_scale(seeds[7], (NE,), ((0, 4),), -0.2, 0.2), 0.1, 0.9)
    diffusion = jnp.clip(0.02 + 0.22 * jax.random.uniform(seeds[8], (NM,), jnp.float32) ** block_scale(seeds[8], (NM,), ((0, 4),), -0.2, 0.2), 0.02, 0.24)
    electron_rate = jnp.clip(jnp.exp(math.log(2.0) - 2.3025851 * jax.random.uniform(seeds[9], (NE,), jnp.float32) ** block_scale(seeds[9], (NE,), ((0, 4),), -0.2, 0.2)), 0.2, 2.0)
    phonon_rate = jnp.clip(jnp.exp(math.log(2.0) - 2.3025851 * jax.random.uniform(seeds[10], (NM,), jnp.float32) ** block_scale(seeds[10], (NM,), ((0, 4),), -0.2, 0.2)), 0.2, 2.0)
    return dict(electrons=electrons, phonons=phonons, emission=emission, absorption=absorption, block_coupling=block_coupling, block_cols=block_cols, upwind=upwind, speed=speed, diffusion=diffusion, electron_rate=electron_rate, phonon_rate=phonon_rate)


def block_term(phonons_flat, block_coupling, block_cols):
    grouped = phonons_flat.reshape(NB, BLK, NX * NY)
    kernel = block_coupling.reshape(NB, BLK, S, BLK)

    def one_row(index):
        cols = block_cols[index]
        valid = (cols >= 0).astype(jnp.float32)
        picked = grouped[jnp.clip(cols, 0, NB - 1).astype(jnp.int32)].astype(jnp.float32)
        picked = picked * valid[:, None, None]
        return jnp.einsum("isj,sjc->ic", kernel[index].astype(jnp.float32), picked)

    rows = lax.map(one_row, jnp.arange(NB, dtype=jnp.int32))
    return rows.reshape(NM, NX * NY)


def reference(electrons, phonons, emission, absorption, block_coupling, block_cols, upwind, speed, diffusion, electron_rate, phonon_rate):
    state_e = electrons
    state_p = phonons
    upward = (upwind == 1)[None]
    for step in range(ITERS):
        field_e = state_e.astype(jnp.float32)
        field_p = state_p.astype(jnp.float32)
        lower = jnp.pad(field_e, ((0, 0), (1, 0), (0, 0)))[:, :-1]
        higher = jnp.pad(field_e, ((0, 0), (0, 1), (0, 0)))[:, 1:]
        f_up = jnp.where(upward, lower, higher)
        padded = jnp.pad(field_p, ((0, 0), (1, 1), (1, 1)))
        lap = padded[:, :-2, 1:-1] + padded[:, 2:, 1:-1] + padded[:, 1:-1, :-2] + padded[:, 1:-1, 2:] - 4.0 * field_p
        flat_e = state_e.reshape(NE, NX * NY)
        flat_p = state_p.reshape(NM, NX * NY)
        emit = jnp.dot(emission, flat_e, preferred_element_type=jnp.float32).reshape(NM, NX, NY)
        gain = jnp.dot(absorption, flat_p, preferred_element_type=jnp.float32).reshape(NE, NX, NY)
        scatter = block_term(flat_p, block_coupling, block_cols).reshape(NM, NX, NY)
        new_e = (field_e - speed[:, None, None] * (field_e - f_up) + 0.5 * gain) / (1.0 + electron_rate[:, None, None])
        new_p = (field_p + diffusion[:, None, None] * lap + 0.5 * (emit + scatter)) / (1.0 + phonon_rate[:, None, None])
        state_e = new_e.astype(jnp.bfloat16)
        state_p = new_p.astype(jnp.bfloat16)
    return state_e, state_p
```

```python
import jax
import jax.numpy as jnp
from jax import lax
from jax.experimental import pallas as pl
from jax.experimental.pallas import tpu as pltpu
from jax.sharding import PartitionSpec as P

NM = 2048
BLK = 128
ITERS = 2
CORES = 2
CHUNKS = 2


def swap_cores(x):
    n = lax.axis_size("mode")
    return lax.ppermute(x, "mode", [(i, i ^ 1) for i in range(n)])


def from_chip(x, offset):
    n = lax.axis_size("mode")
    return lax.ppermute(x, "mode", [((i + CORES * offset) % n, i) for i in range(n)])


def from_space(x, step):
    n = lax.axis_size("space")
    pairs = [(i, i - step) for i in range(n) if 0 <= i - step < n]
    return lax.ppermute(x, "space", pairs)


def step_kernel(e, p, pieces, width, ny, source_ref, *refs):
    piece_refs = refs[:pieces]
    (low_ref, high_ref, up_ref, emission_ref, absorption_ref, dense_ref,
     speed_ref, diffusion_ref, e_rate_ref, p_rate_ref, out_ref, se_ref, sp_ref) = refs[pieces:]
    for j, piece in enumerate(piece_refs):
        owner = source_ref[j]
        se_ref[pl.ds(pl.multiple_of(owner * e, e), e), :] = piece[0:e, :]
        sp_ref[pl.ds(pl.multiple_of(owner * p, p), p), :] = piece[e:, :]
    own_ref = piece_refs[0]
    tile = min(p, 256)

    def around(rows):
        own = own_ref[rows, :].astype(jnp.float32)
        low = low_ref[rows, :].astype(jnp.float32)
        high = high_ref[rows, :].astype(jnp.float32)
        if width == ny:
            return own, low, high
        lower = jnp.concatenate([low, own[:, : width - ny]], axis=1)
        higher = jnp.concatenate([own[:, ny:], high], axis=1)
        return own, lower, higher

    own, lower, higher = around(pl.ds(0, e))
    gain = jnp.dot(absorption_ref[...], sp_ref[...], preferred_element_type=jnp.float32)
    f_up = jnp.where(up_ref[...] == 1, lower, higher)
    out_ref[0:e, :] = (
        (own - speed_ref[...] * (own - f_up) + 0.5 * gain) / (1.0 + e_rate_ref[...])
    ).astype(jnp.bfloat16)

    @pl.loop(0, p // tile)
    def _(i):
        at = pl.multiple_of(i * tile, tile)
        source = jnp.dot(
            emission_ref[pl.ds(at, tile), :], se_ref[...], preferred_element_type=jnp.float32
        ) + jnp.dot(dense_ref[pl.ds(at, tile), :], sp_ref[...], preferred_element_type=jnp.float32)
        own, lower, higher = around(pl.ds(pl.multiple_of(e + at, e), tile))
        column = lax.broadcasted_iota(jnp.int32, (tile, ny), 1)
        left, right = [], []
        for r in range(width // ny):
            row = own[:, r * ny : (r + 1) * ny]
            left.append(jnp.where(column == 0, 0.0, pltpu.roll(row, 1, 1)))
            right.append(jnp.where(column == ny - 1, 0.0, pltpu.roll(row, ny - 1, 1)))
        left, right = jnp.concatenate(left, axis=1), jnp.concatenate(right, axis=1)
        lap = lower + higher + left + right - 4.0 * own
        out_ref[pl.ds(pl.multiple_of(e + at, e), tile), :] = (
            (own + diffusion_ref[pl.ds(at, tile), :] * lap + 0.5 * source)
            / (1.0 + p_rate_ref[pl.ds(at, tile), :])
        ).astype(jnp.bfloat16)


def on_device(
    electrons,
    phonons,
    emission,
    absorption,
    block_coupling,
    block_cols,
    upwind,
    speed,
    diffusion,
    electron_rate,
    phonon_rate,
):
    e, nx, ny = electrons.shape
    p = phonons.shape[0]
    rows = e + p
    n = lax.axis_size("mode")
    chips = n // CORES
    slots = block_coupling.shape[1]
    b_rows = p // BLK
    kernel = block_coupling.reshape(b_rows, BLK, slots, BLK)
    block_ids = jnp.arange(NM // BLK, dtype=jnp.int32)
    hits = (block_cols[:, :, None] == block_ids[None, None, :]).astype(jnp.bfloat16)
    dense = jnp.einsum(
        "bsk,bisj->bikj", hits, kernel, preferred_element_type=jnp.float32
    ).astype(jnp.bfloat16).reshape(p, NM)

    tall = nx // CHUNKS
    width = tall * ny
    me = lax.axis_index("mode")
    chip, core = me // CORES, me % CORES
    sources = jnp.stack(
        [((chip + d) % chips) * CORES + (core ^ c) for d in range(chips) for c in range(CORES)]
    ).astype(jnp.int32)
    speed, diffusion = speed[:, None], diffusion[:, None]
    electron_rate, phonon_rate = electron_rate[:, None], phonon_rate[:, None]
    ups = [upwind[k * tall : (k + 1) * tall].reshape(1, width) for k in range(CHUNKS)]

    def step(pieces, low, high, up):
        whole = pl.BlockSpec(memory_space=pltpu.VMEM)
        operands = (*pieces, low, high, up, emission, absorption, dense, speed, diffusion, electron_rate, phonon_rate)
        return pl.pallas_call(
            lambda *refs: step_kernel(e, p, n, width, ny, *refs),
            out_shape=jax.ShapeDtypeStruct((rows, width), jnp.bfloat16),
            in_specs=[pl.BlockSpec(memory_space=pltpu.SMEM)] + [whole] * len(operands),
            out_specs=whole,
            scratch_shapes=[
                pltpu.VMEM((n * e, width), jnp.bfloat16),
                pltpu.VMEM((n * p, width), jnp.bfloat16),
            ],
            compiler_params=pltpu.CompilerParams(vmem_limit_bytes=32 << 20),
            cost_estimate=pl.CostEstimate(
                flops=2 * width * n * (e * p * 2 + p * p),
                bytes_accessed=2 * ((n + 1) * rows * width + n * (2 * e * p + p * p)),
                transcendentals=0,
            ),
            name="step",
        )(sources, *operands)

    chunks = [
        jnp.concatenate(
            [x[:, k * tall : (k + 1) * tall].reshape(-1, width) for x in (electrons, phonons)], axis=0
        )
        for k in range(CHUNKS)
    ]
    for _ in range(ITERS):
        low = from_space(chunks[-1][:, width - ny :], -1)
        high = from_space(chunks[0][:, :ny], 1)
        edges = [low] + [c[:, width - ny :] for c in chunks[:-1]], [c[:, :ny] for c in chunks[1:]] + [high]
        new = []
        for k, chunk in enumerate(chunks):
            pieces = [chunk, swap_cores(chunk)]
            for d in range(1, chips):
                far = from_chip(chunk, d)
                pieces += [far, swap_cores(far)]
            new.append(step(pieces, edges[0][k], edges[1][k], ups[k]))
        chunks = new
    state = jnp.concatenate([c.reshape(rows, tall, ny) for c in chunks], axis=1)
    return state[:e], state[e:]


def solution(mesh):
    placed = (
        P("mode", ("grp", "space"), None),
        P("mode", ("grp", "space"), None),
        P("mode", None),
        P("mode", None),
        P("mode", None, None),
        P("mode", None),
        P(("grp", "space"), None),
        P("mode"),
        P("mode"),
        P("mode"),
        P("mode"),
    )
    return jax.shard_map(
        on_device,
        mesh=mesh,
        in_specs=placed,
        out_specs=(P("mode", ("grp", "space"), None), P("mode", ("grp", "space"), None)),
        check_vma=False,
    )
```

```python
import jax
import jax.numpy as jnp
from jax import lax
from jax.experimental import pallas as pl
from jax.experimental.pallas import tpu as pltpu
from jax.sharding import PartitionSpec as P

NM = 2048
BLK = 128
ITERS = 2
CORES = 2
CHUNKS = 2

VMEM = pl.BlockSpec(memory_space=pltpu.VMEM)


def swap_cores(x):
    n = lax.axis_size("mode")
    return lax.ppermute(x, "mode", [(i, i ^ 1) for i in range(n)])


def from_chip(x, offset):
    n = lax.axis_size("mode")
    return lax.ppermute(x, "mode", [((i + CORES * offset) % n, i) for i in range(n)])


def from_space(x, step):
    n = lax.axis_size("space")
    pairs = [(i, i - step) for i in range(n) if 0 <= i - step < n]
    return lax.ppermute(x, "space", pairs)


def after(x, *others):
    return lax.optimization_barrier((x, *others))[0]


def flatten_kernel(e, p, nx, ny, e_ref, p_ref, *refs):
    outs, low_ref, high_ref, wide_ref = refs[:-3], refs[-3], refs[-2], refs[-1]
    tall = nx // len(outs)
    for x_ref, base, count in ((e_ref, 0, e), (p_ref, e, p)):
        tile = min(count, 64)

        @pl.loop(0, count // tile)
        def _(i):
            at = pl.multiple_of(i * tile, tile)
            wide_ref[0 : tile * nx, :] = x_ref[pl.ds(pl.multiple_of(at * nx, tile * nx), tile * nx), :].astype(jnp.float32)
            to = pl.ds(pl.multiple_of(base + at, tile), tile)
            for r in range(nx):
                row = wide_ref[pl.ds(r, tile, stride=nx), :].astype(jnp.bfloat16)
                k, c = r // tall, r % tall
                outs[k][to, c * ny : (c + 1) * ny] = row
                if r == 0:
                    low_ref[to, :] = row
                if r == nx - 1:
                    high_ref[to, :] = row


def flatten(electrons, phonons):
    e, nx, ny = electrons.shape
    p = phonons.shape[0]
    chunk = jax.ShapeDtypeStruct((e + p, nx // CHUNKS * ny), jnp.bfloat16)
    edge = jax.ShapeDtypeStruct((e + p, ny), jnp.bfloat16)
    out = pl.pallas_call(
        lambda *refs: flatten_kernel(e, p, nx, ny, *refs),
        out_shape=(chunk,) * CHUNKS + (edge, edge),
        in_specs=[VMEM, VMEM],
        out_specs=(VMEM,) * (CHUNKS + 2),
        scratch_shapes=[pltpu.VMEM((64 * nx, ny), jnp.float32)],
        compiler_params=pltpu.CompilerParams(vmem_limit_bytes=8 << 20),
        cost_estimate=pl.CostEstimate(flops=0, bytes_accessed=4 * (e + p) * nx * ny, transcendentals=0),
        name="flatten",
    )(electrons.reshape(e * nx, ny), phonons.reshape(p * nx, ny))
    return list(out[:CHUNKS]), out[-2], out[-1]


def step_kernel(e, p, pieces, width, ny, nx, last, edge, source_ref, *refs):
    piece_refs, refs = refs[:pieces], refs[pieces:]
    (low_ref, high_ref, up_ref, emission_ref, absorption_ref, dense_ref,
     speed_ref, diffusion_ref, e_rate_ref, p_rate_ref), refs = refs[:10], refs[10:]
    if last:
        done_refs, refs = refs[: CHUNKS - 1], refs[CHUNKS - 1 :]
        e_out_ref, p_out_ref, se_ref, sp_ref, wide_ref = refs
    else:
        out_ref, edge_ref, se_ref, sp_ref = refs if edge is not None else (refs[0], None, *refs[1:])
    for j, piece in enumerate(piece_refs):
        owner = source_ref[j]
        se_ref[pl.ds(pl.multiple_of(owner * e, e), e), :] = piece[0:e, :]
        sp_ref[pl.ds(pl.multiple_of(owner * p, p), p), :] = piece[e:, :]
    own_ref = piece_refs[0]
    tile = min(p, 256)

    def around(rows):
        own = own_ref[rows, :].astype(jnp.float32)
        low = low_ref[rows, low_ref.shape[1] - ny :].astype(jnp.float32)
        high = high_ref[rows, :ny].astype(jnp.float32)
        lower = jnp.concatenate([low, own[:, : width - ny]], axis=1) if width > ny else low
        higher = jnp.concatenate([own[:, ny:], high], axis=1) if width > ny else high
        return own, lower, higher

    def store(new, at, count, base):
        rows = pl.ds(pl.multiple_of(base + at, count), count)
        if not last:
            new = new.astype(jnp.bfloat16)
            out_ref[rows, :] = new
            if edge is not None:
                edge_ref[rows, :] = new[:, edge * ny : (edge + 1) * ny]
            return
        tall = width // ny
        for k, done in enumerate(done_refs):
            old = done[rows, :].astype(jnp.float32)
            for r in range(tall):
                wide_ref[pl.ds(k * tall + r, count, stride=nx), :] = old[:, r * ny : (r + 1) * ny]
        for r in range(tall):
            wide_ref[pl.ds(nx - tall + r, count, stride=nx), :] = new[:, r * ny : (r + 1) * ny]
        to = p_out_ref if base else e_out_ref
        to[pl.ds(pl.multiple_of(at * nx, count * nx), count * nx), :] = wide_ref[0 : count * nx, :].astype(jnp.bfloat16)

    own, lower, higher = around(pl.ds(0, e))
    gain = jnp.dot(absorption_ref[...], sp_ref[...], preferred_element_type=jnp.float32)
    f_up = jnp.where(up_ref[...] == 1, lower, higher)
    new = (own - speed_ref[...] * (own - f_up) + 0.5 * gain) / (1.0 + e_rate_ref[...])
    store(new, 0, e, 0)

    @pl.loop(0, p // tile)
    def _(i):
        at = pl.multiple_of(i * tile, tile)
        source = jnp.dot(
            emission_ref[pl.ds(at, tile), :], se_ref[...], preferred_element_type=jnp.float32
        ) + jnp.dot(dense_ref[pl.ds(at, tile), :], sp_ref[...], preferred_element_type=jnp.float32)
        own, lower, higher = around(pl.ds(pl.multiple_of(e + at, e), tile))
        column = lax.broadcasted_iota(jnp.int32, (tile, ny), 1)
        left, right = [], []
        for r in range(width // ny):
            row = own[:, r * ny : (r + 1) * ny]
            left.append(jnp.where(column == 0, 0.0, pltpu.roll(row, 1, 1)))
            right.append(jnp.where(column == ny - 1, 0.0, pltpu.roll(row, ny - 1, 1)))
        left, right = jnp.concatenate(left, axis=1), jnp.concatenate(right, axis=1)
        lap = lower + higher + left + right - 4.0 * own
        new = (own + diffusion_ref[pl.ds(at, tile), :] * lap + 0.5 * source) / (1.0 + p_rate_ref[pl.ds(at, tile), :])
        store(new, at, tile, e)


def on_device(
    electrons,
    phonons,
    emission,
    absorption,
    block_coupling,
    block_cols,
    upwind,
    speed,
    diffusion,
    electron_rate,
    phonon_rate,
):
    e, nx, ny = electrons.shape
    p = phonons.shape[0]
    rows = e + p
    n = lax.axis_size("mode")
    chips = n // CORES
    slots = block_coupling.shape[1]
    b_rows = p // BLK
    tall = nx // CHUNKS
    width = tall * ny

    chunks, first, final = flatten(electrons, phonons)
    block_coupling = after(block_coupling, chunks[0])
    kernel = block_coupling.reshape(b_rows, BLK, slots, BLK)
    block_ids = jnp.arange(NM // BLK, dtype=jnp.int32)
    hits = (block_cols[:, :, None] == block_ids[None, None, :]).astype(jnp.bfloat16)
    dense = jnp.einsum(
        "bsk,bisj->bikj", hits, kernel, preferred_element_type=jnp.float32
    ).astype(jnp.bfloat16).reshape(p, NM)

    me = lax.axis_index("mode").astype(jnp.uint32)
    chip, core = me // CORES, me % CORES
    sources = jnp.stack(
        [((chip + d) % chips) * CORES + (core ^ c) for d in range(chips) for c in range(CORES)]
    ).astype(jnp.int32)
    speed, diffusion = speed[:, None], diffusion[:, None]
    electron_rate, phonon_rate = electron_rate[:, None], phonon_rate[:, None]
    ups = [upwind[k * tall : (k + 1) * tall].reshape(1, width) for k in range(CHUNKS)]

    def step(pieces, low, high, up, edge, done):
        last = bool(done)
        operands = (*pieces, low, high, up, emission, absorption, dense, speed, diffusion, electron_rate, phonon_rate, *done)
        scratch = [pltpu.VMEM((n * e, width), jnp.bfloat16), pltpu.VMEM((n * p, width), jnp.bfloat16)]
        if last:
            out = (jax.ShapeDtypeStruct((e * nx, ny), jnp.bfloat16), jax.ShapeDtypeStruct((p * nx, ny), jnp.bfloat16))
            scratch.append(pltpu.VMEM((max(e, min(p, 256)) * nx, ny), jnp.float32))
        else:
            out = (jax.ShapeDtypeStruct((rows, width), jnp.bfloat16),)
            if edge is not None:
                out += (jax.ShapeDtypeStruct((rows, ny), jnp.bfloat16),)
        return pl.pallas_call(
            lambda *refs: step_kernel(e, p, n, width, ny, nx, last, edge, *refs),
            out_shape=out,
            in_specs=[pl.BlockSpec(memory_space=pltpu.SMEM)] + [VMEM] * len(operands),
            out_specs=(VMEM,) * len(out),
            scratch_shapes=scratch,
            compiler_params=pltpu.CompilerParams(vmem_limit_bytes=20 << 20),
            cost_estimate=pl.CostEstimate(
                flops=1000,
                bytes_accessed=1000,
                transcendentals=0,
            ),
            name="step",
        )(sources, *operands)

    wait_for = dense
    for i in range(ITERS):
        low, high = from_space(final, -1), from_space(first, 1)
        swapped = [swap_cores(c) for c in chunks]
        far = [[from_chip(c, d) for d in range(1, chips)] for c in chunks]
        new = []
        for k, chunk in enumerate(chunks):
            pieces = [chunk, swapped[k]]
            for f in far[k]:
                f = after(f, wait_for)
                pieces += [f, swap_cores(f)]
            before = low if k == 0 else chunks[k - 1]
            behind = high if k == CHUNKS - 1 else chunks[k + 1]
            final_step = i == ITERS - 1
            edge = None if final_step else {0: 0, CHUNKS - 1: tall - 1}.get(k)
            out = step(pieces, before, behind, ups[k], edge, new if final_step and k == CHUNKS - 1 else [])
            if edge is not None:
                first, final = (out[1], final) if k == 0 else (first, out[1])
            new.append(out[0])
            wait_for = out[0]
        chunks = new
    return out[0].reshape(e, nx, ny), out[1].reshape(p, nx, ny)


def solution(mesh):
    placed = (
        P("mode", ("grp", "space"), None),
        P("mode", ("grp", "space"), None),
        P("mode", None),
        P("mode", None),
        P("mode", None, None),
        P("mode", None),
        P(("grp", "space"), None),
        P("mode"),
        P("mode"),
        P("mode"),
        P("mode"),
    )
    return jax.shard_map(
        on_device,
        mesh=mesh,
        in_specs=placed,
        out_specs=(P("mode", ("grp", "space"), None), P("mode", ("grp", "space"), None)),
        check_vma=False,
    )
```

```python
import jax
import jax.numpy as jnp
from jax import lax
from jax.experimental import pallas as pl
from jax.experimental.pallas import tpu as pltpu
from jax.sharding import PartitionSpec as P

NM = 2048
BLK = 128
ITERS = 2
CORES = 2
CHUNKS = 2

VMEM = pl.BlockSpec(memory_space=pltpu.VMEM)
SMEM = pl.BlockSpec(memory_space=pltpu.SMEM)
COST = pl.CostEstimate(flops=1000, bytes_accessed=1000, transcendentals=0)


def swap_cores(x):
    n = lax.axis_size("mode")
    return lax.ppermute(x, "mode", [(i, i ^ 1) for i in range(n)])


def from_chip(x, offset):
    n = lax.axis_size("mode")
    return lax.ppermute(x, "mode", [((i + CORES * offset) % n, i) for i in range(n)])


def from_space(x, step):
    n = lax.axis_size("space")
    pairs = [(i, i - step) for i in range(n) if 0 <= i - step < n]
    return lax.ppermute(x, "space", pairs)


def after(x, *others):
    return lax.optimization_barrier((x, *others))[0]


def bf16(*shape):
    return jax.ShapeDtypeStruct(shape, jnp.bfloat16)


def call(kernel, out, scratch, operands, specs=None, megabytes=20, name="step"):
    return pl.pallas_call(
        kernel,
        out_shape=out,
        in_specs=specs or [VMEM] * len(operands),
        out_specs=(VMEM,) * len(out),
        scratch_shapes=scratch,
        compiler_params=pltpu.CompilerParams(vmem_limit_bytes=megabytes << 20),
        cost_estimate=COST,
        name=name,
    )(*operands)


def flatten_kernel(nx, ny, x_ref, *refs):
    outs, wide_ref = refs[:-1], refs[-1]
    count = x_ref.shape[0] // nx
    tall = nx // len(outs)
    tile = min(count, 64)

    @pl.loop(0, count // tile)
    def _(i):
        at = pl.multiple_of(i * tile, tile)
        wide_ref[0 : tile * nx, :] = x_ref[pl.ds(pl.multiple_of(at * nx, tile * nx), tile * nx), :].astype(jnp.float32)
        for r in range(nx):
            k, c = r // tall, r % tall
            row = wide_ref[pl.ds(r, tile, stride=nx), :].astype(jnp.bfloat16)
            outs[k][pl.ds(at, tile), c * ny : (c + 1) * ny] = row


def flatten_edges_kernel(nx, ny, x_ref, e_ref, *refs):
    *outs, first_ref, final_ref, wide_ref = refs
    flatten_kernel(nx, ny, x_ref, *outs, wide_ref)
    e = e_ref.shape[0]
    first_ref[0:e, :] = e_ref[:, 0:ny]
    first_ref[e:, :] = outs[0][:, 0:ny]
    final_ref[0:e, :] = e_ref[:, (nx - 1) * ny :]
    final_ref[e:, :] = outs[-1][:, outs[-1].shape[1] - ny :]


def step_kernel(n, e, p, width, ny, nx, cols, edge, last, *refs):
    refs = list(refs)

    def take(count):
        taken = refs[:count]
        del refs[:count]
        return taken

    (source_ref,) = take(1)
    e_refs, p_refs = take(n), take(n)
    (low_e_ref, low_p_ref, high_e_ref, high_p_ref), at_e, at_p = take(4), cols[0][0], cols[1][0]
    low_cols, high_cols, halo_low, halo_high = cols[2]
    (up_ref, emission_ref, absorption_ref, dense_ref, speed_ref, diffusion_ref, e_rate_ref, p_rate_ref) = take(8)
    if last:
        done_e, done_p = take(CHUNKS - 1), take(CHUNKS - 1)
        e_out_ref, p_out_ref, se_ref, sp_ref, wide_ref = refs
    elif edge is not None:
        e_out_ref, p_out_ref, edge_ref, se_ref, sp_ref = refs
    else:
        e_out_ref, p_out_ref, se_ref, sp_ref = refs
    for j in range(n):
        owner = source_ref[j]
        se_ref[pl.ds(pl.multiple_of(owner * e, e), e), :] = e_refs[j][:, cols[0][j] : cols[0][j] + width]
        sp_ref[pl.ds(pl.multiple_of(owner * p, p), p), :] = p_refs[j][:, cols[1][j] : cols[1][j] + width]
    tile = min(p, 256)

    def around(own_ref, low_ref, high_ref, rows, col, k):
        own = own_ref[rows, col : col + width].astype(jnp.float32)
        base = e if k else 0
        low_rows = pl.ds(rows.start + base, rows.size) if halo_low else rows
        high_rows = pl.ds(rows.start + base, rows.size) if halo_high else rows
        low = low_ref[low_rows, low_cols[k] : low_cols[k] + ny].astype(jnp.float32)
        high = high_ref[high_rows, high_cols[k] : high_cols[k] + ny].astype(jnp.float32)
        lower = jnp.concatenate([low, own[:, : width - ny]], axis=1) if width > ny else low
        higher = jnp.concatenate([own[:, ny:], high], axis=1) if width > ny else high
        return own, lower, higher

    def store(new, at, count, phonons):
        out_ref = p_out_ref if phonons else e_out_ref
        rows = pl.ds(at, count)
        if not last:
            new = new.astype(jnp.bfloat16)
            out_ref[rows, :] = new
            if edge is not None:
                edge_rows = pl.ds(at + e if phonons else at, count)
                edge_ref[edge_rows, :] = new[:, edge * ny : (edge + 1) * ny]
            return
        tall = width // ny
        for k, done in enumerate(done_p if phonons else done_e):
            old = done[rows, :].astype(jnp.float32)
            for r in range(tall):
                wide_ref[pl.ds(k * tall + r, count, stride=nx), :] = old[:, r * ny : (r + 1) * ny]
        for r in range(tall):
            wide_ref[pl.ds(nx - tall + r, count, stride=nx), :] = new[:, r * ny : (r + 1) * ny]
        start = at * nx if isinstance(at, int) else pl.multiple_of(at * nx, count * nx)
        out_ref[pl.ds(start, count * nx), :] = wide_ref[0 : count * nx, :].astype(jnp.bfloat16)

    own, lower, higher = around(e_refs[0], low_e_ref, high_e_ref, pl.ds(0, e), at_e, 0)
    gain = jnp.dot(absorption_ref[...], sp_ref[...], preferred_element_type=jnp.float32)
    f_up = jnp.where(up_ref[...] == 1, lower, higher)
    new = (own - speed_ref[...] * (own - f_up) + 0.5 * gain) / (1.0 + e_rate_ref[...])
    store(new, 0, e, False)

    for i in range(p // tile):
        at = i * tile
        source = jnp.dot(
            emission_ref[pl.ds(at, tile), :], se_ref[...], preferred_element_type=jnp.float32
        ) + jnp.dot(dense_ref[pl.ds(at, tile), :], sp_ref[...], preferred_element_type=jnp.float32)
        own, lower, higher = around(p_refs[0], low_p_ref, high_p_ref, pl.ds(at, tile), at_p, 1)
        column = lax.broadcasted_iota(jnp.int32, (tile, ny), 1)
        left, right = [], []
        for r in range(width // ny):
            row = own[:, r * ny : (r + 1) * ny]
            left.append(jnp.where(column == 0, 0.0, pltpu.roll(row, 1, 1)))
            right.append(jnp.where(column == ny - 1, 0.0, pltpu.roll(row, ny - 1, 1)))
        left, right = jnp.concatenate(left, axis=1), jnp.concatenate(right, axis=1)
        lap = lower + higher + left + right - 4.0 * own
        new = (own + diffusion_ref[pl.ds(at, tile), :] * lap + 0.5 * source) / (1.0 + p_rate_ref[pl.ds(at, tile), :])
        store(new, at, tile, True)


def on_device(
    electrons,
    phonons,
    emission,
    absorption,
    block_coupling,
    block_cols,
    upwind,
    speed,
    diffusion,
    electron_rate,
    phonon_rate,
):
    e, nx, ny = electrons.shape
    p = phonons.shape[0]
    n = lax.axis_size("mode")
    chips = n // CORES
    slots = block_coupling.shape[1]
    b_rows = p // BLK
    tall = nx // CHUNKS
    width = tall * ny
    lanes = pltpu.VMEM((64 * nx, ny), jnp.float32)

    (e_all,) = call(
        lambda *refs: flatten_kernel(nx, ny, *refs), (bf16(e, nx * ny),), [lanes],
        (electrons.reshape(e * nx, ny),), megabytes=4, name="flatten",
    )
    far_e = [from_chip(e_all, d) for d in range(1, chips)]
    *p_chunks, first, final = call(
        lambda *refs: flatten_edges_kernel(nx, ny, *refs), (bf16(p, width),) * CHUNKS + (bf16(e + p, ny),) * 2, [lanes],
        (phonons.reshape(p * nx, ny), e_all), megabytes=8, name="flatten",
    )
    block_coupling = after(block_coupling, p_chunks[0])
    kernel = block_coupling.reshape(b_rows, BLK, slots, BLK)
    block_ids = jnp.arange(NM // BLK, dtype=jnp.int32)
    hits = (block_cols[:, :, None] == block_ids[None, None, :]).astype(jnp.bfloat16)
    dense = jnp.einsum(
        "bsk,bisj->bikj", hits, kernel, preferred_element_type=jnp.float32
    ).astype(jnp.bfloat16).reshape(p, NM)

    me = lax.axis_index("mode").astype(jnp.uint32)
    chip, core = me // CORES, me % CORES
    sources = jnp.stack(
        [((chip + d) % chips) * CORES + (core ^ c) for d in range(chips) for c in range(CORES)]
    ).astype(jnp.int32)
    speed, diffusion = speed[:, None], diffusion[:, None]
    electron_rate, phonon_rate = electron_rate[:, None], phonon_rate[:, None]
    ups = [upwind[k * tall : (k + 1) * tall].reshape(1, width) for k in range(CHUNKS)]
    weights = (emission, absorption, dense, speed, diffusion, electron_rate, phonon_rate)

    def step(k, es, ps, low, high, done, want_edge):
        last = bool(done)
        edge = {0: 0, CHUNKS - 1: tall - 1}.get(k) if want_edge else None
        cols = (
            [c for _, c in es], [c for _, c in ps],
            ((low[0][1], low[1][1]), (high[0][1], high[1][1]), k == 0, k == CHUNKS - 1),
        )
        operands = (
            sources, *(x for x, _ in es), *(x for x, _ in ps), low[0][0], low[1][0], high[0][0], high[1][0],
            ups[k], *weights, *(d[0] for d in done), *(d[1] for d in done),
        )
        scratch = [pltpu.VMEM((n * e, width), jnp.bfloat16), pltpu.VMEM((n * p, width), jnp.bfloat16)]
        if last:
            out = (bf16(e * nx, ny), bf16(p * nx, ny))
            scratch.append(pltpu.VMEM((max(e, min(p, 256)) * nx, ny), jnp.float32))
        else:
            out = (bf16(e, width), bf16(p, width)) + ((bf16(e + p, ny),) if edge is not None else ())
        return call(
            lambda *refs: step_kernel(n, e, p, width, ny, nx, cols, edge, last, *refs), out, scratch, operands,
            specs=[SMEM] + [VMEM] * (len(operands) - 1),
        )

    def gathered(own, far, wait_for, col):
        arrays = [own, swap_cores(own)]
        for f in far:
            f = after(f, *wait_for)
            arrays += [f, swap_cores(f)]
        return [(x, col) for x in arrays]

    low, high = from_space(final, -1), from_space(first, 1)
    far_p = [[from_chip(c, d) for d in range(1, chips)] for c in p_chunks]
    everyone = [x for x, _ in gathered(e_all, far_e, (p_chunks[0],), 0)]
    new = []
    for k in range(CHUNKS):
        es = [(x, k * width) for x in everyone]
        ps = gathered(p_chunks[k], far_p[k], (new[-1][0],) if k else (dense, low, high), 0)
        before = ((e_all, k * width - ny), (p_chunks[k - 1], width - ny)) if k else ((low, 0), (low, 0))
        behind = ((e_all, (k + 1) * width), (p_chunks[k + 1], 0)) if k + 1 < CHUNKS else ((high, 0), (high, 0))
        new.append(step(k, es, ps, before, behind, [], True))
    first, final = new[0][2], new[-1][2]
    chunks = [(c[0], c[1]) for c in new]

    low, high = from_space(final, -1), from_space(first, 1)
    far = [[[from_chip(x, d) for d in range(1, chips)] for x in c] for c in chunks]
    done = []
    for k in range(CHUNKS):
        wait_for = (done[-1][0],) if k else (chunks[-1][0], low, high)
        es, ps = (gathered(chunks[k][i], far[k][i], wait_for, 0) for i in range(2))
        before = tuple((x, width - ny) for x in chunks[k - 1]) if k else ((low, 0), (low, 0))
        behind = tuple((x, 0) for x in chunks[k + 1]) if k + 1 < CHUNKS else ((high, 0), (high, 0))
        done.append(step(k, es, ps, before, behind, done if k + 1 == CHUNKS else [], False))
    return done[-1][0].reshape(e, nx, ny), done[-1][1].reshape(p, nx, ny)


def solution(mesh):
    placed = (
        P("mode", ("grp", "space"), None),
        P("mode", ("grp", "space"), None),
        P("mode", None),
        P("mode", None),
        P("mode", None, None),
        P("mode", None),
        P(("grp", "space"), None),
        P("mode"),
        P("mode"),
        P("mode"),
        P("mode"),
    )
    return jax.shard_map(
        on_device,
        mesh=mesh,
        in_specs=placed,
        out_specs=(P("mode", ("grp", "space"), None), P("mode", ("grp", "space"), None)),
        check_vma=False,
    )
```

```python
import jax
import jax.numpy as jnp
from jax import lax
from jax.experimental import pallas as pl
from jax.experimental.pallas import tpu as pltpu
from jax.sharding import PartitionSpec as P

NM = 2048
BLK = 128
ITERS = 2
CORES = 2
CHUNKS = 2

VMEM = pl.BlockSpec(memory_space=pltpu.VMEM)
SMEM = pl.BlockSpec(memory_space=pltpu.SMEM)
COST = pl.CostEstimate(flops=1000, bytes_accessed=1000, transcendentals=0)


def swap_cores(x):
    n = lax.axis_size("mode")
    return lax.ppermute(x, "mode", [(i, i ^ 1) for i in range(n)])


def from_chip(x, offset):
    n = lax.axis_size("mode")
    return lax.ppermute(x, "mode", [((i + CORES * offset) % n, i) for i in range(n)])


def from_space(x, step):
    n = lax.axis_size("space")
    pairs = [(i, i - step) for i in range(n) if 0 <= i - step < n]
    return lax.ppermute(x, "space", pairs)


def from_ring(x, axis, offset):
    n = lax.axis_size(axis)
    return lax.ppermute(x, axis, [((i + offset) % n, i) for i in range(n)])


def after(x, *others):
    return lax.optimization_barrier((x, *others))[0]


def bf16(*shape):
    return jax.ShapeDtypeStruct(shape, jnp.bfloat16)


def call(kernel, out, scratch, operands, specs=None, megabytes=20, name="step"):
    return pl.pallas_call(
        kernel,
        out_shape=out,
        in_specs=specs or [VMEM] * len(operands),
        out_specs=(VMEM,) * len(out),
        scratch_shapes=scratch,
        compiler_params=pltpu.CompilerParams(vmem_limit_bytes=megabytes << 20),
        cost_estimate=COST,
        name=name,
    )(*operands)


def flatten_one(nx, ny, x_ref, outs, wide_ref):
    count = x_ref.shape[0] // nx
    tall = nx // len(outs)
    tile = min(count, 64)

    @pl.loop(0, count // tile)
    def _(i):
        at = pl.multiple_of(i * tile, tile)
        wide_ref[0 : tile * nx, :] = x_ref[pl.ds(pl.multiple_of(at * nx, tile * nx), tile * nx), :].astype(jnp.float32)
        for r in range(nx):
            k, c = r // tall, r % tall
            row = wide_ref[pl.ds(r, tile, stride=nx), :].astype(jnp.bfloat16)
            outs[k][pl.ds(at, tile), c * ny : (c + 1) * ny] = row


def flatten_own_kernel(nx, ny, e_ref, p_ref, e_out_ref, *refs):
    *outs, first_ref, final_ref, wide_ref = refs
    flatten_one(nx, ny, e_ref, [e_out_ref], wide_ref)
    flatten_one(nx, ny, p_ref, outs, wide_ref)
    e = e_out_ref.shape[0]
    first_ref[0:e, :] = e_out_ref[:, 0:ny]
    first_ref[e:, :] = outs[0][:, 0:ny]
    final_ref[0:e, :] = e_out_ref[:, (nx - 1) * ny :]
    final_ref[e:, :] = outs[-1][:, outs[-1].shape[1] - ny :]


def flatten_others_kernel(nx, ny, count, *refs):
    xs, outs, (first_ref, final_ref, wide_ref) = refs[:count], refs[count : 2 * count], refs[2 * count :]
    for x_ref, out_ref in zip(xs, outs):
        flatten_one(nx, ny, x_ref, [out_ref], wide_ref)
    first_ref[...] = outs[1][:, 0:ny]
    final_ref[...] = outs[1][:, (nx - 1) * ny :]


def lent_kernel(n, p, width, ny, shares, place_ref, source_ref, *refs):
    share_refs, refs = refs[:shares], refs[shares:]
    p_refs, refs = refs[: n * CHUNKS], refs[n * CHUNKS :]
    own_ref, low_ref, high_ref, up_ref, speed_ref, rate_ref, out_ref, absorption_ref, sp_ref = refs
    at = 0
    for share_ref in share_refs:
        count = out_ref.shape[0] // place_ref.shape[0]
        for i in range(share_ref.shape[0] // count):
            to = pl.ds(pl.multiple_of(place_ref[at] * count, count), count)
            absorption_ref[to, :] = share_ref[i * count : (i + 1) * count, :]
            at += 1
    for k in range(CHUNKS):
        for j in range(n):
            sp_ref[pl.ds(pl.multiple_of(source_ref[j] * p, p), p), :] = p_refs[k * n + j][...]
        gain = jnp.dot(absorption_ref[...], sp_ref[...], preferred_element_type=jnp.float32)
        start, stop = k * width, (k + 1) * width
        own = own_ref[:, start:stop].astype(jnp.float32)
        low = (own_ref[:, start - ny : start] if k else low_ref[...]).astype(jnp.float32)
        high = (own_ref[:, stop : stop + ny] if k + 1 < CHUNKS else high_ref[...]).astype(jnp.float32)
        lower = jnp.concatenate([low, own[:, : width - ny]], axis=1) if width > ny else low
        higher = jnp.concatenate([own[:, ny:], high], axis=1) if width > ny else high
        f_up = jnp.where(up_ref[:, start:stop] == 1, lower, higher)
        new = (own - speed_ref[...] * (own - f_up) + 0.5 * gain) / (1.0 + rate_ref[...])
        out_ref[:, start:stop] = new.astype(jnp.bfloat16)


def step_kernel(n, e, p, width, ny, nx, cols, edge, last, *refs):
    refs = list(refs)

    def take(count):
        taken = refs[:count]
        del refs[:count]
        return taken

    (source_ref,) = take(1)
    e_refs, p_refs = take(n), take(n)
    (low_e_ref, low_p_ref, high_e_ref, high_p_ref), at_e, at_p = take(4), cols[0][0], cols[1][0]
    low_cols, high_cols, halo_low, halo_high = cols[2]
    (up_ref, emission_ref, absorption_ref, dense_ref, speed_ref, diffusion_ref, e_rate_ref, p_rate_ref) = take(8)
    if last:
        done_e, done_p = take(CHUNKS - 1), take(CHUNKS - 1)
        e_out_ref, p_out_ref, se_ref, sp_ref, wide_ref = refs
    elif edge is not None:
        e_out_ref, p_out_ref, edge_ref, se_ref, sp_ref = refs
    else:
        e_out_ref, p_out_ref, se_ref, sp_ref = refs
    for j in range(n):
        owner = source_ref[j]
        se_ref[pl.ds(pl.multiple_of(owner * e, e), e), :] = e_refs[j][:, cols[0][j] : cols[0][j] + width]
        sp_ref[pl.ds(pl.multiple_of(owner * p, p), p), :] = p_refs[j][:, cols[1][j] : cols[1][j] + width]
    tile = min(p, 256)

    def around(own_ref, low_ref, high_ref, rows, col, k):
        own = own_ref[rows, col : col + width].astype(jnp.float32)
        base = e if k else 0
        low_rows = pl.ds(rows.start + base, rows.size) if halo_low else rows
        high_rows = pl.ds(rows.start + base, rows.size) if halo_high else rows
        low = low_ref[low_rows, low_cols[k] : low_cols[k] + ny].astype(jnp.float32)
        high = high_ref[high_rows, high_cols[k] : high_cols[k] + ny].astype(jnp.float32)
        lower = jnp.concatenate([low, own[:, : width - ny]], axis=1) if width > ny else low
        higher = jnp.concatenate([own[:, ny:], high], axis=1) if width > ny else high
        return own, lower, higher

    def store(new, at, count, phonons):
        out_ref = p_out_ref if phonons else e_out_ref
        rows = pl.ds(at, count)
        if not last:
            new = new.astype(jnp.bfloat16)
            out_ref[rows, :] = new
            if edge is not None:
                edge_rows = pl.ds(at + e if phonons else at, count)
                edge_ref[edge_rows, :] = new[:, edge * ny : (edge + 1) * ny]
            return
        tall = width // ny
        for k, done in enumerate(done_p if phonons else done_e):
            old = done[rows, :].astype(jnp.float32)
            for r in range(tall):
                wide_ref[pl.ds(k * tall + r, count, stride=nx), :] = old[:, r * ny : (r + 1) * ny]
        for r in range(tall):
            wide_ref[pl.ds(nx - tall + r, count, stride=nx), :] = new[:, r * ny : (r + 1) * ny]
        start = at * nx if isinstance(at, int) else pl.multiple_of(at * nx, count * nx)
        out_ref[pl.ds(start, count * nx), :] = wide_ref[0 : count * nx, :].astype(jnp.bfloat16)

    own, lower, higher = around(e_refs[0], low_e_ref, high_e_ref, pl.ds(0, e), at_e, 0)
    gain = jnp.dot(absorption_ref[...], sp_ref[...], preferred_element_type=jnp.float32)
    f_up = jnp.where(up_ref[...] == 1, lower, higher)
    new = (own - speed_ref[...] * (own - f_up) + 0.5 * gain) / (1.0 + e_rate_ref[...])
    store(new, 0, e, False)

    for i in range(p // tile):
        at = i * tile
        source = jnp.dot(
            emission_ref[pl.ds(at, tile), :], se_ref[...], preferred_element_type=jnp.float32
        ) + jnp.dot(dense_ref[pl.ds(at, tile), :], sp_ref[...], preferred_element_type=jnp.float32)
        own, lower, higher = around(p_refs[0], low_p_ref, high_p_ref, pl.ds(at, tile), at_p, 1)
        column = lax.broadcasted_iota(jnp.int32, (tile, ny), 1)
        left, right = [], []
        for r in range(width // ny):
            row = own[:, r * ny : (r + 1) * ny]
            left.append(jnp.where(column == 0, 0.0, pltpu.roll(row, 1, 1)))
            right.append(jnp.where(column == ny - 1, 0.0, pltpu.roll(row, ny - 1, 1)))
        left, right = jnp.concatenate(left, axis=1), jnp.concatenate(right, axis=1)
        lap = lower + higher + left + right - 4.0 * own
        new = (own + diffusion_ref[pl.ds(at, tile), :] * lap + 0.5 * source) / (1.0 + p_rate_ref[pl.ds(at, tile), :])
        store(new, at, tile, True)


def on_device(
    electrons,
    phonons,
    emission,
    absorption,
    block_coupling,
    block_cols,
    upwind,
    speed,
    diffusion,
    electron_rate,
    phonon_rate,
):
    e, nx, ny = electrons.shape
    p = phonons.shape[0]
    n = lax.axis_size("mode")
    chips = n // CORES
    slots = block_coupling.shape[1]
    b_rows = p // BLK
    tall = nx // CHUNKS
    width = tall * ny
    lanes = pltpu.VMEM((64 * nx, ny), jnp.float32)

    groups, spaces = lax.axis_size("grp"), lax.axis_size("space")
    lend = chips == 2 and e % (16 * groups * spaces) == 0
    if lend:
        count = e // (groups * spaces)
        grp, space = lax.axis_index("grp").astype(jnp.uint32), lax.axis_index("space").astype(jnp.uint32)
        start = (grp * spaces + space) * count
        share = from_chip(lax.dynamic_slice(absorption, (start, jnp.zeros_like(start)), (count, NM)), 1)
        far_rates = from_chip(jnp.stack([speed, electron_rate]), 1)
        shares = [share] + [from_ring(share, "space", d) for d in range(1, spaces)]
        column = jnp.concatenate(shares, axis=0)
        shares_of = [column] + [from_ring(column, "grp", d) for d in range(1, groups)]
        places = jnp.stack(
            [((grp + g) % groups) * spaces + (space + d) % spaces for g in range(groups) for d in range(spaces)]
        ).astype(jnp.int32)

    near_e = swap_cores(electrons)
    far_e = [from_chip(electrons, d) for d in range(1, chips)]
    e_all, *p_chunks, first, final = call(
        lambda *refs: flatten_own_kernel(nx, ny, *refs),
        (bf16(e, nx * ny),) + (bf16(p, width),) * CHUNKS + (bf16(e + p, ny),) * 2, [lanes],
        (electrons.reshape(e * nx, ny), phonons.reshape(p * nx, ny)), megabytes=8, name="flatten",
    )
    block_coupling = after(block_coupling, p_chunks[0])
    kernel = block_coupling.reshape(b_rows, BLK, slots, BLK)
    block_ids = jnp.arange(NM // BLK, dtype=jnp.int32)
    hits = (block_cols[:, :, None] == block_ids[None, None, :]).astype(jnp.bfloat16)
    dense = jnp.einsum(
        "bsk,bisj->bikj", hits, kernel, preferred_element_type=jnp.float32
    ).astype(jnp.bfloat16).reshape(p, NM)

    me = lax.axis_index("mode").astype(jnp.uint32)
    chip, core = me // CORES, me % CORES
    sources = jnp.stack(
        [((chip + d) % chips) * CORES + (core ^ c) for d in range(chips) for c in range(CORES)]
    ).astype(jnp.int32)
    ups = [upwind[k * tall : (k + 1) * tall].reshape(1, width) for k in range(CHUNKS)]
    rates = (x[:, None] for x in (speed, diffusion, electron_rate, phonon_rate))
    weights = (emission, absorption, dense, *rates)

    def step(k, es, ps, low, high, done, want_edge):
        last = bool(done)
        edge = {0: 0, CHUNKS - 1: tall - 1}.get(k) if want_edge else None
        cols = (
            [c for _, c in es], [c for _, c in ps],
            ((low[0][1], low[1][1]), (high[0][1], high[1][1]), k == 0, k == CHUNKS - 1),
        )
        operands = (
            sources, *(x for x, _ in es), *(x for x, _ in ps), low[0][0], low[1][0], high[0][0], high[1][0],
            ups[k], *weights, *(d[0] for d in done), *(d[1] for d in done),
        )
        scratch = [pltpu.VMEM((n * e, width), jnp.bfloat16), pltpu.VMEM((n * p, width), jnp.bfloat16)]
        if last:
            out = (bf16(e * nx, ny), bf16(p * nx, ny))
            scratch.append(pltpu.VMEM((max(e, min(p, 256)) * nx, ny), jnp.float32))
        else:
            out = (bf16(e, width), bf16(p, width)) + ((bf16(e + p, ny),) if edge is not None else ())
        return call(
            lambda *refs: step_kernel(n, e, p, width, ny, nx, cols, edge, last, *refs), out, scratch, operands,
            specs=[SMEM] + [VMEM] * (len(operands) - 1),
        )

    def gathered(own, far, wait_for, col):
        arrays = [own, swap_cores(own)]
        for f in far:
            f = after(f, *wait_for)
            arrays += [f, swap_cores(f)]
        return [(x, col) for x in arrays]

    low, high = from_space(final, -1), from_space(first, 1)
    far_p = [[from_chip(c, d) for d in range(1, chips)] for c in p_chunks]
    others = [near_e]
    for f in far_e:
        f = after(f, p_chunks[0], *((share, far_rates) if lend else ()))
        others += [f, swap_cores(f)]
    *others, far_first, far_final = call(
        lambda *refs: flatten_others_kernel(nx, ny, n - 1, *refs),
        (bf16(e, nx * ny),) * (n - 1) + (bf16(e, ny),) * 2, [lanes],
        [x.reshape(e * nx, ny) for x in others], megabytes=12, name="flatten",
    )
    everyone = [e_all, *others]
    if lend:
        far_low, far_high = from_space(far_final, -1), from_space(far_first, 1)
    waits = [(dense, low, high, everyone[1]) + (tuple(shares) if lend else ())]
    new, every_p = [], []
    for k in range(CHUNKS):
        es = [(x, k * width) for x in everyone]
        ps = gathered(p_chunks[k], far_p[k], waits[k], 0)
        before = ((e_all, k * width - ny), (p_chunks[k - 1], width - ny)) if k else ((low, 0), (low, 0))
        behind = ((e_all, (k + 1) * width), (p_chunks[k + 1], 0)) if k + 1 < CHUNKS else ((high, 0), (high, 0))
        new.append(step(k, es, ps, before, behind, [], True))
        every_p += [x for x, _ in ps]
        waits.append((new[-1][0],) + ((far_low, far_high, *shares_of) if lend else ()))
    first, final = new[0][2], new[-1][2]
    chunks = [(c[0], c[1]) for c in new]

    low, high = from_space(final, -1), from_space(first, 1)
    far_p = [[from_chip(c[1], d) for d in range(1, chips)] for c in chunks]
    ready = (chunks[-1][0], low, high)
    if lend:
        own = after(everyone[2], chunks[-1][0])
        operands = (
            places, sources, *shares_of, *every_p, own, far_low, far_high, upwind.reshape(1, nx * ny),
            far_rates[0][:, None], far_rates[1][:, None],
        )
        (lent,) = call(
            lambda *refs: lent_kernel(n, p, width, ny, groups, *refs), (bf16(e, nx * ny),),
            [pltpu.VMEM((e, NM), jnp.bfloat16), pltpu.VMEM((n * p, width), jnp.bfloat16)],
            operands, specs=[SMEM, SMEM] + [VMEM] * (len(operands) - 2), name="lent",
        )
        lent = [lent, swap_cores(lent)]
        ready += (lent[0],)
    else:
        far_e = [[from_chip(c[0], d) for d in range(1, chips)] for c in chunks]
    done = []
    for k in range(CHUNKS):
        wait_for = (done[-1][0],) if k else ready
        if lend:
            es = [(chunks[k][0], 0), (swap_cores(chunks[k][0]), 0)] + [(x, k * width) for x in lent]
        else:
            es = gathered(chunks[k][0], far_e[k], wait_for, 0)
        ps = gathered(chunks[k][1], far_p[k], wait_for, 0)
        before = tuple((x, width - ny) for x in chunks[k - 1]) if k else ((low, 0), (low, 0))
        behind = tuple((x, 0) for x in chunks[k + 1]) if k + 1 < CHUNKS else ((high, 0), (high, 0))
        done.append(step(k, es, ps, before, behind, done if k + 1 == CHUNKS else [], False))
    return done[-1][0].reshape(e, nx, ny), done[-1][1].reshape(p, nx, ny)


def solution(mesh):
    placed = (
        P("mode", ("grp", "space"), None),
        P("mode", ("grp", "space"), None),
        P("mode", None),
        P("mode", None),
        P("mode", None, None),
        P("mode", None),
        P(("grp", "space"), None),
        P("mode"),
        P("mode"),
        P("mode"),
        P("mode"),
    )
    return jax.shard_map(
        on_device,
        mesh=mesh,
        in_specs=placed,
        out_specs=(P("mode", ("grp", "space"), None), P("mode", ("grp", "space"), None)),
        check_vma=False,
    )
```

```python
import jax
import jax.numpy as jnp
from jax import lax
from jax.experimental import pallas as pl
from jax.experimental.pallas import tpu as pltpu
from jax.sharding import PartitionSpec as P

NM = 2048
BLK = 128
ITERS = 2
CORES = 2
CHUNKS = 2

VMEM = pl.BlockSpec(memory_space=pltpu.VMEM)
SMEM = pl.BlockSpec(memory_space=pltpu.SMEM)
ANY = pl.BlockSpec(memory_space=pl.ANY)
COST = pl.CostEstimate(flops=1000, bytes_accessed=1000, transcendentals=0)


def swap_cores(x):
    return exchange(x, "mode", 1)


def exchange(x, axis, bit):
    return lax.ppermute(x, axis, [(i, i ^ bit) for i in range(lax.axis_size(axis))])


def from_chip(x, offset):
    n = lax.axis_size("mode")
    return lax.ppermute(x, "mode", [((i + CORES * offset) % n, i) for i in range(n)])


def halos(a, b):
    n = lax.axis_size("space")
    near = [(i, i ^ 1) for i in range(n) if i ^ 1 < n]
    other = [(i, i + 1 if i % 2 else i - 1) for i in range(n) if 0 <= (i + 1 if i % 2 else i - 1) < n]
    return lax.ppermute(a, "space", near), lax.ppermute(b, "space", other)


def after(x, *others):
    return lax.optimization_barrier((x, *others))[0]


def bf16(*shape):
    return jax.ShapeDtypeStruct(shape, jnp.bfloat16)


def call(kernel, out, scratch, operands, specs, megabytes, name, copies):
    return pl.pallas_call(
        kernel,
        out_shape=out,
        in_specs=specs,
        out_specs=(VMEM,) * len(out),
        scratch_shapes=[*scratch, pltpu.SemaphoreType.DMA((copies,))],
        compiler_params=pltpu.CompilerParams(vmem_limit_bytes=megabytes << 20),
        cost_estimate=COST,
        name=name,
    )(*operands)


class Loader:
    def __init__(self, sems):
        self.sems, self.used = sems, 0

    def start(self, src, dst):
        copy = pltpu.make_async_copy(src, dst, self.sems.at[self.used])
        self.used += 1
        copy.start()
        return copy

    def start_one(self, choose, src, other, dst):
        sem = self.sems.at[self.used]
        self.used += 1

        @pl.when(choose)
        def _():
            pltpu.make_async_copy(src, dst, sem).start()

        @pl.when(jnp.logical_not(choose))
        def _():
            pltpu.make_async_copy(other, dst, sem).start()

        return pltpu.make_async_copy(src, dst, sem)


def rows_at(index, count):
    return pl.ds(pl.multiple_of(index * count, count), count)


def as_column(row):
    return jnp.transpose(jnp.broadcast_to(row, (8, row.shape[1])))[:, 0:1]


def flatten_one(nx, ny, x_ref, outs, wide_ref):
    count = x_ref.shape[0] // nx
    tall = nx // len(outs)
    tile = min(count, 64)

    @pl.loop(0, count // tile)
    def _(i):
        at = pl.multiple_of(i * tile, tile)
        wide_ref[0 : tile * nx, :] = x_ref[pl.ds(pl.multiple_of(at * nx, tile * nx), tile * nx), :].astype(jnp.float32)
        for r in range(nx):
            k, c = r // tall, r % tall
            row = wide_ref[pl.ds(r, tile, stride=nx), :].astype(jnp.bfloat16)
            outs[k][pl.ds(at, tile), c * ny : (c + 1) * ny] = row


def flatten_own_kernel(nx, ny, place_ref, e_ref, p_ref, e_out_ref, *refs):
    *outs, a_ref, b_ref, e_in, p_in, wide_ref, sems = refs
    load = Loader(sems)
    e_copy, p_copy = load.start(e_ref, e_in), load.start(p_ref, p_in)
    e_copy.wait()
    flatten_one(nx, ny, e_in, [e_out_ref], wide_ref)
    p_copy.wait()
    flatten_one(nx, ny, p_in, outs, wide_ref)
    e = e_out_ref.shape[0]
    even = place_ref[0] == 0
    for to_ref, last in ((a_ref, even), (b_ref, jnp.logical_not(even))):

        @pl.when(last)
        def _():
            to_ref[0:e, :] = e_out_ref[:, (nx - 1) * ny :]
            to_ref[e:, :] = outs[-1][:, outs[-1].shape[1] - ny :]

        @pl.when(jnp.logical_not(last))
        def _():
            to_ref[0:e, :] = e_out_ref[:, 0:ny]
            to_ref[e:, :] = outs[0][:, 0:ny]


def flatten_others_kernel(nx, ny, count, *refs):
    xs, outs, ins, (wide_ref, sems) = refs[:count], refs[count : 2 * count], refs[2 * count : 3 * count], refs[3 * count :]
    load = Loader(sems)
    copies = [load.start(x, y) for x, y in zip(xs, ins)]
    for copy, x_ref, out_ref in zip(copies, ins, outs):
        copy.wait()
        flatten_one(nx, ny, x_ref, [out_ref], wide_ref)


def lent_kernel(n, e, p, width, ny, shares, count, place_ref, *refs):
    share_refs, refs = refs[:shares], refs[shares:]
    p_refs, refs = refs[: n * CHUNKS], refs[n * CHUNKS :]
    far_ref, a_ref, b_ref, up_ref, rate_ref, out_ref, absorption_ref, sp_ref, own_ref, edge_ref, sems = refs
    load, first, second = Loader(sems), [], []
    even = place_ref[0] == 0
    at = 1 + n
    for share_ref in share_refs:
        for i in range(share_ref.shape[0] // count):
            to = absorption_ref.at[rows_at(place_ref[at], count), :]
            first.append(load.start(share_ref.at[i * count : (i + 1) * count, :], to))
            at += 1
    for k in range(CHUNKS):
        for j in range(n):
            copy = load.start(p_refs[k * n + j], sp_ref.at[k, rows_at(place_ref[1 + j], p), :])
            (second if k else first).append(copy)
        if not k:
            first.append(load.start(far_ref, own_ref))
            beyond = pl.ds(e + p, e)
            first.append(load.start_one(even, b_ref.at[beyond, :], a_ref.at[beyond, :], edge_ref.at[0:e, :]))
            first.append(load.start_one(even, a_ref.at[beyond, :], b_ref.at[beyond, :], edge_ref.at[e:, :]))
    for k in range(CHUNKS):
        for copy in second if k == 1 else [] if k else first:
            copy.wait()
        gain = jnp.dot(absorption_ref[...], sp_ref[k], preferred_element_type=jnp.float32)
        start, stop = k * width, (k + 1) * width
        own = own_ref[:, start:stop].astype(jnp.float32)
        low = (own_ref[:, start - ny : start] if k else edge_ref[0:e, :]).astype(jnp.float32)
        high = (own_ref[:, stop : stop + ny] if k + 1 < CHUNKS else edge_ref[e:, :]).astype(jnp.float32)
        lower = jnp.concatenate([low, own[:, : width - ny]], axis=1) if width > ny else low
        higher = jnp.concatenate([own[:, ny:], high], axis=1) if width > ny else high
        f_up = jnp.where(up_ref[:, start:stop] == 1, lower, higher)
        speed, rate = as_column(rate_ref[0:1, :]), as_column(rate_ref[1:2, :])
        new = (own - speed * (own - f_up) + 0.5 * gain) / (1.0 + rate)
        out_ref[:, start:stop] = new.astype(jnp.bfloat16)


def step_kernel(n, e, p, width, ny, nx, k, cols, edges, last, place_ref, *refs):
    refs = list(refs)

    def take(count):
        taken = refs[:count]
        del refs[:count]
        return taken

    e_refs, p_refs, before, behind = take(n), take(n), take(2), take(2)
    emission_hbm, absorption_hbm, dense_hbm, up_ref, speed_ref, diffusion_ref, e_rate_ref, p_rate_ref = take(8)
    done = take(2 * (CHUNKS - 1)) if last else []
    border = take(3 if edges == 3 else 2) if edges else []
    e_out_ref, p_out_ref = take(2)
    to_refs = take(2) if edges else []
    se_ref, sp_ref, emission_ref, absorption_ref, dense_ref, low_ref, high_ref = take(7)
    done_ref, wide_ref = take(2) if last else (None, None)
    first_ref, final_ref = take(2) if edges else (None, None)
    load = Loader(refs[0])
    tall = width // ny
    even = place_ref[0] == 0
    me = place_ref[1]

    early = [load.start(absorption_hbm, absorption_ref)]
    for j in range(n):
        early.append(load.start(p_refs[j], sp_ref.at[rows_at(place_ref[1 + j], p), :]))
    for j in range(n):
        late_e = load.start(e_refs[j].at[:, cols[j] : cols[j] + width], se_ref.at[rows_at(place_ref[1 + j], e), :])
        early.append(late_e)
    if k == 0:
        early.append(load.start_one(even, before[1].at[0 : e + p, :], before[0].at[0 : e + p, :], low_ref))
    else:
        early.append(load.start(before[0].at[:, pl.ds((cols[0] or before[0].shape[1]) - ny, ny)], low_ref.at[0:e, :]))
        early.append(load.start(before[1].at[:, width - ny : width], low_ref.at[e:, :]))
    if k == CHUNKS - 1:
        early.append(load.start_one(even, behind[0].at[0 : e + p, :], behind[1].at[0 : e + p, :], high_ref))
    else:
        next_col = cols[0] + width if behind[0].shape[1] > width else 0
        early.append(load.start(behind[0].at[:, next_col : next_col + ny], high_ref.at[0:e, :]))
        early.append(load.start(behind[1].at[:, 0:ny], high_ref.at[e:, :]))
    late = [load.start(emission_hbm, emission_ref), load.start(dense_hbm, dense_ref)]
    for i, array in enumerate(done):
        place = i // 2
        to = done_ref.at[place, 0:e, :] if i % 2 == 0 else done_ref.at[place, e:, :]
        late.append(load.start(array, to))
    if edges:
        late.append(load.start(border[0].at[:, 0:ny], first_ref.at[0:e, :]))
        late.append(load.start(border[1].at[:, 0:ny], first_ref.at[e : e + p, :]))
        if edges == 3:
            late.append(load.start(border[2].at[:, 0:ny], first_ref.at[e + p :, :]))
            late.append(load.start(border[2].at[:, (nx - 1) * ny :], final_ref.at[e + p :, :]))
    tile = min(p, 256)

    def around(x_ref, rows, base):
        own = x_ref[rows, :].astype(jnp.float32)
        low, high = low_ref[base, :].astype(jnp.float32), high_ref[base, :].astype(jnp.float32)
        lower = jnp.concatenate([low, own[:, : width - ny]], axis=1) if width > ny else low
        higher = jnp.concatenate([own[:, ny:], high], axis=1) if width > ny else high
        return own, lower, higher

    def store(new, at, count, base):
        out_ref = p_out_ref if base else e_out_ref
        if not last:
            new = new.astype(jnp.bfloat16)
            out_ref[at : at + count, :] = new
            if edges:
                final_ref[base + at : base + at + count, :] = new[:, width - ny :]
            return
        for c in range(CHUNKS - 1):
            old = done_ref[c, base + at : base + at + count, :].astype(jnp.float32)
            for r in range(tall):
                wide_ref[pl.ds(c * tall + r, count, stride=nx), :] = old[:, r * ny : (r + 1) * ny]
        for r in range(tall):
            wide_ref[pl.ds(nx - tall + r, count, stride=nx), :] = new[:, r * ny : (r + 1) * ny]
        out_ref[at * nx : (at + count) * nx, :] = wide_ref[0 : count * nx, :].astype(jnp.bfloat16)

    for copy in early:
        copy.wait()
    gain = jnp.dot(absorption_ref[...], sp_ref[...], preferred_element_type=jnp.float32)
    own, lower, higher = around(se_ref, rows_at(me, e), pl.ds(0, e))
    f_up = jnp.where(up_ref[...] == 1, lower, higher)
    new = (own - as_column(speed_ref[...]) * (own - f_up) + 0.5 * gain) / (1.0 + as_column(e_rate_ref[...]))
    for copy in late:
        copy.wait()
    store(new, 0, e, 0)

    for at in range(0, p, tile):
        source = jnp.dot(
            emission_ref[at : at + tile, :], se_ref[...], preferred_element_type=jnp.float32
        ) + jnp.dot(dense_ref[at : at + tile, :], sp_ref[...], preferred_element_type=jnp.float32)
        rows = pl.ds(pl.multiple_of(me * p + at, tile), tile)
        own, lower, higher = around(sp_ref, rows, pl.ds(e + at, tile))
        column = lax.broadcasted_iota(jnp.int32, (tile, ny), 1)
        left, right = [], []
        for r in range(tall):
            row = own[:, r * ny : (r + 1) * ny]
            left.append(jnp.where(column == 0, 0.0, pltpu.roll(row, 1, 1)))
            right.append(jnp.where(column == ny - 1, 0.0, pltpu.roll(row, ny - 1, 1)))
        left, right = jnp.concatenate(left, axis=1), jnp.concatenate(right, axis=1)
        lap = lower + higher + left + right - 4.0 * own
        diffusion, rate = as_column(diffusion_ref[:, at : at + tile]), as_column(p_rate_ref[:, at : at + tile])
        store((own + diffusion * lap + 0.5 * source) / (1.0 + rate), at, tile, e)

    if edges:
        for to_ref, is_final in ((to_refs[0], even), (to_refs[1], jnp.logical_not(even))):

            @pl.when(is_final)
            def _():
                to_ref[...] = final_ref[...]

            @pl.when(jnp.logical_not(is_final))
            def _():
                to_ref[...] = first_ref[...]


def on_device(
    electrons,
    phonons,
    emission,
    absorption,
    block_coupling,
    block_cols,
    upwind,
    speed,
    diffusion,
    electron_rate,
    phonon_rate,
):
    e, nx, ny = electrons.shape
    p = phonons.shape[0]
    n = lax.axis_size("mode")
    chips = n // CORES
    slots = block_coupling.shape[1]
    b_rows = p // BLK
    tall = nx // CHUNKS
    width = tall * ny
    lanes = pltpu.VMEM((64 * nx, ny), jnp.float32)
    groups, spaces = lax.axis_size("grp"), lax.axis_size("space")
    me, space, grp = (lax.axis_index(a).astype(jnp.uint32) for a in ("mode", "space", "grp"))
    chip, core = me // CORES, me % CORES
    places = [space % 2] + [((chip + d) % chips) * CORES + (core ^ c) for d in range(chips) for c in range(CORES)]

    bits = [("grp", b) for b in (1, 2, 4, 8) if b < groups] + [("space", b) for b in (1, 2, 4, 8) if b < spaces]
    lend = chips == 2 and 1 << len(bits) == groups * spaces and e % (16 * groups * spaces) == 0 and len(bits) > 0
    near_e = swap_cores(electrons)
    far_e = [from_chip(electrons, d) for d in range(1, chips)]
    if lend:
        count = e // (groups * spaces)
        start = (grp * spaces + space) * count
        shares = [from_chip(lax.dynamic_slice(absorption, (start, jnp.zeros_like(start)), (count, NM)), 1)]
        far_rates = from_chip(jnp.stack([speed, electron_rate]), 1)
        own_share, held = shares[0], [(0, 0)]
        for axis, bit in bits:
            whole = jnp.concatenate(shares, axis=0) if len(shares) > 1 else shares[0]
            shares = [whole, exchange(whole, axis, bit)]
            held = held + [(g ^ bit, s) if axis == "grp" else (g, s ^ bit) for g, s in held]
        places += [(grp ^ g) * spaces + (space ^ s) for g, s in held]
    places = jnp.stack(places).astype(jnp.int32)

    e_all, *p_chunks, to_a, to_b = call(
        lambda *refs: flatten_own_kernel(nx, ny, *refs),
        (bf16(e, nx * ny),) + (bf16(p, width),) * CHUNKS + (bf16(e + p, ny),) * 2,
        [pltpu.VMEM((e * nx, ny), jnp.bfloat16), pltpu.VMEM((p * nx, ny), jnp.bfloat16), lanes],
        (places, electrons.reshape(e * nx, ny), phonons.reshape(p * nx, ny)), [SMEM, ANY, ANY], 8, "flatten", 2,
    )
    block_coupling = after(block_coupling, p_chunks[0])
    kernel = block_coupling.reshape(b_rows, BLK, slots, BLK)
    block_ids = jnp.arange(NM // BLK, dtype=jnp.int32)
    hits = (block_cols[:, :, None] == block_ids[None, None, :]).astype(jnp.bfloat16)
    dense = jnp.einsum(
        "bsk,bisj->bikj", hits, kernel, preferred_element_type=jnp.float32
    ).astype(jnp.bfloat16).reshape(p, NM)

    ups = [upwind[k * tall : (k + 1) * tall].reshape(1, width) for k in range(CHUNKS)]
    weights = (emission, absorption, dense)
    rates = (speed[None], diffusion[None], electron_rate[None], phonon_rate[None])

    def step(k, es, ps, before, behind, done, border):
        last, edges = bool(done), len(border)
        done = [x for d in done for x in d]
        operands = (
            places, *(x for x, _ in es), *ps, *before, *behind, *weights, ups[k], *rates, *done, *border,
        )
        specs = [SMEM] + [ANY] * (2 * n + 7) + [VMEM] * 5 + [ANY] * (len(done) + edges)
        scratch = [
            pltpu.VMEM(shape, jnp.bfloat16)
            for shape in (
                (n * e, width), (n * p, width), (p, n * e), (e, n * p), (p, NM), (e + p, ny), (e + p, ny)
            )
        ]
        if last:
            out = (bf16(e * nx, ny), bf16(p * nx, ny))
            scratch += [
                pltpu.VMEM((CHUNKS - 1, e + p, width), jnp.bfloat16),
                pltpu.VMEM((max(e, min(p, 256)) * nx, ny), jnp.float32),
            ]
        else:
            edge_rows = e + p + (e if edges == 3 else 0)
            out = (bf16(e, width), bf16(p, width)) + (bf16(edge_rows, ny),) * (2 if edges else 0)
            scratch += [pltpu.VMEM((edge_rows, ny), jnp.bfloat16)] * (2 if edges else 0)
        return call(
            lambda *refs: step_kernel(n, e, p, width, ny, nx, k, [c for _, c in es], edges, last, *refs),
            out, scratch, operands, specs, 28, "step", 2 * n + 7 + len(done) + edges + 1,
        )

    def gathered(own, far, wait_for):
        arrays = [own, swap_cores(own)]
        for f in far:
            f = after(f, *wait_for)
            arrays += [f, swap_cores(f)]
        return arrays

    halo = halos(to_a, to_b)
    far_p = [[from_chip(c, d) for d in range(1, chips)] for c in p_chunks]
    others = [near_e]
    for f in far_e:
        f = after(f, p_chunks[0], *((own_share, far_rates) if lend else ()))
        others += [f, swap_cores(f)]
    others = call(
        lambda *refs: flatten_others_kernel(nx, ny, n - 1, *refs), (bf16(e, nx * ny),) * (n - 1),
        [pltpu.VMEM((e * nx, ny), jnp.bfloat16)] * (n - 1) + [lanes],
        [x.reshape(e * nx, ny) for x in others], [ANY] * (n - 1), 12, "flatten", n - 1,
    )
    everyone = [e_all, *others]
    waits = (dense, *halo, everyone[1])
    new, every_p = [], []
    for k in range(CHUNKS):
        ps = gathered(p_chunks[k], far_p[k], waits)
        new.append(step(
            k, [(x, k * width) for x in everyone], ps, (e_all, p_chunks[k - 1]) if k else halo,
            (e_all, p_chunks[k + 1]) if k + 1 < CHUNKS else halo, [],
            () if k + 1 < CHUNKS else (*new[0][:2], *([everyone[2]] if lend else [])),
        ))
        every_p += ps
        waits = (new[-1][1], *(shares if lend else ()))
    halo = halos(new[-1][2], new[-1][3])
    chunks = [c[:2] for c in new]

    far_p = [[from_chip(c[1], d) for d in range(1, chips)] for c in chunks]
    ready = (chunks[-1][1], *halo)
    if lend:
        operands = (places, *shares, *every_p, everyone[2], *halo, upwind.reshape(1, nx * ny), far_rates)
        (lent,) = call(
            lambda *refs: lent_kernel(n, e, p, width, ny, 2, count, *refs), (bf16(e, nx * ny),),
            [
                pltpu.VMEM(shape, jnp.bfloat16)
                for shape in ((e, NM), (CHUNKS, n * p, width), (e, nx * ny), (2 * e, ny))
            ],
            operands, [SMEM] + [ANY] * (len(operands) - 3) + [VMEM, VMEM], 16, "lent",
            groups * spaces + n * CHUNKS + 3,
        )
        lent = [lent, swap_cores(lent)]
        ready += (lent[0],)
    else:
        far_e = [[from_chip(c[0], d) for d in range(1, chips)] for c in chunks]
    done = []
    for k in range(CHUNKS):
        waits = (done[-1][1],) if k else ready
        if lend:
            es = [(chunks[k][0], 0), (swap_cores(chunks[k][0]), 0)] + [(x, k * width) for x in lent]
        else:
            es = [(x, 0) for x in gathered(chunks[k][0], far_e[k], waits)]
        done.append(step(
            k, es, gathered(chunks[k][1], far_p[k], waits), chunks[k - 1] if k else halo,
            chunks[k + 1] if k + 1 < CHUNKS else halo, done if k + 1 == CHUNKS else [], (),
        ))
    return done[-1][0].reshape(e, nx, ny), done[-1][1].reshape(p, nx, ny)


def solution(mesh):
    placed = (
        P("mode", ("grp", "space"), None),
        P("mode", ("grp", "space"), None),
        P("mode", None),
        P("mode", None),
        P("mode", None, None),
        P("mode", None),
        P(("grp", "space"), None),
        P("mode"),
        P("mode"),
        P("mode"),
        P("mode"),
    )
    return jax.shard_map(
        on_device,
        mesh=mesh,
        in_specs=placed,
        out_specs=(P("mode", ("grp", "space"), None), P("mode", ("grp", "space"), None)),
        check_vma=False,
    )
```

```python
import jax
import jax.numpy as jnp
from jax import lax
from jax.experimental import pallas as pl
from jax.experimental.pallas import tpu as pltpu
from jax.sharding import PartitionSpec as P

NM = 2048
BLK = 128
ITERS = 2
CORES = 2
CHUNKS = 2

VMEM = pl.BlockSpec(memory_space=pltpu.VMEM)
SMEM = pl.BlockSpec(memory_space=pltpu.SMEM)
ANY = pl.BlockSpec(memory_space=pl.ANY)
COST = pl.CostEstimate(flops=1000, bytes_accessed=1000, transcendentals=0)


def swap_cores(x):
    return exchange(x, "mode", 1)


def exchange(x, axis, bit):
    return lax.ppermute(x, axis, [(i, i ^ bit) for i in range(lax.axis_size(axis))])


def from_chip(x, offset):
    n = lax.axis_size("mode")
    return lax.ppermute(x, "mode", [((i + CORES * offset) % n, i) for i in range(n)])


def halos(a, b):
    n = lax.axis_size("space")
    near = [(i, i ^ 1) for i in range(n) if i ^ 1 < n]
    other = [(i, i + 1 if i % 2 else i - 1) for i in range(n) if 0 <= (i + 1 if i % 2 else i - 1) < n]
    return lax.ppermute(a, "space", near), lax.ppermute(b, "space", other)


def after(x, *others):
    return lax.optimization_barrier((x, *others))[0]


def bf16(*shape):
    return jax.ShapeDtypeStruct(shape, jnp.bfloat16)


def call(kernel, out, scratch, operands, specs, megabytes, name, copies):
    return pl.pallas_call(
        kernel,
        out_shape=out,
        in_specs=specs,
        out_specs=(VMEM,) * len(out),
        scratch_shapes=[*scratch, pltpu.SemaphoreType.DMA((copies,))],
        compiler_params=pltpu.CompilerParams(vmem_limit_bytes=megabytes << 20),
        cost_estimate=COST,
        name=name,
    )(*operands)


class Loader:
    def __init__(self, sems):
        self.sems, self.used = sems, 0

    def start(self, src, dst):
        copy = pltpu.make_async_copy(src, dst, self.sems.at[self.used])
        self.used += 1
        copy.start()
        return copy

    def start_one(self, choose, src, other, dst):
        sem = self.sems.at[self.used]
        self.used += 1

        @pl.when(choose)
        def _():
            pltpu.make_async_copy(src, dst, sem).start()

        @pl.when(jnp.logical_not(choose))
        def _():
            pltpu.make_async_copy(other, dst, sem).start()

        return pltpu.make_async_copy(src, dst, sem)


def rows_at(index, count):
    return pl.ds(pl.multiple_of(index * count, count), count)


def as_column(row):
    return jnp.transpose(jnp.broadcast_to(row, (8, row.shape[1])))[:, 0:1]


def flatten_one(nx, ny, x_ref, outs, wide_ref):
    count = x_ref.shape[0] // nx
    tall = nx // len(outs)
    tile = min(count, 64)

    @pl.loop(0, count // tile)
    def _(i):
        at = pl.multiple_of(i * tile, tile)
        wide_ref[0 : tile * nx, :] = x_ref[pl.ds(pl.multiple_of(at * nx, tile * nx), tile * nx), :].astype(jnp.float32)
        for r in range(nx):
            k, c = r // tall, r % tall
            row = wide_ref[pl.ds(r, tile, stride=nx), :].astype(jnp.bfloat16)
            outs[k][pl.ds(at, tile), c * ny : (c + 1) * ny] = row


def flatten_own_kernel(nx, ny, place_ref, e_ref, p_ref, e_out_ref, *refs):
    *outs, a_ref, b_ref, e_in, p_in, wide_ref, sems = refs
    load = Loader(sems)
    e_copy, p_copy = load.start(e_ref, e_in), load.start(p_ref, p_in)
    e_copy.wait()
    flatten_one(nx, ny, e_in, [e_out_ref], wide_ref)
    p_copy.wait()
    flatten_one(nx, ny, p_in, outs, wide_ref)
    e = e_out_ref.shape[0]
    even = place_ref[0] == 0
    for to_ref, last in ((a_ref, even), (b_ref, jnp.logical_not(even))):

        @pl.when(last)
        def _():
            to_ref[0:e, :] = e_out_ref[:, (nx - 1) * ny :]
            to_ref[e:, :] = outs[-1][:, outs[-1].shape[1] - ny :]

        @pl.when(jnp.logical_not(last))
        def _():
            to_ref[0:e, :] = e_out_ref[:, 0:ny]
            to_ref[e:, :] = outs[0][:, 0:ny]


def flatten_others_kernel(nx, ny, count, place_ref, *refs):
    refs = list(refs)
    xs, outs, (a_ref, b_ref), ins = refs[:count], refs[count : 2 * count], refs[2 * count : 2 * count + 2], refs[2 * count + 2 : -2]
    wide_ref, sems = refs[-2:]
    load = Loader(sems)
    copies = [load.start(x, y) for x, y in zip(xs, ins)]
    for copy, x_ref, out_ref in zip(copies, ins, outs):
        copy.wait()
        flatten_one(nx, ny, x_ref, [out_ref], wide_ref)
    even = place_ref[0] == 0
    for to_ref, last in ((a_ref, even), (b_ref, jnp.logical_not(even))):

        @pl.when(last)
        def _():
            to_ref[...] = outs[1][:, (nx - 1) * ny :]

        @pl.when(jnp.logical_not(last))
        def _():
            to_ref[...] = outs[1][:, 0:ny]


def stack_kernel(*refs):
    *x_refs, out_ref, sems = refs
    load = Loader(sems)
    count = x_refs[0].shape[0]
    copies = [load.start(x, out_ref.at[i * count : (i + 1) * count, :]) for i, x in enumerate(x_refs)]
    for copy in copies:
        copy.wait()


def lent_kernel(n, e, p, width, ny, shares, count, place_ref, *refs):
    share_refs, refs = refs[:shares], refs[shares:]
    p_refs, refs = refs[: n * CHUNKS], refs[n * CHUNKS :]
    far_ref, a_ref, b_ref, up_ref, rate_ref = refs[:5]
    out_refs, (absorption_ref, sp_ref, own_ref, edge_ref, sems) = refs[5 : 5 + CHUNKS], refs[5 + CHUNKS :]
    load, first, second = Loader(sems), [], []
    even = place_ref[0] == 0
    at = 1 + n
    for share_ref in share_refs:
        for i in range(share_ref.shape[0] // count):
            to = absorption_ref.at[rows_at(place_ref[at], count), :]
            first.append(load.start(share_ref.at[i * count : (i + 1) * count, :], to))
            at += 1
    for k in range(CHUNKS):
        for j in range(n):
            copy = load.start(p_refs[k * n + j], sp_ref.at[k, rows_at(place_ref[1 + j], p), :])
            (second if k else first).append(copy)
        if not k:
            first.append(load.start(far_ref, own_ref))
            first.append(load.start_one(even, b_ref, a_ref, edge_ref.at[0:e, :]))
            first.append(load.start_one(even, a_ref, b_ref, edge_ref.at[e:, :]))
    for k in range(CHUNKS):
        for copy in second if k == 1 else [] if k else first:
            copy.wait()
        gain = jnp.dot(absorption_ref[...], sp_ref[k], preferred_element_type=jnp.float32)
        start, stop = k * width, (k + 1) * width
        own = own_ref[:, start:stop].astype(jnp.float32)
        low = (own_ref[:, start - ny : start] if k else edge_ref[0:e, :]).astype(jnp.float32)
        high = (own_ref[:, stop : stop + ny] if k + 1 < CHUNKS else edge_ref[e:, :]).astype(jnp.float32)
        lower = jnp.concatenate([low, own[:, : width - ny]], axis=1) if width > ny else low
        higher = jnp.concatenate([own[:, ny:], high], axis=1) if width > ny else high
        f_up = jnp.where(up_ref[:, start:stop] == 1, lower, higher)
        speed, rate = as_column(rate_ref[0:1, :]), as_column(rate_ref[1:2, :])
        new = (own - speed * (own - f_up) + 0.5 * gain) / (1.0 + rate)
        out_refs[k][...] = new.astype(jnp.bfloat16)


def step_kernel(n, e, p, width, ny, nx, k, cols, edges, last, place_ref, *refs):
    refs = list(refs)

    def take(count):
        taken = refs[:count]
        del refs[:count]
        return taken

    e_refs, p_refs, before, behind = take(n), take(n), take(2), take(2)
    emission_hbm, absorption_hbm, dense_hbm, up_ref, speed_ref, diffusion_ref, e_rate_ref, p_rate_ref = take(8)
    done = take(2 * (CHUNKS - 1)) if last else []
    border = take(2) if edges else []
    e_out_ref, p_out_ref = take(2)
    to_refs = take(2) if edges else []
    se_ref, sp_ref, emission_ref, absorption_ref, dense_ref, low_ref, high_ref = take(7)
    done_ref, wide_ref = take(2) if last else (None, None)
    first_ref, final_ref = take(2) if edges else (None, None)
    load = Loader(refs[0])
    tall = width // ny
    even = place_ref[0] == 0
    me = place_ref[1]

    early = [load.start(absorption_hbm, absorption_ref)]
    for j in range(n):
        early.append(load.start(p_refs[j], sp_ref.at[rows_at(place_ref[1 + j], p), :]))
    for j in range(n):
        late_e = load.start(e_refs[j].at[:, cols[j] : cols[j] + width], se_ref.at[rows_at(place_ref[1 + j], e), :])
        early.append(late_e)
    if k == 0:
        early.append(load.start_one(even, before[1], before[0], low_ref))
    else:
        early.append(load.start(before[0].at[:, pl.ds((cols[0] or before[0].shape[1]) - ny, ny)], low_ref.at[0:e, :]))
        early.append(load.start(before[1].at[:, width - ny : width], low_ref.at[e:, :]))
    if k == CHUNKS - 1:
        early.append(load.start_one(even, behind[0], behind[1], high_ref))
    else:
        next_col = cols[0] + width if behind[0].shape[1] > width else 0
        early.append(load.start(behind[0].at[:, next_col : next_col + ny], high_ref.at[0:e, :]))
        early.append(load.start(behind[1].at[:, 0:ny], high_ref.at[e:, :]))
    late = [load.start(emission_hbm, emission_ref), load.start(dense_hbm, dense_ref)]
    for i, array in enumerate(done):
        place = i // 2
        to = done_ref.at[place, 0:e, :] if i % 2 == 0 else done_ref.at[place, e:, :]
        late.append(load.start(array, to))
    if edges:
        late.append(load.start(border[0].at[:, 0:ny], first_ref.at[0:e, :]))
        late.append(load.start(border[1].at[:, 0:ny], first_ref.at[e : e + p, :]))
    tile = min(p, 256)

    def around(x_ref, rows, base):
        own = x_ref[rows, :].astype(jnp.float32)
        low, high = low_ref[base, :].astype(jnp.float32), high_ref[base, :].astype(jnp.float32)
        lower = jnp.concatenate([low, own[:, : width - ny]], axis=1) if width > ny else low
        higher = jnp.concatenate([own[:, ny:], high], axis=1) if width > ny else high
        return own, lower, higher

    def store(new, at, count, base):
        out_ref = p_out_ref if base else e_out_ref
        if not last:
            new = new.astype(jnp.bfloat16)
            out_ref[at : at + count, :] = new
            if edges:
                final_ref[base + at : base + at + count, :] = new[:, width - ny :]
            return
        for c in range(CHUNKS - 1):
            old = done_ref[c, base + at : base + at + count, :].astype(jnp.float32)
            for r in range(tall):
                wide_ref[pl.ds(c * tall + r, count, stride=nx), :] = old[:, r * ny : (r + 1) * ny]
        for r in range(tall):
            wide_ref[pl.ds(nx - tall + r, count, stride=nx), :] = new[:, r * ny : (r + 1) * ny]
        out_ref[at * nx : (at + count) * nx, :] = wide_ref[0 : count * nx, :].astype(jnp.bfloat16)

    for copy in early:
        copy.wait()
    gain = jnp.dot(absorption_ref[...], sp_ref[...], preferred_element_type=jnp.float32)
    own, lower, higher = around(se_ref, rows_at(me, e), pl.ds(0, e))
    f_up = jnp.where(up_ref[...] == 1, lower, higher)
    new = (own - as_column(speed_ref[...]) * (own - f_up) + 0.5 * gain) / (1.0 + as_column(e_rate_ref[...]))
    for copy in late:
        copy.wait()
    store(new, 0, e, 0)

    for at in range(0, p, tile):
        source = jnp.dot(
            emission_ref[at : at + tile, :], se_ref[...], preferred_element_type=jnp.float32
        ) + jnp.dot(dense_ref[at : at + tile, :], sp_ref[...], preferred_element_type=jnp.float32)
        rows = pl.ds(pl.multiple_of(me * p + at, tile), tile)
        own, lower, higher = around(sp_ref, rows, pl.ds(e + at, tile))
        column = lax.broadcasted_iota(jnp.int32, (tile, ny), 1)
        left, right = [], []
        for r in range(tall):
            row = own[:, r * ny : (r + 1) * ny]
            left.append(jnp.where(column == 0, 0.0, pltpu.roll(row, 1, 1)))
            right.append(jnp.where(column == ny - 1, 0.0, pltpu.roll(row, ny - 1, 1)))
        left, right = jnp.concatenate(left, axis=1), jnp.concatenate(right, axis=1)
        lap = lower + higher + left + right - 4.0 * own
        diffusion, rate = as_column(diffusion_ref[:, at : at + tile]), as_column(p_rate_ref[:, at : at + tile])
        store((own + diffusion * lap + 0.5 * source) / (1.0 + rate), at, tile, e)

    if edges:
        for to_ref, is_final in ((to_refs[0], even), (to_refs[1], jnp.logical_not(even))):

            @pl.when(is_final)
            def _():
                to_ref[...] = final_ref[...]

            @pl.when(jnp.logical_not(is_final))
            def _():
                to_ref[...] = first_ref[...]


def on_device(
    electrons,
    phonons,
    emission,
    absorption,
    block_coupling,
    block_cols,
    upwind,
    speed,
    diffusion,
    electron_rate,
    phonon_rate,
):
    e, nx, ny = electrons.shape
    p = phonons.shape[0]
    n = lax.axis_size("mode")
    chips = n // CORES
    slots = block_coupling.shape[1]
    b_rows = p // BLK
    tall = nx // CHUNKS
    width = tall * ny
    lanes = pltpu.VMEM((64 * nx, ny), jnp.float32)
    groups, spaces = lax.axis_size("grp"), lax.axis_size("space")
    me, space, grp = (lax.axis_index(a).astype(jnp.uint32) for a in ("mode", "space", "grp"))
    chip, core = me // CORES, me % CORES
    places = [space % 2] + [((chip + d) % chips) * CORES + (core ^ c) for d in range(chips) for c in range(CORES)]

    lend = False
    if lend:
        count = e // (groups * spaces)
        start = (grp * spaces + space) * count
        share = from_chip(lax.dynamic_slice(absorption, (start, jnp.zeros_like(start)), (count, NM)), 1)
        far_rates = from_chip(jnp.stack([speed, electron_rate]), 1)
        places += [(grp ^ g) * spaces + (space ^ s) for g in range(groups) for s in range(spaces)]
    places = jnp.stack(places).astype(jnp.int32)

    near_e = swap_cores(electrons)
    far_e = [from_chip(electrons, d) for d in range(1, chips)]
    e_all, *p_chunks, to_a, to_b = call(
        lambda *refs: flatten_own_kernel(nx, ny, *refs),
        (bf16(e, nx * ny),) + (bf16(p, width),) * CHUNKS + (bf16(e + p, ny),) * 2,
        [pltpu.VMEM((e * nx, ny), jnp.bfloat16), pltpu.VMEM((p * nx, ny), jnp.bfloat16), lanes],
        (places, electrons.reshape(e * nx, ny), phonons.reshape(p * nx, ny)), [SMEM, ANY, ANY], 8, "flatten", 2,
    )
    block_coupling = after(block_coupling, p_chunks[0])
    kernel = block_coupling.reshape(b_rows, BLK, slots, BLK)
    block_ids = jnp.arange(NM // BLK, dtype=jnp.int32)
    hits = (block_cols[:, :, None] == block_ids[None, None, :]).astype(jnp.bfloat16)
    dense = jnp.einsum(
        "bsk,bisj->bikj", hits, kernel, preferred_element_type=jnp.float32
    ).astype(jnp.bfloat16).reshape(p, NM)

    ups = [upwind[k * tall : (k + 1) * tall].reshape(1, width) for k in range(CHUNKS)]
    weights = (emission, absorption, dense)
    rates = (speed[None], diffusion[None], electron_rate[None], phonon_rate[None])

    def step(k, es, ps, before, behind, done, border):
        last, edges = bool(done), len(border)
        done = [x for d in done for x in d]
        operands = (
            places, *(x for x, _ in es), *ps, *before, *behind, *weights, ups[k], *rates, *done, *border,
        )
        specs = [SMEM] + [ANY] * (2 * n + 7) + [VMEM] * 5 + [ANY] * (len(done) + edges)
        scratch = [
            pltpu.VMEM(shape, jnp.bfloat16)
            for shape in (
                (n * e, width), (n * p, width), (p, n * e), (e, n * p), (p, NM), (e + p, ny), (e + p, ny)
            )
        ]
        if last:
            out = (bf16(e * nx, ny), bf16(p * nx, ny))
            scratch += [
                pltpu.VMEM((CHUNKS - 1, e + p, width), jnp.bfloat16),
                pltpu.VMEM((max(e, min(p, 256)) * nx, ny), jnp.float32),
            ]
        else:
            out = (bf16(e, width), bf16(p, width)) + (bf16(e + p, ny),) * edges
            scratch += [pltpu.VMEM((e + p, ny), jnp.bfloat16)] * edges
        return call(
            lambda *refs: step_kernel(n, e, p, width, ny, nx, k, [c for _, c in es], edges, last, *refs),
            out, scratch, operands, specs, 28, "step", 2 * n + 7 + len(done) + edges + 1,
        )

    def gathered(own, far, wait_for):
        arrays = [own, swap_cores(own)]
        for f in far:
            f = after(f, *wait_for)
            arrays += [f, swap_cores(f)]
        return arrays

    halo = halos(to_a, to_b)
    far_p = [[from_chip(c, d) for d in range(1, chips)] for c in p_chunks]
    if lend:
        shares = [share] + [exchange(share, "space", d) for d in range(1, spaces)]
        (column,) = call(
            stack_kernel, (bf16(count * spaces, NM),), [], shares, [ANY] * spaces, 4, "stack", spaces,
        )
        columns = (column, exchange(column, "grp", 1))
    others = [near_e]
    for f in far_e:
        f = after(f, p_chunks[0], *(*halo, ), *(() if lend else ()))
        others += [f, swap_cores(f)]
    *others, far_a, far_b = call(
        lambda *refs: flatten_others_kernel(nx, ny, n - 1, *refs),
        (bf16(e, nx * ny),) * (n - 1) + (bf16(e, ny),) * 2,
        [pltpu.VMEM((e * nx, ny), jnp.bfloat16)] * (n - 1) + [lanes],
        [places, *(x.reshape(e * nx, ny) for x in others)], [SMEM] + [ANY] * (n - 1), 12, "flatten", n - 1,
    )
    far_halo = halos(far_a, far_b) if lend else ()
    everyone = [e_all, *others]
    waits = (dense, *halo, *(() if lend else ()))
    new, every_p = [], []
    for k in range(CHUNKS):
        ps = gathered(p_chunks[k], far_p[k], waits)
        new.append(step(
            k, [(x, k * width) for x in everyone], ps, (e_all, p_chunks[k - 1]) if k else halo,
            (e_all, p_chunks[k + 1]) if k + 1 < CHUNKS else halo, [],
            () if k + 1 < CHUNKS else new[0][:2],
        ))
        every_p += ps
        waits = (new[-1][1], *(() if lend else ()))
    halo = halos(new[-1][2], new[-1][3])
    chunks = [c[:2] for c in new]

    far_p = [[from_chip(c[1], d) for d in range(1, chips)] for c in chunks]
    ready = (chunks[-1][1], *halo, *(() if lend else ()))

    def lend_electrons(last_of_all):
        operands = (places, *columns, *every_p, everyone[2], *far_halo, upwind.reshape(1, nx * ny), far_rates)
        return call(
            lambda *refs: lent_kernel(n, e, p, width, ny, 2, count, *refs), (bf16(e, width),) * CHUNKS,
            [
                pltpu.VMEM(shape, jnp.bfloat16)
                for shape in ((e, NM), (CHUNKS, n * p, width), (e, nx * ny), (2 * e, ny))
            ],
            operands, [SMEM] + [ANY] * (len(operands) - 3) + [VMEM, VMEM], 16, "lent",
            groups * spaces + n * CHUNKS + 3,
        )

    if not lend:
        far_e = [[from_chip(c[0], d) for d in range(1, chips)] for c in chunks]
    done = []
    for k in range(CHUNKS):
        waits = (done[-1][1],) if k else ready
        ps = gathered(chunks[k][1], far_p[k], waits)
        if lend and not k:
            lent = lend_electrons(ps[-1])
        if lend:
            es = [(chunks[k][0], 0), (swap_cores(chunks[k][0]), 0)] + [(lent[k], 0), (swap_cores(lent[k]), 0)]
        else:
            es = [(x, 0) for x in gathered(chunks[k][0], far_e[k], waits)]
        done.append(step(
            k, es, ps, chunks[k - 1] if k else halo,
            chunks[k + 1] if k + 1 < CHUNKS else halo, done if k + 1 == CHUNKS else [], (),
        ))
    return done[-1][0].reshape(e, nx, ny), done[-1][1].reshape(p, nx, ny)


def solution(mesh):
    placed = (
        P("mode", ("grp", "space"), None),
        P("mode", ("grp", "space"), None),
        P("mode", None),
        P("mode", None),
        P("mode", None, None),
        P("mode", None),
        P(("grp", "space"), None),
        P("mode"),
        P("mode"),
        P("mode"),
        P("mode"),
    )
    return jax.shard_map(
        on_device,
        mesh=mesh,
        in_specs=placed,
        out_specs=(P("mode", ("grp", "space"), None), P("mode", ("grp", "space"), None)),
        check_vma=False,
    )
```

```python
import jax
import jax.numpy as jnp
from jax import lax
from jax.experimental import pallas as pl
from jax.experimental.pallas import tpu as pltpu
from jax.sharding import PartitionSpec as P

NM = 2048
BLK = 128
ITERS = 2
CORES = 2
CHUNKS = 2
PARTS = (1, 2)

VMEM = pl.BlockSpec(memory_space=pltpu.VMEM)
SMEM = pl.BlockSpec(memory_space=pltpu.SMEM)
ANY = pl.BlockSpec(memory_space=pl.ANY)
COST = pl.CostEstimate(flops=1000, bytes_accessed=1000, transcendentals=0)


def swap_cores(x):
    n = lax.axis_size("mode")
    return lax.ppermute(x, "mode", [(i, i ^ 1) for i in range(n)])


def from_chip(x, offset):
    n = lax.axis_size("mode")
    return lax.ppermute(x, "mode", [((i + CORES * offset) % n, i) for i in range(n)])


def halos(a, b):
    n = lax.axis_size("space")
    near = [(i, i ^ 1) for i in range(n) if i ^ 1 < n]
    other = [(i, i + 1 if i % 2 else i - 1) for i in range(n) if 0 <= (i + 1 if i % 2 else i - 1) < n]
    return lax.ppermute(a, "space", near), lax.ppermute(b, "space", other)


def after(x, *others):
    return lax.optimization_barrier((x, *others))[0]


def bf16(*shape):
    return jax.ShapeDtypeStruct(shape, jnp.bfloat16)


def call(kernel, out, scratch, operands, specs, megabytes, name, copies):
    return pl.pallas_call(
        kernel,
        out_shape=out,
        in_specs=specs,
        out_specs=(VMEM,) * len(out),
        scratch_shapes=[*scratch, pltpu.SemaphoreType.DMA((copies,))],
        compiler_params=pltpu.CompilerParams(vmem_limit_bytes=megabytes << 20),
        cost_estimate=COST,
        name=name,
    )(*operands)


class Loader:
    def __init__(self, sems):
        self.sems, self.used = sems, 0

    def start(self, src, dst):
        copy = pltpu.make_async_copy(src, dst, self.sems.at[self.used])
        self.used += 1
        copy.start()
        return copy

    def start_one(self, choose, src, other, dst):
        sem = self.sems.at[self.used]
        self.used += 1

        @pl.when(choose)
        def _():
            pltpu.make_async_copy(src, dst, sem).start()

        @pl.when(jnp.logical_not(choose))
        def _():
            pltpu.make_async_copy(other, dst, sem).start()

        return pltpu.make_async_copy(src, dst, sem)


def rows_at(index, count):
    return pl.ds(pl.multiple_of(index * count, count), count)


def rows_of(base, i, part):
    return pl.ds(base + i * part.shape[0], part.shape[0])


def as_column(row):
    return jnp.transpose(jnp.broadcast_to(row, (8, row.shape[1])))[:, 0:1]


def flatten_one(nx, ny, x_ref, outs, wide_ref):
    count = x_ref.shape[0] // nx
    tall = nx // len(outs)
    tile = min([count, 64] + [out.shape[0] for parts in outs for out in parts])
    for at in range(0, count, tile):
        wide_ref[0 : tile * nx, :] = x_ref[at * nx : (at + tile) * nx, :].astype(jnp.float32)
        for r in range(nx):
            k, c = r // tall, r % tall
            row = wide_ref[pl.ds(r, tile, stride=nx), :].astype(jnp.bfloat16)
            part, offset = divmod(at, outs[k][0].shape[0])
            outs[k][part][offset : offset + tile, c * ny : (c + 1) * ny] = row


def flatten_own_kernel(nx, ny, counts, place_ref, e_ref, p_ref, e_out_ref, *refs):
    *flat, a_ref, b_ref, e_in, p_in, wide_ref, sems = refs
    outs = []
    for count in counts:
        outs.append(flat[:count])
        flat = flat[count:]
    load = Loader(sems)
    e_copy, p_copy = load.start(e_ref, e_in), load.start(p_ref, p_in)
    e_copy.wait()
    flatten_one(nx, ny, e_in, [[e_out_ref]], wide_ref)
    p_copy.wait()
    flatten_one(nx, ny, p_in, outs, wide_ref)
    e = e_out_ref.shape[0]
    even = place_ref[0] == 0

    def put(to_ref, parts, col, e_col):
        to_ref[0:e, :] = e_out_ref[:, e_col : e_col + ny]
        at = e
        for part in parts:
            to_ref[at : at + part.shape[0], :] = part[:, col : col + ny]
            at += part.shape[0]

    for to_ref, last in ((a_ref, even), (b_ref, jnp.logical_not(even))):

        @pl.when(last)
        def _():
            put(to_ref, outs[-1], outs[-1][0].shape[1] - ny, (nx - 1) * ny)

        @pl.when(jnp.logical_not(last))
        def _():
            put(to_ref, outs[0], 0, 0)


def flatten_others_kernel(nx, ny, count, *refs):
    xs, outs, ins, (wide_ref, sems) = refs[:count], refs[count : 2 * count], refs[2 * count : -2], refs[-2:]
    load = Loader(sems)
    copies = [load.start(x, y) for x, y in zip(xs, ins)]
    for copy, x_ref, out_ref in zip(copies, ins, outs):
        copy.wait()
        flatten_one(nx, ny, x_ref, [[out_ref]], wide_ref)


def unflatten(olds, new, nx, ny, at, out_ref, wide_ref):
    count, tall = new.shape[0], new.shape[1] // ny
    for c, chunk in enumerate([*(x.astype(jnp.float32) for x in olds), new]):
        for r in range(tall):
            wide_ref[pl.ds(c * tall + r, count, stride=nx), :] = chunk[:, r * ny : (r + 1) * ny]
    out_ref[at * nx : (at + count) * nx, :] = wide_ref[0 : count * nx, :].astype(jnp.bfloat16)


def emit_kernel(n, e, p, ny, nx, place_ref, *refs):
    e_refs, (rest_ref, emission_ref, p_rate_ref), refs = refs[:n], refs[n : n + 3], refs[n + 3 :]
    done_refs, (out_ref, se_ref, wide_ref, sems) = refs[: CHUNKS - 1], refs[CHUNKS - 1 :]
    load = Loader(sems)
    copies = [load.start(x, se_ref.at[rows_at(place_ref[1 + j], e), :]) for j, x in enumerate(e_refs)]
    for copy in copies:
        copy.wait()
    tile = min(p, 256)
    for at in range(0, p, tile):
        emit = jnp.dot(emission_ref[at : at + tile, :], se_ref[...], preferred_element_type=jnp.float32)
        new = (rest_ref[at : at + tile, :] + 0.5 * emit) / (1.0 + as_column(p_rate_ref[:, at : at + tile]))
        unflatten([x[at : at + tile, :] for x in done_refs], new, nx, ny, at, out_ref, wide_ref)


def step_kernel(n, e, p, width, ny, nx, k, cols, counts, edges, last, place_ref, *refs):
    refs = list(refs)

    def take(count):
        taken = refs[:count]
        del refs[:count]
        return taken

    e_refs, p_refs = take(1 if last else n), [take(counts[0]) for _ in range(n)]
    before, behind = (take(1), take(counts[1])), (take(1), take(counts[2]))
    (emission_hbm,) = [None] if last else take(1)
    absorption_hbm, dense_hbm, up_ref, speed_ref, diffusion_ref, e_rate_ref, p_rate_ref = take(7)
    done = take(CHUNKS - 1) if last else []
    border = take(2) if edges else []
    e_out_ref, p_out_ref = take(2)
    to_refs = take(2) if edges else []
    (emission_ref,) = [None] if last else take(1)
    se_ref, sp_ref, absorption_ref, dense_ref, low_ref, high_ref = take(6)
    done_ref, wide_ref = take(2) if last else (None, None)
    first_ref, final_ref = take(2) if edges else (None, None)
    load = Loader(refs[0])
    tall = width // ny
    even = place_ref[0] == 0
    me = place_ref[1]
    me_e = 0 if last else me

    early = [load.start(absorption_hbm, absorption_ref)]
    for j in range(n):
        for i, part in enumerate(p_refs[j]):
            early.append(load.start(part, sp_ref.at[rows_at(place_ref[1 + j] * counts[0] + i, p // counts[0]), :]))
    for j, e_ref in enumerate(e_refs):
        to = se_ref if last else se_ref.at[rows_at(place_ref[1 + j], e), :]
        early.append(load.start(e_ref.at[:, cols[j] : cols[j] + width], to))
    if k == 0:
        early.append(load.start_one(even, before[1][0], before[0][0], low_ref))
    else:
        col = (cols[0] or before[0][0].shape[1]) - ny
        early.append(load.start(before[0][0].at[:, col : col + ny], low_ref.at[0:e, :]))
        for i, part in enumerate(before[1]):
            early.append(load.start(part.at[:, width - ny : width], low_ref.at[rows_of(e, i, part), :]))
    if k == CHUNKS - 1:
        early.append(load.start_one(even, behind[0][0], behind[1][0], high_ref))
    else:
        col = cols[0] + width if behind[0][0].shape[1] > width else 0
        early.append(load.start(behind[0][0].at[:, col : col + ny], high_ref.at[0:e, :]))
        for i, part in enumerate(behind[1]):
            early.append(load.start(part.at[:, 0:ny], high_ref.at[rows_of(e, i, part), :]))
    late = [load.start(dense_hbm, dense_ref)]
    if not last:
        late.append(load.start(emission_hbm, emission_ref))
    for i, array in enumerate(done):
        late.append(load.start(array, done_ref.at[i]))
    if edges:
        late.append(load.start(border[0].at[:, 0:ny], first_ref.at[0:e, :]))
        late.append(load.start(border[1].at[:, 0:ny], first_ref.at[e : e + p, :]))
    tile = min(p, 256)

    def around(x_ref, rows, base):
        own = x_ref[rows, :].astype(jnp.float32)
        low, high = low_ref[base, :].astype(jnp.float32), high_ref[base, :].astype(jnp.float32)
        lower = jnp.concatenate([low, own[:, : width - ny]], axis=1) if width > ny else low
        higher = jnp.concatenate([own[:, ny:], high], axis=1) if width > ny else high
        return own, lower, higher

    def store(new, at, count, base):
        out_ref = p_out_ref if base else e_out_ref
        if not last:
            new = new.astype(jnp.bfloat16)
            out_ref[at : at + count, :] = new
            if edges:
                final_ref[base + at : base + at + count, :] = new[:, width - ny :]
            return
        unflatten([done_ref[c, at : at + count, :] for c in range(CHUNKS - 1)], new, nx, ny, at, out_ref, wide_ref)

    for copy in early:
        copy.wait()
    gain = jnp.dot(absorption_ref[...], sp_ref[...], preferred_element_type=jnp.float32)
    own, lower, higher = around(se_ref, rows_at(me_e, e), pl.ds(0, e))
    f_up = jnp.where(up_ref[...] == 1, lower, higher)
    new = (own - as_column(speed_ref[...]) * (own - f_up) + 0.5 * gain) / (1.0 + as_column(e_rate_ref[...]))
    for copy in late:
        copy.wait()
    store(new, 0, e, 0)

    for at in range(0, p, tile):
        source = jnp.dot(dense_ref[at : at + tile, :], sp_ref[...], preferred_element_type=jnp.float32)
        if not last:
            source += jnp.dot(emission_ref[at : at + tile, :], se_ref[...], preferred_element_type=jnp.float32)
        rows = pl.ds(pl.multiple_of(me * p + at, tile), tile)
        own, lower, higher = around(sp_ref, rows, pl.ds(e + at, tile))
        column = lax.broadcasted_iota(jnp.int32, (tile, ny), 1)
        left, right = [], []
        for r in range(tall):
            row = own[:, r * ny : (r + 1) * ny]
            left.append(jnp.where(column == 0, 0.0, pltpu.roll(row, 1, 1)))
            right.append(jnp.where(column == ny - 1, 0.0, pltpu.roll(row, ny - 1, 1)))
        left, right = jnp.concatenate(left, axis=1), jnp.concatenate(right, axis=1)
        lap = lower + higher + left + right - 4.0 * own
        diffusion, rate = as_column(diffusion_ref[:, at : at + tile]), as_column(p_rate_ref[:, at : at + tile])
        new = own + diffusion * lap + 0.5 * source
        if last:
            p_out_ref[at : at + tile, :] = new
        else:
            store(new / (1.0 + rate), at, tile, e)

    if edges:
        for to_ref, is_final in ((to_refs[0], even), (to_refs[1], jnp.logical_not(even))):

            @pl.when(is_final)
            def _():
                to_ref[...] = final_ref[...]

            @pl.when(jnp.logical_not(is_final))
            def _():
                to_ref[...] = first_ref[...]


def on_device(
    electrons,
    phonons,
    emission,
    absorption,
    block_coupling,
    block_cols,
    upwind,
    speed,
    diffusion,
    electron_rate,
    phonon_rate,
):
    e, nx, ny = electrons.shape
    p = phonons.shape[0]
    n = lax.axis_size("mode")
    chips = n // CORES
    slots = block_coupling.shape[1]
    b_rows = p // BLK
    tall = nx // CHUNKS
    width = tall * ny
    lanes = pltpu.VMEM((64 * nx, ny), jnp.float32)
    me, space = (lax.axis_index(a).astype(jnp.uint32) for a in ("mode", "space"))
    chip, core = me // CORES, me % CORES
    places = [space % 2] + [((chip + d) % chips) * CORES + (core ^ c) for d in range(chips) for c in range(CORES)]

    places = jnp.stack(places).astype(jnp.int32)

    near_e = swap_cores(electrons)
    far_e = [from_chip(electrons, d) for d in range(1, chips)]
    e_all, *flat, to_a, to_b = call(
        lambda *refs: flatten_own_kernel(nx, ny, PARTS, *refs),
        (bf16(e, nx * ny),) + tuple(bf16(p // count, width) for count in PARTS for _ in range(count))
        + (bf16(e + p, ny),) * 2,
        [pltpu.VMEM((e * nx, ny), jnp.bfloat16), pltpu.VMEM((p * nx, ny), jnp.bfloat16), lanes],
        (places, electrons.reshape(e * nx, ny), phonons.reshape(p * nx, ny)), [SMEM, ANY, ANY], 8, "flatten", 2,
    )
    p_chunks = [flat[sum(PARTS[:k]) : sum(PARTS[: k + 1])] for k in range(CHUNKS)]
    block_coupling = after(block_coupling, flat[0])
    kernel = block_coupling.reshape(b_rows, BLK, slots, BLK)
    block_ids = jnp.arange(NM // BLK, dtype=jnp.int32)
    hits = (block_cols[:, :, None] == block_ids[None, None, :]).astype(jnp.bfloat16)
    dense = jnp.einsum(
        "bsk,bisj->bikj", hits, kernel, preferred_element_type=jnp.float32
    ).astype(jnp.bfloat16).reshape(p, NM)

    ups = [upwind[k * tall : (k + 1) * tall].reshape(1, width) for k in range(CHUNKS)]
    weights = (emission, absorption, dense)
    rates = (speed[None], diffusion[None], electron_rate[None], phonon_rate[None])

    def step(k, es, ps, before, behind, done, border):
        last, edges = bool(done), len(border)
        done = [d[0] for d in done]
        es = es[:1] if last else es
        matrices = weights[1:] if last else weights
        counts = (len(ps[0]), len(before[1]), len(behind[1]))
        operands = (
            places, *(x for x, _ in es), *(x for parts in ps for x in parts), before[0], *before[1], behind[0],
            *behind[1], *matrices, ups[k], *rates, *done, *border,
        )
        large = len(es) + n * counts[0] + counts[1] + counts[2] + 2 + len(matrices)
        specs = [SMEM] + [ANY] * large + [VMEM] * 5 + [ANY] * (len(done) + edges)
        scratch = [
            pltpu.VMEM(shape, jnp.bfloat16)
            for shape in (
                *([] if last else [(p, n * e)]), (len(es) * e, width), (n * p, width), (e, n * p), (p, NM),
                (e + p, ny), (e + p, ny),
            )
        ]
        if last:
            out = (bf16(e * nx, ny), jax.ShapeDtypeStruct((p, width), jnp.float32))
            scratch += [pltpu.VMEM((CHUNKS - 1, e, width), jnp.bfloat16), pltpu.VMEM((e * nx, ny), jnp.float32)]
        else:
            out = (bf16(e, width), bf16(p, width)) + (bf16(e + p, ny),) * edges
            scratch += [pltpu.VMEM((e + p, ny), jnp.bfloat16)] * edges
        return call(
            lambda *refs: step_kernel(n, e, p, width, ny, nx, k, [c for _, c in es], counts, edges, last, *refs),
            out, scratch, operands, specs, 28, "step", large + len(done) + edges + 1,
        )

    def emit(es, rest, done):
        operands = (places, *(x for x, _ in es), rest, emission, rates[3], *(d[1] for d in done))
        return call(
            lambda *refs: emit_kernel(n, e, p, ny, nx, *refs), (bf16(p * nx, ny),),
            [pltpu.VMEM((n * e, width), jnp.bfloat16), pltpu.VMEM((min(p, 256) * nx, ny), jnp.float32)],
            operands, [SMEM] + [ANY] * n + [VMEM] * (2 + CHUNKS), 16, "emit", n,
        )[0]

    def gathered(own, far, wait_for):
        arrays = []
        for f in far:
            f = after(f, *wait_for)
            arrays += [f, swap_cores(f)]
        return [own, swap_cores(own)] + arrays

    halo = halos(to_a, to_b)
    far_p = [[[from_chip(x, d) for d in range(1, chips)] for x in parts] for parts in p_chunks]
    others = [near_e]
    for f in far_e:
        f = after(f, flat[0], *halo)
        others += [f, swap_cores(f)]
    others = call(
        lambda *refs: flatten_others_kernel(nx, ny, n - 1, *refs),
        (bf16(e, nx * ny),) * (n - 1),
        [pltpu.VMEM((e * nx, ny), jnp.bfloat16)] * (n - 1) + [lanes],
        [x.reshape(e * nx, ny) for x in others], [ANY] * (n - 1), 12, "flatten", n - 1,
    )
    everyone = [e_all, *others]
    waits = (dense, *halo)
    new = []
    for k in range(CHUNKS):
        ps = list(zip(*(gathered(x, far, waits) for x, far in zip(p_chunks[k], far_p[k]))))
        new.append(step(
            k, [(x, k * width) for x in everyone], ps,
            (e_all, p_chunks[k - 1]) if k else (halo[0], halo[1:]),
            (e_all, p_chunks[k + 1]) if k + 1 < CHUNKS else (halo[0], halo[1:]), [],
            () if k + 1 < CHUNKS else new[0][:2],
        ))
        waits = (new[-1][1],)
    halo = halos(new[-1][2], new[-1][3])
    chunks = [c[:2] for c in new]

    far_p = [[from_chip(c[1], d) for d in range(1, chips)] for c in chunks]
    ready = (chunks[-1][1], *halo)
    far_e = [[from_chip(c[0], d) for d in range(1, chips)] for c in chunks]

    def everyone_at(k, waits):
        return [(x, 0) for x in gathered(chunks[k][0], far_e[k], waits)]

    done = []
    for k in range(CHUNKS):
        waits = (done[-1][1],) if k else ready
        ps = [[x] for x in gathered(chunks[k][1], far_p[k], waits)]
        last = k + 1 == CHUNKS
        out = step(
            k, [(chunks[k][0], 0)] if last else everyone_at(k, waits), ps,
            (chunks[k - 1][0], chunks[k - 1][1:]) if k else (halo[0], halo[1:]),
            (halo[0], halo[1:]) if last else (chunks[k + 1][0], chunks[k + 1][1:]), done if last else [], (),
        )
        if not last:
            done.append(out)
    e_out, rest = out
    p_out = emit(everyone_at(CHUNKS - 1, (rest,)), rest, done)
    return e_out.reshape(e, nx, ny), p_out.reshape(p, nx, ny)


def solution(mesh):
    placed = (
        P("mode", ("grp", "space"), None),
        P("mode", ("grp", "space"), None),
        P("mode", None),
        P("mode", None),
        P("mode", None, None),
        P("mode", None),
        P(("grp", "space"), None),
        P("mode"),
        P("mode"),
        P("mode"),
        P("mode"),
    )
    return jax.shard_map(
        on_device,
        mesh=mesh,
        in_specs=placed,
        out_specs=(P("mode", ("grp", "space"), None), P("mode", ("grp", "space"), None)),
        check_vma=False,
    )
```

```python
import jax
import jax.numpy as jnp
from jax import lax
from jax.experimental import pallas as pl
from jax.experimental.pallas import tpu as pltpu
from jax.sharding import PartitionSpec as P

NM = 2048
BLK = 128
ITERS = 2
CORES = 2
CHUNKS = 2
SHARES = (3, 5)
PARTS = (1, 1)
NEXT_E_PARTS = 1

VMEM = pl.BlockSpec(memory_space=pltpu.VMEM)
SMEM = pl.BlockSpec(memory_space=pltpu.SMEM)
ANY = pl.BlockSpec(memory_space=pl.ANY)
COST = pl.CostEstimate(flops=1000, bytes_accessed=1000, transcendentals=0)


def swap_cores(x):
    n = lax.axis_size("mode")
    return lax.ppermute(x, "mode", [(i, i ^ 1) for i in range(n)])


def from_chip(x, offset):
    n = lax.axis_size("mode")
    return lax.ppermute(x, "mode", [((i + CORES * offset) % n, i) for i in range(n)])


def halos(a, b):
    n = lax.axis_size("space")
    near = [(i, i ^ 1) for i in range(n) if i ^ 1 < n]
    other = [(i, i + 1 if i % 2 else i - 1) for i in range(n) if 0 <= (i + 1 if i % 2 else i - 1) < n]
    return lax.ppermute(a, "space", near), lax.ppermute(b, "space", other)


def after(x, *others):
    return lax.optimization_barrier((x, *others))[0]


def bf16(*shape):
    return jax.ShapeDtypeStruct(shape, jnp.bfloat16)


def call(kernel, out, scratch, operands, specs, megabytes, name, copies):
    return pl.pallas_call(
        kernel,
        out_shape=out,
        in_specs=specs,
        out_specs=(VMEM,) * len(out),
        scratch_shapes=[*scratch, pltpu.SemaphoreType.DMA((copies,))],
        compiler_params=pltpu.CompilerParams(vmem_limit_bytes=megabytes << 20),
        cost_estimate=COST,
        name=name,
    )(*operands)


class Loader:
    def __init__(self, sems):
        self.sems, self.used = sems, 0

    def start(self, src, dst):
        copy = pltpu.make_async_copy(src, dst, self.sems.at[self.used])
        self.used += 1
        copy.start()
        return copy

    def start_one(self, choose, src, other, dst):
        sem = self.sems.at[self.used]
        self.used += 1

        @pl.when(choose)
        def _():
            pltpu.make_async_copy(src, dst, sem).start()

        @pl.when(jnp.logical_not(choose))
        def _():
            pltpu.make_async_copy(other, dst, sem).start()

        return pltpu.make_async_copy(src, dst, sem)


def rows_at(index, count):
    return pl.ds(pl.multiple_of(index * count, count), count)


def rows_of(base, i, part):
    return pl.ds(base + i * part.shape[0], part.shape[0])


def as_column(row):
    return jnp.transpose(jnp.broadcast_to(row, (8, row.shape[1])))[:, 0:1]


def flatten_one(nx, ny, x_ref, outs, wide_ref):
    count = x_ref.shape[0] // nx
    chunk_of = [(k, c) for k, parts in enumerate(outs) for c in range(parts[0].shape[1] // ny)]
    tile = min([count, 64] + [out.shape[0] for parts in outs for out in parts])
    for at in range(0, count, tile):
        wide_ref[0 : tile * nx, :] = x_ref[at * nx : (at + tile) * nx, :].astype(jnp.float32)
        for r in range(nx):
            k, c = chunk_of[r]
            row = wide_ref[pl.ds(r, tile, stride=nx), :].astype(jnp.bfloat16)
            part, offset = divmod(at, outs[k][0].shape[0])
            outs[k][part][offset : offset + tile, c * ny : (c + 1) * ny] = row


def flatten_own_kernel(nx, ny, counts, place_ref, e_ref, p_ref, e_out_ref, *refs):
    *flat, a_ref, b_ref, e_in, p_in, wide_ref, sems = refs
    outs = []
    for count in counts:
        outs.append(flat[:count])
        flat = flat[count:]
    load = Loader(sems)
    e_copy, p_copy = load.start(e_ref, e_in), load.start(p_ref, p_in)
    e_copy.wait()
    flatten_one(nx, ny, e_in, [[e_out_ref]], wide_ref)
    p_copy.wait()
    flatten_one(nx, ny, p_in, outs, wide_ref)
    e = e_out_ref.shape[0]
    even = place_ref[0] == 0

    def put(to_ref, parts, col, e_col):
        to_ref[0:e, :] = e_out_ref[:, e_col : e_col + ny]
        at = e
        for part in parts:
            to_ref[at : at + part.shape[0], :] = part[:, col : col + ny]
            at += part.shape[0]

    for to_ref, last in ((a_ref, even), (b_ref, jnp.logical_not(even))):

        @pl.when(last)
        def _():
            put(to_ref, outs[-1], outs[-1][0].shape[1] - ny, (nx - 1) * ny)

        @pl.when(jnp.logical_not(last))
        def _():
            put(to_ref, outs[0], 0, 0)


def flatten_others_kernel(nx, ny, count, *refs):
    xs, outs, ins, (wide_ref, sems) = refs[:count], refs[count : 2 * count], refs[2 * count : -2], refs[-2:]
    load = Loader(sems)
    copies = [load.start(x, y) for x, y in zip(xs, ins)]
    for copy, x_ref, out_ref in zip(copies, ins, outs):
        copy.wait()
        flatten_one(nx, ny, x_ref, [[out_ref]], wide_ref)


def unflatten(olds, new, nx, ny, at, out_ref, wide_ref):
    count, row = new.shape[0], 0
    for chunk in [*(x.astype(jnp.float32) for x in olds), new]:
        for r in range(chunk.shape[1] // ny):
            wide_ref[pl.ds(row, count, stride=nx), :] = chunk[:, r * ny : (r + 1) * ny]
            row += 1
    out_ref[at * nx : (at + count) * nx, :] = wide_ref[0 : count * nx, :].astype(jnp.bfloat16)


def finish_kernel(n, e, p, ny, nx, place_ref, *refs):
    far = n - CORES
    far_refs, refs = refs[:far], refs[far:]
    rest_e_ref, rest_p_ref, absorption_ref, dense_ref, e_rate_ref, p_rate_ref = refs[:6]
    done_e, done_p, refs = refs[6 : 5 + CHUNKS], refs[5 + CHUNKS : 4 + 2 * CHUNKS], refs[4 + 2 * CHUNKS :]
    e_out_ref, p_out_ref, p_ref, wide_ref, sems = refs
    load = Loader(sems)
    copies = [load.start(x, p_ref.at[j]) for j, x in enumerate(far_refs)]
    for copy in copies:
        copy.wait()

    def product(weight_ref, at, count):
        total = 0.0
        for j in range(far):
            columns = rows_at(place_ref[1 + CORES + j], p)
            total += jnp.dot(weight_ref[at : at + count, columns], p_ref[j], preferred_element_type=jnp.float32)
        return total

    tile = min(p, 256)
    pieces = [(0, e, absorption_ref, rest_e_ref, e_rate_ref, done_e, e_out_ref)]
    pieces += [(at, tile, dense_ref, rest_p_ref, p_rate_ref, done_p, p_out_ref) for at in range(0, p, tile)]
    for at, count, weight_ref, rest_ref, rate_ref, done, out_ref in pieces:
        total = rest_ref[at : at + count, :] + 0.5 * product(weight_ref, at, count)
        new = total / (1.0 + as_column(rate_ref[:, at : at + count]))
        unflatten([x[at : at + count, :] for x in done], new, nx, ny, at, out_ref, wide_ref)


def step_kernel(n, e, p, width, ny, nx, k, cols, counts, edges, last, place_ref, *refs):
    refs = list(refs)

    def take(count):
        taken = refs[:count]
        del refs[:count]
        return taken

    e_refs, p_refs = [take(counts[3]) for _ in range(n)], [take(counts[0]) for _ in range(CORES if last else n)]
    before, behind = (take(counts[4]), take(counts[1])), (take(counts[5]), take(counts[2]))
    emission_hbm, absorption_hbm, dense_hbm, up_ref, speed_ref, diffusion_ref, e_rate_ref, p_rate_ref = take(8)
    border = (take(counts[6]), take(1)) if edges else ()
    e_out_refs, p_out_ref = take(counts[7]), *take(1)
    to_refs = take(2) if edges else []
    se_ref, sp_ref, emission_ref, absorption_ref, dense_ref, low_ref, high_ref = take(7)
    first_ref, final_ref = take(2) if edges else (None, None)
    load = Loader(refs[0])
    tall = width // ny
    even = place_ref[0] == 0
    me = place_ref[1]
    me_p = 0 if last else me

    early = [load.start(absorption_hbm, absorption_ref)]
    for j, parts in enumerate(p_refs):
        owner = j if last else place_ref[1 + j]
        for i, part in enumerate(parts):
            early.append(load.start(part, sp_ref.at[rows_at(owner * counts[0] + i, p // counts[0]), :]))
    for j, parts in enumerate(e_refs):
        for i, part in enumerate(parts):
            to = se_ref.at[rows_at(place_ref[1 + j] * counts[3] + i, e // counts[3]), :]
            early.append(load.start(part.at[:, cols[j] : cols[j] + width], to))
    if k == 0:
        early.append(load.start_one(even, before[1][0], before[0][0], low_ref))
    else:
        col = cols[0] - ny
        for i, part in enumerate(before[0]):
            early.append(load.start(part.at[:, col : col + ny], low_ref.at[rows_of(0, i, part), :]))
        for i, part in enumerate(before[1]):
            early.append(load.start(part.at[:, part.shape[1] - ny :], low_ref.at[rows_of(e, i, part), :]))
    if k == CHUNKS - 1:
        early.append(load.start_one(even, behind[0][0], behind[1][0], high_ref))
    else:
        col = cols[0] + width
        for i, part in enumerate(behind[0]):
            early.append(load.start(part.at[:, col : col + ny], high_ref.at[rows_of(0, i, part), :]))
        for i, part in enumerate(behind[1]):
            early.append(load.start(part.at[:, 0:ny], high_ref.at[rows_of(e, i, part), :]))
    late = [load.start(dense_hbm, dense_ref), load.start(emission_hbm, emission_ref)]
    if edges:
        for i, part in enumerate(border[0]):
            late.append(load.start(part.at[:, 0:ny], first_ref.at[rows_of(0, i, part), :]))
        for i, part in enumerate(e_out_refs):
            late.append(load.start(border[0][0].at[rows_of(0, i, part), :], part.at[:, 0 : part.shape[1] - width]))
        late.append(load.start(border[1][0].at[:, 0:ny], first_ref.at[e : e + p, :]))
    tile = min(p, 256)

    def around(x_ref, rows, base):
        own = x_ref[rows, :].astype(jnp.float32)
        low, high = low_ref[base, :].astype(jnp.float32), high_ref[base, :].astype(jnp.float32)
        lower = jnp.concatenate([low, own[:, : width - ny]], axis=1) if width > ny else low
        higher = jnp.concatenate([own[:, ny:], high], axis=1) if width > ny else high
        return own, lower, higher

    def store(new, at, count, base):
        new = new.astype(jnp.bfloat16)
        if base:
            p_out_ref[at : at + count, :] = new
        else:
            for i, part in enumerate(e_out_refs):
                columns = slice(part.shape[1] - width, part.shape[1])
                part[:, columns] = new[i * part.shape[0] : (i + 1) * part.shape[0], :]
        if edges:
            final_ref[base + at : base + at + count, :] = new[:, width - ny :]

    def product(weight_ref, at, count):
        if not last:
            return jnp.dot(weight_ref[at : at + count, :], sp_ref[...], preferred_element_type=jnp.float32)
        total = 0.0
        for j in range(CORES):
            weight = weight_ref[at : at + count, rows_at(place_ref[1 + j], p)]
            total += jnp.dot(weight, sp_ref[j * p : (j + 1) * p, :], preferred_element_type=jnp.float32)
        return total

    for copy in early:
        copy.wait()
    gain = product(absorption_ref, 0, e)
    own, lower, higher = around(se_ref, rows_at(me, e), pl.ds(0, e))
    f_up = jnp.where(up_ref[...] == 1, lower, higher)
    new = own - as_column(speed_ref[...]) * (own - f_up) + 0.5 * gain
    if last:
        e_out_refs[0][...] = new
    else:
        store(new / (1.0 + as_column(e_rate_ref[...])), 0, e, 0)
    for copy in late:
        copy.wait()

    for at in range(0, p, tile):
        source = product(dense_ref, at, tile) + jnp.dot(
            emission_ref[at : at + tile, :], se_ref[...], preferred_element_type=jnp.float32
        )
        rows = pl.ds(pl.multiple_of(me_p * p + at, tile), tile)
        own, lower, higher = around(sp_ref, rows, pl.ds(e + at, tile))
        column = lax.broadcasted_iota(jnp.int32, (tile, ny), 1)
        left, right = [], []
        for r in range(tall):
            row = own[:, r * ny : (r + 1) * ny]
            left.append(jnp.where(column == 0, 0.0, pltpu.roll(row, 1, 1)))
            right.append(jnp.where(column == ny - 1, 0.0, pltpu.roll(row, ny - 1, 1)))
        left, right = jnp.concatenate(left, axis=1), jnp.concatenate(right, axis=1)
        lap = lower + higher + left + right - 4.0 * own
        diffusion, rate = as_column(diffusion_ref[:, at : at + tile]), as_column(p_rate_ref[:, at : at + tile])
        new = own + diffusion * lap + 0.5 * source
        if last:
            p_out_ref[at : at + tile, :] = new
        else:
            store(new / (1.0 + rate), at, tile, e)

    if edges:
        for to_ref, is_final in ((to_refs[0], even), (to_refs[1], jnp.logical_not(even))):

            @pl.when(is_final)
            def _():
                to_ref[...] = final_ref[...]

            @pl.when(jnp.logical_not(is_final))
            def _():
                to_ref[...] = first_ref[...]


def on_device(
    electrons,
    phonons,
    emission,
    absorption,
    block_coupling,
    block_cols,
    upwind,
    speed,
    diffusion,
    electron_rate,
    phonon_rate,
):
    e, nx, ny = electrons.shape
    p = phonons.shape[0]
    n = lax.axis_size("mode")
    chips = n // CORES
    slots = block_coupling.shape[1]
    b_rows = p // BLK
    talls = [nx * share // sum(SHARES) for share in SHARES]
    starts = [sum(talls[:k]) for k in range(CHUNKS)]
    widths = [tall * ny for tall in talls]
    lanes = pltpu.VMEM((64 * nx, ny), jnp.float32)
    me, space = (lax.axis_index(a).astype(jnp.uint32) for a in ("mode", "space"))
    chip, core = me // CORES, me % CORES
    places = [space % 2] + [((chip + d) % chips) * CORES + (core ^ c) for d in range(chips) for c in range(CORES)]

    places = jnp.stack(places).astype(jnp.int32)

    near_e = swap_cores(electrons)
    far_e = [from_chip(electrons, d) for d in range(1, chips)]
    e_all, *flat, to_a, to_b = call(
        lambda *refs: flatten_own_kernel(nx, ny, PARTS, *refs),
        (bf16(e, nx * ny),) + tuple(bf16(p // count, width) for count, width in zip(PARTS, widths) for _ in range(count))
        + (bf16(e + p, ny),) * 2,
        [pltpu.VMEM((e * nx, ny), jnp.bfloat16), pltpu.VMEM((p * nx, ny), jnp.bfloat16), lanes],
        (places, electrons.reshape(e * nx, ny), phonons.reshape(p * nx, ny)), [SMEM, ANY, ANY], 8, "flatten", 2,
    )
    p_chunks = [flat[sum(PARTS[:k]) : sum(PARTS[: k + 1])] for k in range(CHUNKS)]
    block_coupling = after(block_coupling, flat[0])
    kernel = block_coupling.reshape(b_rows, BLK, slots, BLK)
    block_ids = jnp.arange(NM // BLK, dtype=jnp.int32)
    hits = (block_cols[:, :, None] == block_ids[None, None, :]).astype(jnp.bfloat16)
    dense = jnp.einsum(
        "bsk,bisj->bikj", hits, kernel, preferred_element_type=jnp.float32
    ).astype(jnp.bfloat16).reshape(p, NM)

    ups = [upwind[a : a + tall].reshape(1, tall * ny) for a, tall in zip(starts, talls)]
    weights = (emission, absorption, dense)
    rates = (speed[None], diffusion[None], electron_rate[None], phonon_rate[None])

    def step(k, es, ps, before, behind, last, border):
        edges, width = len(border), widths[k]
        e_parts = NEXT_E_PARTS if edges else 1
        counts = (
            len(ps[0]), len(before[1]), len(behind[1]), len(es[0][0]), len(before[0]), len(behind[0]),
            len(border[0]) if edges else 0, e_parts,
        )
        operands = (
            places, *(x for parts, _ in es for x in parts), *(x for parts in ps for x in parts), *before[0],
            *before[1], *behind[0], *behind[1], *weights, ups[k], *rates, *(x for parts in border for x in parts),
        )
        large = n * counts[3] + len(ps) * counts[0] + sum(counts[1:3]) + sum(counts[4:6]) + 3
        specs = [SMEM] + [ANY] * large + [VMEM] * 5 + [ANY] * sum(len(parts) for parts in border)
        scratch = [
            pltpu.VMEM(shape, jnp.bfloat16)
            for shape in (
                (n * e, width), (len(ps) * p, width), (p, n * e), (e, n * p), (p, NM), (e + p, ny), (e + p, ny),
            )
        ]
        if last:
            out = tuple(jax.ShapeDtypeStruct((count, width), jnp.float32) for count in (e, p))
        else:
            out = (bf16(e // e_parts, nx * ny if edges else width),) * e_parts + (bf16(p, width),) + (bf16(e + p, ny),) * edges
            scratch += [pltpu.VMEM((e + p, ny), jnp.bfloat16)] * edges
        out = call(
            lambda *refs: step_kernel(n, e, p, width, ny, nx, k, [c for _, c in es], counts, edges, last, *refs),
            out, scratch, operands, specs, 28, "step", large + counts[6] + e_parts + 2,
        )
        return (list(out[:e_parts]), *out[e_parts:])

    def finish(far, rest, done):
        operands = (
            places, *far, *rest, absorption, dense, rates[2], rates[3], *(d[0][0] for d in done), *(d[1] for d in done),
        )
        return call(
            lambda *refs: finish_kernel(n, e, p, ny, nx, *refs), (bf16(e * nx, ny), bf16(p * nx, ny)),
            [pltpu.VMEM((len(far), p, widths[-1]), jnp.bfloat16), pltpu.VMEM((max(e, min(p, 256)) * nx, ny), jnp.float32)],
            operands, [SMEM] + [ANY] * len(far) + [VMEM] * (4 + 2 * CHUNKS), 24, "finish", len(far),
        )

    def gathered(own, far, wait_for):
        arrays = []
        for f in far:
            f = after(f, *wait_for)
            arrays += [f, swap_cores(f)]
        return [own, swap_cores(own)] + arrays

    halo = halos(to_a, to_b)
    far_p = [[[from_chip(x, d) for d in range(1, chips)] for x in parts] for parts in p_chunks]
    others = [near_e]
    for f in far_e:
        f = after(f, flat[0], *halo)
        others += [f, swap_cores(f)]
    others = call(
        lambda *refs: flatten_others_kernel(nx, ny, n - 1, *refs),
        (bf16(e, nx * ny),) * (n - 1),
        [pltpu.VMEM((e * nx, ny), jnp.bfloat16)] * (n - 1) + [lanes],
        [x.reshape(e * nx, ny) for x in others], [ANY] * (n - 1), 12, "flatten", n - 1,
    )
    everyone = [e_all, *others]
    waits = (dense, *halo)
    new = []
    for k in range(CHUNKS):
        ps = list(zip(*(gathered(x, far, waits) for x, far in zip(p_chunks[k], far_p[k]))))
        new.append(step(
            k, [([x], starts[k] * ny) for x in everyone], ps,
            ([e_all], p_chunks[k - 1]) if k else (halo[:1], halo[1:]),
            ([e_all], p_chunks[k + 1]) if k + 1 < CHUNKS else (halo[:1], halo[1:]), False,
            () if k + 1 < CHUNKS else (new[0][0], new[0][1:2]),
        ))
        waits = (new[-1][1],)
    halo = halos(new[-1][2], new[-1][3])
    e_next, p_next = new[-1][0], [c[1] for c in new]

    far_p = [[from_chip(x, d) for d in range(1, chips)] for x in p_next]
    first_p = gathered(p_next[0], far_p[0], (p_next[-1],))
    everyone = zip(*(gathered(x, [from_chip(x, d) for d in range(1, chips)], (first_p[-1], *halo)) for x in e_next))
    everyone = list(everyone)
    done = []
    for k in range(CHUNKS):
        last = k + 1 == CHUNKS
        es = [(parts, starts[k] * ny) for parts in everyone]
        ps = [p_next[k], swap_cores(p_next[k])] if last else first_p
        done.append(step(
            k, es, [[x] for x in ps], (e_next, p_next[k - 1 : k]) if k else (halo[:1], halo[1:]),
            (halo[:1], halo[1:]) if last else (e_next, p_next[k + 1 : k + 2]), last, (),
        ))
    rest = done.pop()
    far = []
    for f in far_p[-1]:
        f = after(f, rest[1], done[-1][1])
        far += [f, swap_cores(f)]
    e_out, p_out = finish(far, (rest[0][0], rest[1]), done)
    return e_out.reshape(e, nx, ny), p_out.reshape(p, nx, ny)


def solution(mesh):
    placed = (
        P("mode", ("grp", "space"), None),
        P("mode", ("grp", "space"), None),
        P("mode", None),
        P("mode", None),
        P("mode", None, None),
        P("mode", None),
        P(("grp", "space"), None),
        P("mode"),
        P("mode"),
        P("mode"),
        P("mode"),
    )
    return jax.shard_map(
        on_device,
        mesh=mesh,
        in_specs=placed,
        out_specs=(P("mode", ("grp", "space"), None), P("mode", ("grp", "space"), None)),
        check_vma=False,
    )
```

```python
import jax
import jax.numpy as jnp
from jax import lax
from jax.experimental import pallas as pl
from jax.experimental.pallas import tpu as pltpu
from jax.sharding import PartitionSpec as P

NM = 2048
BLK = 128
ITERS = 2
CORES = 2
CHUNKS = 2
SHARES = (3, 5)
PARTS = (1, 1)
NEXT_E_PARTS = 1

VMEM = pl.BlockSpec(memory_space=pltpu.VMEM)
SMEM = pl.BlockSpec(memory_space=pltpu.SMEM)
ANY = pl.BlockSpec(memory_space=pl.ANY)
COST = pl.CostEstimate(flops=1000, bytes_accessed=1000, transcendentals=0)


def swap_cores(x):
    n = lax.axis_size("mode")
    return lax.ppermute(x, "mode", [(i, i ^ 1) for i in range(n)])


def from_chip(x, offset):
    n = lax.axis_size("mode")
    return lax.ppermute(x, "mode", [((i + CORES * offset) % n, i) for i in range(n)])


def halos(a, b):
    n = lax.axis_size("space")
    near = [(i, i ^ 1) for i in range(n) if i ^ 1 < n]
    other = [(i, i + 1 if i % 2 else i - 1) for i in range(n) if 0 <= (i + 1 if i % 2 else i - 1) < n]
    return lax.ppermute(a, "space", near), lax.ppermute(b, "space", other)


def after(x, *others):
    return lax.optimization_barrier((x, *others))[0]


def bf16(*shape):
    return jax.ShapeDtypeStruct(shape, jnp.bfloat16)


def call(kernel, out, scratch, operands, specs, megabytes, name, copies):
    return pl.pallas_call(
        kernel,
        out_shape=out,
        in_specs=specs,
        out_specs=(VMEM,) * len(out),
        scratch_shapes=[*scratch, pltpu.SemaphoreType.DMA((copies,))],
        compiler_params=pltpu.CompilerParams(vmem_limit_bytes=megabytes << 20),
        cost_estimate=COST,
        name=name,
    )(*operands)


class Loader:
    def __init__(self, sems):
        self.sems, self.used = sems, 0

    def start(self, src, dst):
        copy = pltpu.make_async_copy(src, dst, self.sems.at[self.used])
        self.used += 1
        copy.start()
        return copy

    def start_one(self, choose, src, other, dst):
        sem = self.sems.at[self.used]
        self.used += 1

        @pl.when(choose)
        def _():
            pltpu.make_async_copy(src, dst, sem).start()

        @pl.when(jnp.logical_not(choose))
        def _():
            pltpu.make_async_copy(other, dst, sem).start()

        return pltpu.make_async_copy(src, dst, sem)


def rows_at(index, count):
    return pl.ds(pl.multiple_of(index * count, count), count)


def rows_of(base, i, part):
    return pl.ds(base + i * part.shape[0], part.shape[0])


def as_column(row):
    return jnp.transpose(jnp.broadcast_to(row, (8, row.shape[1])))[:, 0:1]


def flatten_one(nx, ny, x_ref, outs, wide_ref):
    count = x_ref.shape[0] // nx
    chunk_of = [(k, c) for k, parts in enumerate(outs) for c in range(parts[0].shape[1] // ny)]
    tile = min([count, 64] + [out.shape[0] for parts in outs for out in parts])
    for at in range(0, count, tile):
        wide_ref[0 : tile * nx, :] = x_ref[at * nx : (at + tile) * nx, :].astype(jnp.float32)
        for r in range(nx):
            k, c = chunk_of[r]
            row = wide_ref[pl.ds(r, tile, stride=nx), :].astype(jnp.bfloat16)
            part, offset = divmod(at, outs[k][0].shape[0])
            outs[k][part][offset : offset + tile, c * ny : (c + 1) * ny] = row


def flatten_own_kernel(nx, ny, counts, place_ref, e_ref, p_ref, e_out_ref, *refs):
    *flat, a_ref, b_ref, e_in, p_in, wide_ref, sems = refs
    outs = []
    for count in counts:
        outs.append(flat[:count])
        flat = flat[count:]
    load = Loader(sems)
    e_copy, p_copy = load.start(e_ref, e_in), load.start(p_ref, p_in)
    e_copy.wait()
    flatten_one(nx, ny, e_in, [[e_out_ref]], wide_ref)
    p_copy.wait()
    flatten_one(nx, ny, p_in, outs, wide_ref)
    e = e_out_ref.shape[0]
    even = place_ref[0] == 0

    def put(to_ref, parts, col, e_col):
        to_ref[0:e, :] = e_out_ref[:, e_col : e_col + ny]
        at = e
        for part in parts:
            to_ref[at : at + part.shape[0], :] = part[:, col : col + ny]
            at += part.shape[0]

    for to_ref, last in ((a_ref, even), (b_ref, jnp.logical_not(even))):

        @pl.when(last)
        def _():
            put(to_ref, outs[-1], outs[-1][0].shape[1] - ny, (nx - 1) * ny)

        @pl.when(jnp.logical_not(last))
        def _():
            put(to_ref, outs[0], 0, 0)


def flatten_others_kernel(nx, ny, count, *refs):
    xs, outs, ins, (wide_ref, sems) = refs[:count], refs[count : 2 * count], refs[2 * count : -2], refs[-2:]
    load = Loader(sems)
    copies = [load.start(x, y) for x, y in zip(xs, ins)]
    for copy, x_ref, out_ref in zip(copies, ins, outs):
        copy.wait()
        flatten_one(nx, ny, x_ref, [[out_ref]], wide_ref)


def unflatten(olds, new, nx, ny, at, out_ref, wide_ref):
    count, row = new.shape[0], 0
    for chunk in [*(x.astype(jnp.float32) for x in olds), new]:
        for r in range(chunk.shape[1] // ny):
            wide_ref[pl.ds(row, count, stride=nx), :] = chunk[:, r * ny : (r + 1) * ny]
            row += 1
    out_ref[at * nx : (at + count) * nx, :] = wide_ref[0 : count * nx, :].astype(jnp.bfloat16)


def finish_kernel(n, e, p, ny, nx, place_ref, *refs):
    far = n - CORES
    far_refs, refs = refs[:far], refs[far:]
    rest_e_ref, rest_p_ref, absorption_ref, dense_ref, e_rate_ref, p_rate_ref = refs[:6]
    done_e, done_p, refs = refs[6 : 5 + CHUNKS], refs[5 + CHUNKS : 4 + 2 * CHUNKS], refs[4 + 2 * CHUNKS :]
    e_out_ref, p_out_ref, p_ref, wide_ref, sems = refs
    load = Loader(sems)
    copies = [load.start(x, p_ref.at[j]) for j, x in enumerate(far_refs)]
    for copy in copies:
        copy.wait()

    def product(weight_ref, at, count):
        total = 0.0
        for j in range(far):
            columns = rows_at(place_ref[1 + CORES + j], p)
            total += jnp.dot(weight_ref[at : at + count, columns], p_ref[j], preferred_element_type=jnp.float32)
        return total

    tile = min(p, 256)
    pieces = [(0, e, absorption_ref, rest_e_ref, e_rate_ref, done_e, e_out_ref)]
    pieces += [(at, tile, dense_ref, rest_p_ref, p_rate_ref, done_p, p_out_ref) for at in range(0, p, tile)]
    for at, count, weight_ref, rest_ref, rate_ref, done, out_ref in pieces:
        total = rest_ref[at : at + count, :] + 0.5 * product(weight_ref, at, count)
        new = total / (1.0 + as_column(rate_ref[:, at : at + count]))
        unflatten([x[at : at + count, :] for x in done], new, nx, ny, at, out_ref, wide_ref)


def step_kernel(n, e, p, width, ny, nx, k, cols, counts, edges, last, place_ref, *refs):
    refs = list(refs)

    def take(count):
        taken = refs[:count]
        del refs[:count]
        return taken

    e_refs, p_refs = [take(counts[3]) for _ in range(n)], [take(counts[0]) for _ in range(CORES if last else n)]
    before, behind = (take(counts[4]), take(counts[1])), (take(counts[5]), take(counts[2]))
    emission_ref, absorption_ref, dense_ref, up_ref, speed_ref, diffusion_ref, e_rate_ref, p_rate_ref = take(8)
    border = (take(counts[6]), take(1)) if edges else ()
    e_out_refs, p_out_ref = take(counts[7]), *take(1)
    to_refs = take(2) if edges else []
    se_ref, sp_ref, low_ref, high_ref = take(4)
    first_ref, final_ref = take(2) if edges else (None, None)
    load = Loader(refs[0])
    tall = width // ny
    even = place_ref[0] == 0
    me = place_ref[1]
    me_p = 0 if last else me

    early, middle = [], []
    for j, parts in enumerate(p_refs):
        owner = j if last else place_ref[1 + j]
        for i, part in enumerate(parts):
            early.append(load.start(part, sp_ref.at[rows_at(owner * counts[0] + i, p // counts[0]), :]))
    for j, parts in enumerate(e_refs):
        for i, part in enumerate(parts):
            to = se_ref.at[rows_at(place_ref[1 + j] * counts[3] + i, e // counts[3]), :]
            (middle if j else early).append(load.start(part.at[:, cols[j] : cols[j] + width], to))
    if k == 0:
        early.append(load.start_one(even, before[1][0], before[0][0], low_ref))
    else:
        col = cols[0] - ny
        for i, part in enumerate(before[0]):
            early.append(load.start(part.at[:, col : col + ny], low_ref.at[rows_of(0, i, part), :]))
        for i, part in enumerate(before[1]):
            early.append(load.start(part.at[:, part.shape[1] - ny :], low_ref.at[rows_of(e, i, part), :]))
    if k == CHUNKS - 1:
        early.append(load.start_one(even, behind[0][0], behind[1][0], high_ref))
    else:
        col = cols[0] + width
        for i, part in enumerate(behind[0]):
            early.append(load.start(part.at[:, col : col + ny], high_ref.at[rows_of(0, i, part), :]))
        for i, part in enumerate(behind[1]):
            early.append(load.start(part.at[:, 0:ny], high_ref.at[rows_of(e, i, part), :]))
    late = []
    if edges:
        for i, part in enumerate(border[0]):
            late.append(load.start(part.at[:, 0:ny], first_ref.at[rows_of(0, i, part), :]))
        for i, part in enumerate(e_out_refs):
            late.append(load.start(border[0][0].at[rows_of(0, i, part), :], part.at[:, 0 : part.shape[1] - width]))
        late.append(load.start(border[1][0].at[:, 0:ny], first_ref.at[e : e + p, :]))
    tile = min(p, 256)

    def around(x_ref, rows, base):
        own = x_ref[rows, :].astype(jnp.float32)
        low, high = low_ref[base, :].astype(jnp.float32), high_ref[base, :].astype(jnp.float32)
        lower = jnp.concatenate([low, own[:, : width - ny]], axis=1) if width > ny else low
        higher = jnp.concatenate([own[:, ny:], high], axis=1) if width > ny else high
        return own, lower, higher

    def store(new, at, count, base):
        new = new.astype(jnp.bfloat16)
        if base:
            p_out_ref[at : at + count, :] = new
        else:
            for i, part in enumerate(e_out_refs):
                columns = slice(part.shape[1] - width, part.shape[1])
                part[:, columns] = new[i * part.shape[0] : (i + 1) * part.shape[0], :]
        if edges:
            final_ref[base + at : base + at + count, :] = new[:, width - ny :]

    def product(weight_ref, at, count):
        if not last:
            return jnp.dot(weight_ref[at : at + count, :], sp_ref[...], preferred_element_type=jnp.float32)
        total = 0.0
        for j in range(CORES):
            weight = weight_ref[at : at + count, rows_at(place_ref[1 + j], p)]
            total += jnp.dot(weight, sp_ref[j * p : (j + 1) * p, :], preferred_element_type=jnp.float32)
        return total

    for copy in early:
        copy.wait()
    gain = product(absorption_ref, 0, e)
    own, lower, higher = around(se_ref, rows_at(me, e), pl.ds(0, e))
    f_up = jnp.where(up_ref[...] == 1, lower, higher)
    new = own - as_column(speed_ref[...]) * (own - f_up) + 0.5 * gain
    if last:
        e_out_refs[0][...] = new
    else:
        store(new / (1.0 + as_column(e_rate_ref[...])), 0, e, 0)
    for copy in middle + late:
        copy.wait()

    for at in range(0, p, tile):
        source = product(dense_ref, at, tile) + jnp.dot(
            emission_ref[at : at + tile, :], se_ref[...], preferred_element_type=jnp.float32
        )
        rows = pl.ds(pl.multiple_of(me_p * p + at, tile), tile)
        own, lower, higher = around(sp_ref, rows, pl.ds(e + at, tile))
        column = lax.broadcasted_iota(jnp.int32, (tile, ny), 1)
        left, right = [], []
        for r in range(tall):
            row = own[:, r * ny : (r + 1) * ny]
            left.append(jnp.where(column == 0, 0.0, pltpu.roll(row, 1, 1)))
            right.append(jnp.where(column == ny - 1, 0.0, pltpu.roll(row, ny - 1, 1)))
        left, right = jnp.concatenate(left, axis=1), jnp.concatenate(right, axis=1)
        lap = lower + higher + left + right - 4.0 * own
        diffusion, rate = as_column(diffusion_ref[:, at : at + tile]), as_column(p_rate_ref[:, at : at + tile])
        new = own + diffusion * lap + 0.5 * source
        if last:
            p_out_ref[at : at + tile, :] = new
        else:
            store(new / (1.0 + rate), at, tile, e)

    if edges:
        for to_ref, is_final in ((to_refs[0], even), (to_refs[1], jnp.logical_not(even))):

            @pl.when(is_final)
            def _():
                to_ref[...] = final_ref[...]

            @pl.when(jnp.logical_not(is_final))
            def _():
                to_ref[...] = first_ref[...]


def on_device(
    electrons,
    phonons,
    emission,
    absorption,
    block_coupling,
    block_cols,
    upwind,
    speed,
    diffusion,
    electron_rate,
    phonon_rate,
):
    e, nx, ny = electrons.shape
    p = phonons.shape[0]
    n = lax.axis_size("mode")
    chips = n // CORES
    slots = block_coupling.shape[1]
    b_rows = p // BLK
    talls = [nx * share // sum(SHARES) for share in SHARES]
    starts = [sum(talls[:k]) for k in range(CHUNKS)]
    widths = [tall * ny for tall in talls]
    lanes = pltpu.VMEM((64 * nx, ny), jnp.float32)
    me, space = (lax.axis_index(a).astype(jnp.uint32) for a in ("mode", "space"))
    chip, core = me // CORES, me % CORES
    places = [space % 2] + [((chip + d) % chips) * CORES + (core ^ c) for d in range(chips) for c in range(CORES)]

    places = jnp.stack(places).astype(jnp.int32)

    near_e = swap_cores(electrons)
    far_e = [from_chip(electrons, d) for d in range(1, chips)]
    e_all, *flat, to_a, to_b = call(
        lambda *refs: flatten_own_kernel(nx, ny, PARTS, *refs),
        (bf16(e, nx * ny),) + tuple(bf16(p // count, width) for count, width in zip(PARTS, widths) for _ in range(count))
        + (bf16(e + p, ny),) * 2,
        [pltpu.VMEM((e * nx, ny), jnp.bfloat16), pltpu.VMEM((p * nx, ny), jnp.bfloat16), lanes],
        (places, electrons.reshape(e * nx, ny), phonons.reshape(p * nx, ny)), [SMEM, ANY, ANY], 8, "flatten", 2,
    )
    p_chunks = [flat[sum(PARTS[:k]) : sum(PARTS[: k + 1])] for k in range(CHUNKS)]
    block_coupling = after(block_coupling, flat[0])
    kernel = block_coupling.reshape(b_rows, BLK, slots, BLK)
    block_ids = jnp.arange(NM // BLK, dtype=jnp.int32)
    hits = (block_cols[:, :, None] == block_ids[None, None, :]).astype(jnp.bfloat16)
    dense = jnp.einsum(
        "bsk,bisj->bikj", hits, kernel, preferred_element_type=jnp.float32
    ).astype(jnp.bfloat16).reshape(p, NM)

    ups = [upwind[a : a + tall].reshape(1, tall * ny) for a, tall in zip(starts, talls)]
    weights = (emission, absorption, dense)
    rates = (speed[None], diffusion[None], electron_rate[None], phonon_rate[None])

    def step(k, es, ps, before, behind, last, border):
        edges, width = len(border), widths[k]
        e_parts = NEXT_E_PARTS if edges else 1
        counts = (
            len(ps[0]), len(before[1]), len(behind[1]), len(es[0][0]), len(before[0]), len(behind[0]),
            len(border[0]) if edges else 0, e_parts,
        )
        operands = (
            places, *(x for parts, _ in es for x in parts), *(x for parts in ps for x in parts), *before[0],
            *before[1], *behind[0], *behind[1], *weights, ups[k], *rates, *(x for parts in border for x in parts),
        )
        large = n * counts[3] + len(ps) * counts[0] + sum(counts[1:3]) + sum(counts[4:6])
        specs = [SMEM] + [ANY] * large + [VMEM] * 8 + [ANY] * sum(len(parts) for parts in border)
        scratch = [
            pltpu.VMEM(shape, jnp.bfloat16)
            for shape in (
                (n * e, width), (len(ps) * p, width), (e + p, ny), (e + p, ny),
            )
        ]
        if last:
            out = tuple(jax.ShapeDtypeStruct((count, width), jnp.float32) for count in (e, p))
        else:
            out = (bf16(e // e_parts, nx * ny if edges else width),) * e_parts + (bf16(p, width),) + (bf16(e + p, ny),) * edges
            scratch += [pltpu.VMEM((e + p, ny), jnp.bfloat16)] * edges
        out = call(
            lambda *refs: step_kernel(n, e, p, width, ny, nx, k, [c for _, c in es], counts, edges, last, *refs),
            out, scratch, operands, specs, 24, "step", large + counts[6] + e_parts + 2,
        )
        return (list(out[:e_parts]), *out[e_parts:])

    def finish(far, rest, done):
        operands = (
            places, *far, *rest, absorption, dense, rates[2], rates[3], *(d[0][0] for d in done), *(d[1] for d in done),
        )
        return call(
            lambda *refs: finish_kernel(n, e, p, ny, nx, *refs), (bf16(e * nx, ny), bf16(p * nx, ny)),
            [pltpu.VMEM((len(far), p, widths[-1]), jnp.bfloat16), pltpu.VMEM((max(e, min(p, 256)) * nx, ny), jnp.float32)],
            operands, [SMEM] + [ANY] * len(far) + [VMEM] * (4 + 2 * CHUNKS), 24, "finish", len(far),
        )

    def gathered(own, far, wait_for):
        arrays = []
        for f in far:
            f = after(f, *wait_for)
            arrays += [f, swap_cores(f)]
        return [own, swap_cores(own)] + arrays

    halo = halos(to_a, to_b)
    far_p = [[[from_chip(x, d) for d in range(1, chips)] for x in parts] for parts in p_chunks]
    others = [near_e]
    for f in far_e:
        f = after(f, flat[0], *halo)
        others += [f, swap_cores(f)]
    others = call(
        lambda *refs: flatten_others_kernel(nx, ny, n - 1, *refs),
        (bf16(e, nx * ny),) * (n - 1),
        [pltpu.VMEM((e * nx, ny), jnp.bfloat16)] * (n - 1) + [lanes],
        [x.reshape(e * nx, ny) for x in others], [ANY] * (n - 1), 12, "flatten", n - 1,
    )
    everyone = [e_all, *others]
    waits = (dense, *halo)
    new = []
    for k in range(CHUNKS):
        ps = list(zip(*(gathered(x, far, waits) for x, far in zip(p_chunks[k], far_p[k]))))
        new.append(step(
            k, [([x], starts[k] * ny) for x in everyone], ps,
            ([e_all], p_chunks[k - 1]) if k else (halo[:1], halo[1:]),
            ([e_all], p_chunks[k + 1]) if k + 1 < CHUNKS else (halo[:1], halo[1:]), False,
            () if k + 1 < CHUNKS else (new[0][0], new[0][1:2]),
        ))
        waits = (new[-1][1],)
    halo = halos(new[-1][2], new[-1][3])
    e_next, p_next = new[-1][0], [c[1] for c in new]

    far_p = [[from_chip(x, d) for d in range(1, chips)] for x in p_next]
    first_p = gathered(p_next[0], far_p[0], (p_next[-1],))
    everyone = zip(*(gathered(x, [from_chip(x, d) for d in range(1, chips)], (first_p[-1], *halo)) for x in e_next))
    everyone = list(everyone)
    done = []
    for k in range(CHUNKS):
        last = k + 1 == CHUNKS
        es = [(parts, starts[k] * ny) for parts in everyone]
        ps = [p_next[k], swap_cores(p_next[k])] if last else first_p
        done.append(step(
            k, es, [[x] for x in ps], (e_next, p_next[k - 1 : k]) if k else (halo[:1], halo[1:]),
            (halo[:1], halo[1:]) if last else (e_next, p_next[k + 1 : k + 2]), last, (),
        ))
    rest = done.pop()
    far = []
    for f in far_p[-1]:
        f = after(f, rest[1], done[-1][1])
        far += [f, swap_cores(f)]
    e_out, p_out = finish(far, (rest[0][0], rest[1]), done)
    return e_out.reshape(e, nx, ny), p_out.reshape(p, nx, ny)


def solution(mesh):
    placed = (
        P("mode", ("grp", "space"), None),
        P("mode", ("grp", "space"), None),
        P("mode", None),
        P("mode", None),
        P("mode", None, None),
        P("mode", None),
        P(("grp", "space"), None),
        P("mode"),
        P("mode"),
        P("mode"),
        P("mode"),
    )
    return jax.shard_map(
        on_device,
        mesh=mesh,
        in_specs=placed,
        out_specs=(P("mode", ("grp", "space"), None), P("mode", ("grp", "space"), None)),
        check_vma=False,
    )
```

```python
import jax
import jax.numpy as jnp
from jax import lax
from jax.experimental import pallas as pl
from jax.experimental.pallas import tpu as pltpu
from jax.sharding import PartitionSpec as P

NM = 2048
BLK = 128
ITERS = 2
CORES = 2
TILE = 512
CHUNKS = 2
SHARES = (3, 5)
PARTS = (1, 1)
NEXT_E_PARTS = 1

VMEM = pl.BlockSpec(memory_space=pltpu.VMEM)
SMEM = pl.BlockSpec(memory_space=pltpu.SMEM)
ANY = pl.BlockSpec(memory_space=pl.ANY)
COST = pl.CostEstimate(flops=1000, bytes_accessed=1000, transcendentals=0)


def swap_cores(x):
    n = lax.axis_size("mode")
    return lax.ppermute(x, "mode", [(i, i ^ 1) for i in range(n)])


def from_chip(x, offset):
    n = lax.axis_size("mode")
    return lax.ppermute(x, "mode", [((i + CORES * offset) % n, i) for i in range(n)])


def halos(a, b):
    n = lax.axis_size("space")
    near = [(i, i ^ 1) for i in range(n) if i ^ 1 < n]
    other = [(i, i + 1 if i % 2 else i - 1) for i in range(n) if 0 <= (i + 1 if i % 2 else i - 1) < n]
    return lax.ppermute(a, "space", near), lax.ppermute(b, "space", other)


def after(x, *others):
    return lax.optimization_barrier((x, *others))[0]


def bf16(*shape):
    return jax.ShapeDtypeStruct(shape, jnp.bfloat16)


def call(kernel, out, scratch, operands, specs, megabytes, name, copies):
    return pl.pallas_call(
        kernel,
        out_shape=out,
        in_specs=specs,
        out_specs=(VMEM,) * len(out),
        scratch_shapes=[*scratch, pltpu.SemaphoreType.DMA((copies,))],
        compiler_params=pltpu.CompilerParams(vmem_limit_bytes=megabytes << 20),
        cost_estimate=COST,
        name=name,
    )(*operands)


class Loader:
    def __init__(self, sems):
        self.sems, self.used = sems, 0

    def start(self, src, dst):
        copy = pltpu.make_async_copy(src, dst, self.sems.at[self.used])
        self.used += 1
        copy.start()
        return copy

    def start_one(self, choose, src, other, dst):
        sem = self.sems.at[self.used]
        self.used += 1

        @pl.when(choose)
        def _():
            pltpu.make_async_copy(src, dst, sem).start()

        @pl.when(jnp.logical_not(choose))
        def _():
            pltpu.make_async_copy(other, dst, sem).start()

        return pltpu.make_async_copy(src, dst, sem)


def rows_at(index, count):
    return pl.ds(pl.multiple_of(index * count, count), count)


def rows_of(base, i, part):
    return pl.ds(base + i * part.shape[0], part.shape[0])


def as_column(row):
    return jnp.transpose(jnp.broadcast_to(row, (8, row.shape[1])))[:, 0:1]


def flatten_one(nx, ny, x_ref, outs, wide_ref):
    count = x_ref.shape[0] // nx
    chunk_of = [(k, c) for k, parts in enumerate(outs) for c in range(parts[0].shape[1] // ny)]
    tile = min([count, 64] + [out.shape[0] for parts in outs for out in parts])
    for at in range(0, count, tile):
        wide_ref[0 : tile * nx, :] = x_ref[at * nx : (at + tile) * nx, :].astype(jnp.float32)
        for r in range(nx):
            k, c = chunk_of[r]
            row = wide_ref[pl.ds(r, tile, stride=nx), :].astype(jnp.bfloat16)
            part, offset = divmod(at, outs[k][0].shape[0])
            outs[k][part][offset : offset + tile, c * ny : (c + 1) * ny] = row


def flatten_own_kernel(nx, ny, counts, place_ref, e_ref, p_ref, e_out_ref, *refs):
    *flat, a_ref, b_ref, e_in, p_in, wide_ref, sems = refs
    outs = []
    for count in counts:
        outs.append(flat[:count])
        flat = flat[count:]
    load = Loader(sems)
    e_copy, p_copy = load.start(e_ref, e_in), load.start(p_ref, p_in)
    e_copy.wait()
    flatten_one(nx, ny, e_in, [[e_out_ref]], wide_ref)
    p_copy.wait()
    flatten_one(nx, ny, p_in, outs, wide_ref)
    e = e_out_ref.shape[0]
    even = place_ref[0] == 0

    def put(to_ref, parts, col, e_col):
        to_ref[0:e, :] = e_out_ref[:, e_col : e_col + ny]
        at = e
        for part in parts:
            to_ref[at : at + part.shape[0], :] = part[:, col : col + ny]
            at += part.shape[0]

    for to_ref, last in ((a_ref, even), (b_ref, jnp.logical_not(even))):

        @pl.when(last)
        def _():
            put(to_ref, outs[-1], outs[-1][0].shape[1] - ny, (nx - 1) * ny)

        @pl.when(jnp.logical_not(last))
        def _():
            put(to_ref, outs[0], 0, 0)


def flatten_others_kernel(nx, ny, count, *refs):
    xs, outs, ins, (wide_ref, sems) = refs[:count], refs[count : 2 * count], refs[2 * count : -2], refs[-2:]
    load = Loader(sems)
    copies = [load.start(x, y) for x, y in zip(xs, ins)]
    for copy, x_ref, out_ref in zip(copies, ins, outs):
        copy.wait()
        flatten_one(nx, ny, x_ref, [[out_ref]], wide_ref)


def unflatten(olds, new, nx, ny, at, out_ref, wide_ref):
    count, row = new.shape[0], 0
    for chunk in [*(x.astype(jnp.float32) for x in olds), new]:
        for r in range(chunk.shape[1] // ny):
            wide_ref[pl.ds(row, count, stride=nx), :] = chunk[:, r * ny : (r + 1) * ny]
            row += 1
    out_ref[at * nx : (at + count) * nx, :] = wide_ref[0 : count * nx, :].astype(jnp.bfloat16)


def products(p, which, place_ref, p_refs):
    def product(weight_ref, at, count):
        total = 0.0
        for j, x_ref in zip(which, p_refs):
            columns = rows_at(place_ref[1 + j], p)
            total += jnp.dot(weight_ref[at : at + count, columns], x_ref[...], preferred_element_type=jnp.float32)
        return total

    return product


def add_kernel(e, p, which, place_ref, *refs):
    far_refs, (rest_e_ref, rest_p_ref, absorption_ref, dense_ref, e_out_ref, p_out_ref), scratch = (
        refs[: len(which)], refs[len(which) : len(which) + 6], refs[len(which) + 6 :]
    )
    load = Loader(scratch[-1])
    copies = [load.start(x, y) for x, y in zip(far_refs, scratch)]
    for copy in copies:
        copy.wait()
    product = products(p, which, place_ref, scratch[:-1])
    e_out_ref[...] = rest_e_ref[...] + 0.5 * product(absorption_ref, 0, e)
    p_out_ref[...] = rest_p_ref[...] + 0.5 * product(dense_ref, 0, p)


def finish_kernel(e, p, ny, nx, which, place_ref, *refs):
    far_refs, refs = refs[: len(which)], refs[len(which) :]
    rest_e_ref, rest_p_ref, absorption_ref, dense_ref, e_rate_ref, p_rate_ref = refs[:6]
    done_e, done_p, refs = refs[6 : 5 + CHUNKS], refs[5 + CHUNKS : 4 + 2 * CHUNKS], refs[4 + 2 * CHUNKS :]
    (e_out_ref, p_out_ref), scratch, wide_ref, sems = refs[:2], refs[2:-2], refs[-2], refs[-1]
    load = Loader(sems)
    copies = [load.start(x, y) for x, y in zip(far_refs, scratch)]
    for copy in copies:
        copy.wait()
    product = products(p, which, place_ref, scratch)
    tile = min(p, TILE)
    pieces = [(0, e, absorption_ref, rest_e_ref, e_rate_ref, done_e, e_out_ref)]
    pieces += [(at, tile, dense_ref, rest_p_ref, p_rate_ref, done_p, p_out_ref) for at in range(0, p, tile)]
    for at, count, weight_ref, rest_ref, rate_ref, done, out_ref in pieces:
        total = rest_ref[at : at + count, :] + 0.5 * product(weight_ref, at, count)
        new = total / (1.0 + as_column(rate_ref[:, at : at + count]))
        unflatten([x[at : at + count, :] for x in done], new, nx, ny, at, out_ref, wide_ref)


def step_kernel(n, e, p, width, ny, nx, k, cols, counts, edges, last, place_ref, *refs):
    refs = list(refs)

    def take(count):
        taken = refs[:count]
        del refs[:count]
        return taken

    e_refs, p_refs = [take(counts[3]) for _ in range(n)], [take(counts[0]) for _ in range(CORES if last else n)]
    before, behind = (take(counts[4]), take(counts[1])), (take(counts[5]), take(counts[2]))
    emission_ref, absorption_ref, dense_ref, up_ref, speed_ref, diffusion_ref, e_rate_ref, p_rate_ref = take(8)
    border = (take(counts[6]), take(1)) if edges else ()
    e_out_refs, p_out_ref = take(counts[7]), *take(1)
    to_refs = take(2) if edges else []
    se_ref, sp_ref, low_ref, high_ref = take(4)
    first_ref, final_ref = take(2) if edges else (None, None)
    load = Loader(refs[0])
    tall = width // ny
    even = place_ref[0] == 0
    me = place_ref[1]
    me_p = 0 if last else me

    early, middle = [], []
    for j, parts in enumerate(p_refs):
        owner = j if last else place_ref[1 + j]
        for i, part in enumerate(parts):
            early.append(load.start(part, sp_ref.at[rows_at(owner * counts[0] + i, p // counts[0]), :]))
    for j, parts in enumerate(e_refs):
        for i, part in enumerate(parts):
            to = se_ref.at[rows_at(place_ref[1 + j] * counts[3] + i, e // counts[3]), :]
            (middle if j else early).append(load.start(part.at[:, cols[j] : cols[j] + width], to))
    if k == 0:
        early.append(load.start_one(even, before[1][0], before[0][0], low_ref))
    else:
        col = cols[0] - ny
        for i, part in enumerate(before[0]):
            early.append(load.start(part.at[:, col : col + ny], low_ref.at[rows_of(0, i, part), :]))
        for i, part in enumerate(before[1]):
            early.append(load.start(part.at[:, part.shape[1] - ny :], low_ref.at[rows_of(e, i, part), :]))
    if k == CHUNKS - 1:
        early.append(load.start_one(even, behind[0][0], behind[1][0], high_ref))
    else:
        col = cols[0] + width
        for i, part in enumerate(behind[0]):
            early.append(load.start(part.at[:, col : col + ny], high_ref.at[rows_of(0, i, part), :]))
        for i, part in enumerate(behind[1]):
            early.append(load.start(part.at[:, 0:ny], high_ref.at[rows_of(e, i, part), :]))
    late = []
    if edges:
        for i, part in enumerate(border[0]):
            late.append(load.start(part.at[:, 0:ny], first_ref.at[rows_of(0, i, part), :]))
        for i, part in enumerate(e_out_refs):
            late.append(load.start(border[0][0].at[rows_of(0, i, part), :], part.at[:, 0 : part.shape[1] - width]))
        late.append(load.start(border[1][0].at[:, 0:ny], first_ref.at[e : e + p, :]))
    tile = min(p, TILE)

    def around(x_ref, rows, base):
        own = x_ref[rows, :].astype(jnp.float32)
        low, high = low_ref[base, :].astype(jnp.float32), high_ref[base, :].astype(jnp.float32)
        lower = jnp.concatenate([low, own[:, : width - ny]], axis=1) if width > ny else low
        higher = jnp.concatenate([own[:, ny:], high], axis=1) if width > ny else high
        return own, lower, higher

    def store(new, at, count, base):
        new = new.astype(jnp.bfloat16)
        if base:
            p_out_ref[at : at + count, :] = new
        else:
            for i, part in enumerate(e_out_refs):
                columns = slice(part.shape[1] - width, part.shape[1])
                part[:, columns] = new[i * part.shape[0] : (i + 1) * part.shape[0], :]
        if edges:
            final_ref[base + at : base + at + count, :] = new[:, width - ny :]

    def product(weight_ref, at, count):
        if not last:
            return jnp.dot(weight_ref[at : at + count, :], sp_ref[...], preferred_element_type=jnp.float32)
        total = 0.0
        for j in range(CORES):
            weight = weight_ref[at : at + count, rows_at(place_ref[1 + j], p)]
            total += jnp.dot(weight, sp_ref[j * p : (j + 1) * p, :], preferred_element_type=jnp.float32)
        return total

    for copy in early:
        copy.wait()
    gain = product(absorption_ref, 0, e)
    own, lower, higher = around(se_ref, rows_at(me, e), pl.ds(0, e))
    f_up = jnp.where(up_ref[...] == 1, lower, higher)
    new = own - as_column(speed_ref[...]) * (own - f_up) + 0.5 * gain
    if last:
        e_out_refs[0][...] = new
    else:
        store(new / (1.0 + as_column(e_rate_ref[...])), 0, e, 0)
    for copy in middle + late:
        copy.wait()

    for at in range(0, p, tile):
        source = product(dense_ref, at, tile) + jnp.dot(
            emission_ref[at : at + tile, :], se_ref[...], preferred_element_type=jnp.float32
        )
        rows = pl.ds(pl.multiple_of(me_p * p + at, tile), tile)
        own, lower, higher = around(sp_ref, rows, pl.ds(e + at, tile))
        column = lax.broadcasted_iota(jnp.int32, (tile, ny), 1)
        left, right = [], []
        for r in range(tall):
            row = own[:, r * ny : (r + 1) * ny]
            left.append(jnp.where(column == 0, 0.0, pltpu.roll(row, 1, 1)))
            right.append(jnp.where(column == ny - 1, 0.0, pltpu.roll(row, ny - 1, 1)))
        left, right = jnp.concatenate(left, axis=1), jnp.concatenate(right, axis=1)
        lap = lower + higher + left + right - 4.0 * own
        diffusion, rate = as_column(diffusion_ref[:, at : at + tile]), as_column(p_rate_ref[:, at : at + tile])
        new = own + diffusion * lap + 0.5 * source
        if last:
            p_out_ref[at : at + tile, :] = new
        else:
            store(new / (1.0 + rate), at, tile, e)

    if edges:
        for to_ref, is_final in ((to_refs[0], even), (to_refs[1], jnp.logical_not(even))):

            @pl.when(is_final)
            def _():
                to_ref[...] = final_ref[...]

            @pl.when(jnp.logical_not(is_final))
            def _():
                to_ref[...] = first_ref[...]


def on_device(
    electrons,
    phonons,
    emission,
    absorption,
    block_coupling,
    block_cols,
    upwind,
    speed,
    diffusion,
    electron_rate,
    phonon_rate,
):
    e, nx, ny = electrons.shape
    p = phonons.shape[0]
    n = lax.axis_size("mode")
    chips = n // CORES
    slots = block_coupling.shape[1]
    b_rows = p // BLK
    talls = [nx * share // sum(SHARES) for share in SHARES]
    starts = [sum(talls[:k]) for k in range(CHUNKS)]
    widths = [tall * ny for tall in talls]
    lanes = pltpu.VMEM((64 * nx, ny), jnp.float32)
    me, space = (lax.axis_index(a).astype(jnp.uint32) for a in ("mode", "space"))
    chip, core = me // CORES, me % CORES
    places = [space % 2] + [((chip + d) % chips) * CORES + (core ^ c) for d in range(chips) for c in range(CORES)]

    places = jnp.stack(places).astype(jnp.int32)

    near_e = swap_cores(electrons)
    far_e = [from_chip(electrons, d) for d in range(1, chips)]
    e_all, *flat, to_a, to_b = call(
        lambda *refs: flatten_own_kernel(nx, ny, PARTS, *refs),
        (bf16(e, nx * ny),) + tuple(bf16(p // count, width) for count, width in zip(PARTS, widths) for _ in range(count))
        + (bf16(e + p, ny),) * 2,
        [pltpu.VMEM((e * nx, ny), jnp.bfloat16), pltpu.VMEM((p * nx, ny), jnp.bfloat16), lanes],
        (places, electrons.reshape(e * nx, ny), phonons.reshape(p * nx, ny)), [SMEM, ANY, ANY], 8, "flatten", 2,
    )
    p_chunks = [flat[sum(PARTS[:k]) : sum(PARTS[: k + 1])] for k in range(CHUNKS)]
    block_coupling = after(block_coupling, flat[0])
    kernel = block_coupling.reshape(b_rows, BLK, slots, BLK)
    block_ids = jnp.arange(NM // BLK, dtype=jnp.int32)
    hits = (block_cols[:, :, None] == block_ids[None, None, :]).astype(jnp.bfloat16)
    dense = jnp.einsum(
        "bsk,bisj->bikj", hits, kernel, preferred_element_type=jnp.float32
    ).astype(jnp.bfloat16).reshape(p, NM)

    ups = [upwind[a : a + tall].reshape(1, tall * ny) for a, tall in zip(starts, talls)]
    weights = (emission, absorption, dense)
    rates = (speed[None], diffusion[None], electron_rate[None], phonon_rate[None])

    def step(k, es, ps, before, behind, last, border):
        edges, width = len(border), widths[k]
        e_parts = NEXT_E_PARTS if edges else 1
        counts = (
            len(ps[0]), len(before[1]), len(behind[1]), len(es[0][0]), len(before[0]), len(behind[0]),
            len(border[0]) if edges else 0, e_parts,
        )
        operands = (
            places, *(x for parts, _ in es for x in parts), *(x for parts in ps for x in parts), *before[0],
            *before[1], *behind[0], *behind[1], *weights, ups[k], *rates, *(x for parts in border for x in parts),
        )
        large = n * counts[3] + len(ps) * counts[0] + sum(counts[1:3]) + sum(counts[4:6])
        specs = [SMEM] + [ANY] * large + [VMEM] * 8 + [ANY] * sum(len(parts) for parts in border)
        scratch = [
            pltpu.VMEM(shape, jnp.bfloat16)
            for shape in (
                (n * e, width), (len(ps) * p, width), (e + p, ny), (e + p, ny),
            )
        ]
        if last:
            out = tuple(jax.ShapeDtypeStruct((count, width), jnp.float32) for count in (e, p))
        else:
            out = (bf16(e // e_parts, nx * ny if edges else width),) * e_parts + (bf16(p, width),) + (bf16(e + p, ny),) * edges
            scratch += [pltpu.VMEM((e + p, ny), jnp.bfloat16)] * edges
        out = call(
            lambda *refs: step_kernel(n, e, p, width, ny, nx, k, [c for _, c in es], counts, edges, last, *refs),
            out, scratch, operands, specs, 24, "step", large + counts[6] + e_parts + 2,
        )
        return (list(out[:e_parts]), *out[e_parts:])

    def add(far, which, rest):
        return call(
            lambda *refs: add_kernel(e, p, which, *refs),
            tuple(jax.ShapeDtypeStruct((count, widths[-1]), jnp.float32) for count in (e, p)),
            [pltpu.VMEM((p, widths[-1]), jnp.bfloat16) for _ in far], (places, *far, *rest, absorption, dense),
            [SMEM] + [ANY] * len(far) + [VMEM] * 4, 20, "add", len(far),
        )

    def finish(far, which, rest, done):
        operands = (
            places, *far, *rest, absorption, dense, rates[2], rates[3], *(d[0][0] for d in done), *(d[1] for d in done),
        )
        return call(
            lambda *refs: finish_kernel(e, p, ny, nx, which, *refs), (bf16(e * nx, ny), bf16(p * nx, ny)),
            [pltpu.VMEM((p, widths[-1]), jnp.bfloat16) for _ in far]
            + [pltpu.VMEM((max(e, min(p, TILE)) * nx, ny), jnp.float32)],
            operands, [SMEM] + [ANY] * len(far) + [VMEM] * (4 + 2 * CHUNKS), 24, "finish", len(far),
        )

    def gathered(own, far, wait_for):
        arrays = []
        for f in far:
            f = after(f, *wait_for)
            arrays += [f, swap_cores(f)]
        return [own, swap_cores(own)] + arrays

    halo = halos(to_a, to_b)
    far_p = [[[from_chip(x, d) for d in range(1, chips)] for x in parts] for parts in p_chunks]
    others = [near_e]
    for f in far_e:
        f = after(f, flat[0], *halo)
        others += [f, swap_cores(f)]
    others = call(
        lambda *refs: flatten_others_kernel(nx, ny, n - 1, *refs),
        (bf16(e, nx * ny),) * (n - 1),
        [pltpu.VMEM((e * nx, ny), jnp.bfloat16)] * (n - 1) + [lanes],
        [x.reshape(e * nx, ny) for x in others], [ANY] * (n - 1), 12, "flatten", n - 1,
    )
    everyone = [e_all, *others]
    waits = (dense, *halo)
    new = []
    for k in range(CHUNKS):
        ps = list(zip(*(gathered(x, far, waits) for x, far in zip(p_chunks[k], far_p[k]))))
        new.append(step(
            k, [([x], starts[k] * ny) for x in everyone], ps,
            ([e_all], p_chunks[k - 1]) if k else (halo[:1], halo[1:]),
            ([e_all], p_chunks[k + 1]) if k + 1 < CHUNKS else (halo[:1], halo[1:]), False,
            () if k + 1 < CHUNKS else (new[0][0], new[0][1:2]),
        ))
        waits = (new[-1][1],)
    halo = halos(new[-1][2], new[-1][3])
    e_next, p_next = new[-1][0], [c[1] for c in new]

    far_p = [[from_chip(x, d) for d in range(1, chips)] for x in p_next]
    first_p = gathered(p_next[0], far_p[0], (p_next[-1],))
    everyone = zip(*(gathered(x, [from_chip(x, d) for d in range(1, chips)], (first_p[-1], *halo)) for x in e_next))
    everyone = list(everyone)
    done = []
    for k in range(CHUNKS):
        last = k + 1 == CHUNKS
        es = [(parts, starts[k] * ny) for parts in everyone]
        ps = [p_next[k], swap_cores(p_next[k])] if last else first_p
        done.append(step(
            k, es, [[x] for x in ps], (e_next, p_next[k - 1 : k]) if k else (halo[:1], halo[1:]),
            (halo[:1], halo[1:]) if last else (e_next, p_next[k + 1 : k + 2]), last, (),
        ))
    rest = done.pop()
    far = [after(f, rest[1], done[-1][1]) for f in far_p[-1]]
    passed = [swap_cores(f) for f in far]
    direct = [CORES * (d + 1) for d in range(len(far))]
    rest = add(far, direct, (rest[0][0], rest[1]))
    e_out, p_out = finish(passed, [j + 1 for j in direct], rest, done)
    return e_out.reshape(e, nx, ny), p_out.reshape(p, nx, ny)


def solution(mesh):
    placed = (
        P("mode", ("grp", "space"), None),
        P("mode", ("grp", "space"), None),
        P("mode", None),
        P("mode", None),
        P("mode", None, None),
        P("mode", None),
        P(("grp", "space"), None),
        P("mode"),
        P("mode"),
        P("mode"),
        P("mode"),
    )
    return jax.shard_map(
        on_device,
        mesh=mesh,
        in_specs=placed,
        out_specs=(P("mode", ("grp", "space"), None), P("mode", ("grp", "space"), None)),
        check_vma=False,
    )
```

```python
import jax
import jax.numpy as jnp
from jax import lax
from jax.experimental import pallas as pl
from jax.experimental.pallas import tpu as pltpu
from jax.sharding import PartitionSpec as P

NM = 2048
BLK = 128
ITERS = 2
CORES = 2
TILE = 512
LAST_TILE = 256
CHUNKS = 2
SHARES = (3, 5)
PARTS = (1, 1)
NEXT_E_PARTS = 1

VMEM = pl.BlockSpec(memory_space=pltpu.VMEM)
SMEM = pl.BlockSpec(memory_space=pltpu.SMEM)
ANY = pl.BlockSpec(memory_space=pl.ANY)
COST = pl.CostEstimate(flops=1000, bytes_accessed=1000, transcendentals=0)


def swap_cores(x):
    n = lax.axis_size("mode")
    return lax.ppermute(x, "mode", [(i, i ^ 1) for i in range(n)])


def from_chip(x, offset):
    n = lax.axis_size("mode")
    return lax.ppermute(x, "mode", [((i + CORES * offset) % n, i) for i in range(n)])


def halos(a, b):
    n = lax.axis_size("space")
    near = [(i, i ^ 1) for i in range(n) if i ^ 1 < n]
    other = [(i, i + 1 if i % 2 else i - 1) for i in range(n) if 0 <= (i + 1 if i % 2 else i - 1) < n]
    return lax.ppermute(a, "space", near), lax.ppermute(b, "space", other)


def after(x, *others):
    return lax.optimization_barrier((x, *others))[0]


def bf16(*shape):
    return jax.ShapeDtypeStruct(shape, jnp.bfloat16)


def call(kernel, out, scratch, operands, specs, megabytes, name, copies, out_spec=VMEM):
    return pl.pallas_call(
        kernel,
        out_shape=out,
        in_specs=specs,
        out_specs=(out_spec,) * len(out),
        scratch_shapes=[*scratch, pltpu.SemaphoreType.DMA((copies,))],
        compiler_params=pltpu.CompilerParams(vmem_limit_bytes=megabytes << 20),
        cost_estimate=COST,
        name=name,
    )(*operands)


class Loader:
    def __init__(self, sems):
        self.sems, self.used = sems, 0

    def start(self, src, dst):
        copy = pltpu.make_async_copy(src, dst, self.sems.at[self.used])
        self.used += 1
        copy.start()
        return copy

    def start_one(self, choose, src, other, dst):
        sem = self.sems.at[self.used]
        self.used += 1

        @pl.when(choose)
        def _():
            pltpu.make_async_copy(src, dst, sem).start()

        @pl.when(jnp.logical_not(choose))
        def _():
            pltpu.make_async_copy(other, dst, sem).start()

        return pltpu.make_async_copy(src, dst, sem)


def rows_at(index, count):
    return pl.ds(pl.multiple_of(index * count, count), count)


def rows_of(base, i, part):
    return pl.ds(base + i * part.shape[0], part.shape[0])


def as_column(row):
    return jnp.transpose(jnp.broadcast_to(row, (8, row.shape[1])))[:, 0:1]


def flatten_one(nx, ny, x_ref, outs, wide_ref):
    count = x_ref.shape[0] // nx
    chunk_of = [(k, c) for k, parts in enumerate(outs) for c in range(parts[0].shape[1] // ny)]
    tile = min([count, 64] + [out.shape[0] for parts in outs for out in parts])
    for at in range(0, count, tile):
        wide_ref[0 : tile * nx, :] = x_ref[at * nx : (at + tile) * nx, :].astype(jnp.float32)
        for r in range(nx):
            k, c = chunk_of[r]
            row = wide_ref[pl.ds(r, tile, stride=nx), :].astype(jnp.bfloat16)
            part, offset = divmod(at, outs[k][0].shape[0])
            outs[k][part][offset : offset + tile, c * ny : (c + 1) * ny] = row


def flatten_own_kernel(nx, ny, counts, place_ref, e_ref, p_ref, e_out_ref, *refs):
    *flat, a_ref, b_ref, e_in, p_in, wide_ref, sems = refs
    outs = []
    for count in counts:
        outs.append(flat[:count])
        flat = flat[count:]
    load = Loader(sems)
    e_copy, p_copy = load.start(e_ref, e_in), load.start(p_ref, p_in)
    e_copy.wait()
    flatten_one(nx, ny, e_in, [[e_out_ref]], wide_ref)
    p_copy.wait()
    flatten_one(nx, ny, p_in, outs, wide_ref)
    e = e_out_ref.shape[0]
    even = place_ref[0] == 0

    def put(to_ref, parts, col, e_col):
        to_ref[0:e, :] = e_out_ref[:, e_col : e_col + ny]
        at = e
        for part in parts:
            to_ref[at : at + part.shape[0], :] = part[:, col : col + ny]
            at += part.shape[0]

    for to_ref, last in ((a_ref, even), (b_ref, jnp.logical_not(even))):

        @pl.when(last)
        def _():
            put(to_ref, outs[-1], outs[-1][0].shape[1] - ny, (nx - 1) * ny)

        @pl.when(jnp.logical_not(last))
        def _():
            put(to_ref, outs[0], 0, 0)


def flatten_others_kernel(nx, ny, count, *refs):
    xs, outs, ins, (wide_ref, sems) = refs[:count], refs[count : 2 * count], refs[2 * count : -2], refs[-2:]
    load = Loader(sems)
    copies = [load.start(x, y) for x, y in zip(xs, ins)]
    for copy, x_ref, out_ref in zip(copies, ins, outs):
        copy.wait()
        flatten_one(nx, ny, x_ref, [[out_ref]], wide_ref)


def unflatten(olds, new, nx, ny, at, out_ref, wide_ref):
    count, row = new.shape[0], 0
    for chunk in [*(x.astype(jnp.float32) for x in olds), new]:
        for r in range(chunk.shape[1] // ny):
            wide_ref[pl.ds(row, count, stride=nx), :] = chunk[:, r * ny : (r + 1) * ny]
            row += 1
    out_ref[at * nx : (at + count) * nx, :] = wide_ref[0 : count * nx, :].astype(jnp.bfloat16)


def products(p, which, place_ref, p_refs):
    def product(weight_ref, at, count):
        total = 0.0
        for j, x_ref in zip(which, p_refs):
            columns = rows_at(place_ref[1 + j], p)
            total += jnp.dot(weight_ref[at : at + count, columns], x_ref[...], preferred_element_type=jnp.float32)
        return total

    return product


def add_kernel(e, p, which, place_ref, *refs):
    far_refs, (rest_e_ref, rest_p_ref, absorption_ref, dense_ref, e_out_ref, p_out_ref), scratch = (
        refs[: len(which)], refs[len(which) : len(which) + 6], refs[len(which) + 6 :]
    )
    load = Loader(scratch[-1])
    copies = [load.start(x, y) for x, y in zip(far_refs, scratch)]
    for copy in copies:
        copy.wait()
    product = products(p, which, place_ref, scratch[:-1])
    e_out_ref[...] = rest_e_ref[...] + 0.5 * product(absorption_ref, 0, e)
    p_out_ref[...] = rest_p_ref[...] + 0.5 * product(dense_ref, 0, p)


def finish_kernel(e, p, ny, nx, which, place_ref, *refs):
    far_refs, refs = refs[: len(which)], refs[len(which) :]
    rest_e_ref, rest_p_ref, absorption_ref, dense_ref, e_rate_ref, p_rate_ref = refs[:6]
    done_e, done_p, refs = refs[6 : 5 + CHUNKS], refs[5 + CHUNKS : 4 + 2 * CHUNKS], refs[4 + 2 * CHUNKS :]
    (e_hbm, p_hbm), scratch, (e_out_ref, p_out_ref, wide_ref, sems) = refs[:2], refs[2:-4], refs[-4:]
    load = Loader(sems)
    copies = [load.start(x, y) for x, y in zip(far_refs, scratch)]
    for copy in copies:
        copy.wait()
    product = products(p, which, place_ref, scratch)
    tile, stores = min(p, LAST_TILE), []
    pieces = [(0, e, absorption_ref, rest_e_ref, e_rate_ref, done_e, e_out_ref, e_hbm)]
    pieces += [(at, tile, dense_ref, rest_p_ref, p_rate_ref, done_p, p_out_ref, p_hbm) for at in range(0, p, tile)]
    for at, count, weight_ref, rest_ref, rate_ref, done, out_ref, hbm_ref in pieces:
        total = rest_ref[at : at + count, :] + 0.5 * product(weight_ref, at, count)
        new = total / (1.0 + as_column(rate_ref[:, at : at + count]))
        unflatten([x[at : at + count, :] for x in done], new, nx, ny, at, out_ref, wide_ref)
        rows = pl.ds(at * nx, count * nx)
        stores.append(load.start(out_ref.at[rows, :], hbm_ref.at[rows, :]))
    for copy in stores:
        copy.wait()


def step_kernel(n, e, p, width, ny, nx, k, cols, counts, edges, last, only, place_ref, *refs):
    refs = list(refs)

    def take(count):
        taken = refs[:count]
        del refs[:count]
        return taken

    e_refs, p_refs = [take(counts[3]) for _ in range(n)], [take(counts[0]) for _ in range(CORES if last else n)]
    before, behind = (take(counts[4]), take(counts[1])), (take(counts[5]), take(counts[2]))
    emission_ref, absorption_ref, dense_ref, up_ref, speed_ref, diffusion_ref, e_rate_ref, p_rate_ref = take(8)
    border = (take(counts[6]), take(1)) if edges else ()
    next_refs = take(counts[7]) if only == "p" else []
    e_out_refs = take(counts[7]) if only != "p" else []
    (p_out_ref,) = take(1) if only != "e" else [None]
    rims = edges and only != "e"
    to_refs = take(2) if rims else []
    se_ref, sp_ref, low_ref, high_ref = take(4)
    first_ref, final_ref = take(2) if rims else (None, None)
    load = Loader(refs[0])
    tall = width // ny
    even = place_ref[0] == 0
    me = place_ref[1]
    me_p = 0 if last else me

    early, middle = [], []
    for j, parts in enumerate(p_refs):
        owner = j if last else place_ref[1 + j]
        for i, part in enumerate(parts):
            early.append(load.start(part, sp_ref.at[rows_at(owner * counts[0] + i, p // counts[0]), :]))
    for j, parts in enumerate(e_refs[:1] if only == "e" else e_refs):
        for i, part in enumerate(parts):
            to = se_ref.at[rows_at(place_ref[1 + j] * counts[3] + i, e // counts[3]), :]
            (middle if j else early).append(load.start(part.at[:, cols[j] : cols[j] + width], to))
    if k == 0:
        early.append(load.start_one(even, before[1][0], before[0][0], low_ref))
    else:
        col = cols[0] - ny
        for i, part in enumerate(before[0]):
            early.append(load.start(part.at[:, col : col + ny], low_ref.at[rows_of(0, i, part), :]))
        for i, part in enumerate(before[1]):
            early.append(load.start(part.at[:, part.shape[1] - ny :], low_ref.at[rows_of(e, i, part), :]))
    if k == CHUNKS - 1:
        early.append(load.start_one(even, behind[0][0], behind[1][0], high_ref))
    else:
        col = cols[0] + width
        for i, part in enumerate(behind[0]):
            early.append(load.start(part.at[:, col : col + ny], high_ref.at[rows_of(0, i, part), :]))
        for i, part in enumerate(behind[1]):
            early.append(load.start(part.at[:, 0:ny], high_ref.at[rows_of(e, i, part), :]))
    late = []
    if edges:
        for i, part in enumerate(e_out_refs):
            late.append(load.start(border[0][0].at[rows_of(0, i, part), :], part.at[:, 0 : part.shape[1] - width]))
    if rims:
        for i, part in enumerate(border[0]):
            late.append(load.start(part.at[:, 0:ny], first_ref.at[rows_of(0, i, part), :]))
        late.append(load.start(border[1][0].at[:, 0:ny], first_ref.at[e : e + p, :]))
        for i, part in enumerate(next_refs):
            late.append(load.start(part.at[:, part.shape[1] - ny :], final_ref.at[rows_of(0, i, part), :]))
    tile = min(p, TILE)

    def around(x_ref, rows, base):
        own = x_ref[rows, :].astype(jnp.float32)
        low, high = low_ref[base, :].astype(jnp.float32), high_ref[base, :].astype(jnp.float32)
        lower = jnp.concatenate([low, own[:, : width - ny]], axis=1) if width > ny else low
        higher = jnp.concatenate([own[:, ny:], high], axis=1) if width > ny else high
        return own, lower, higher

    def store(new, at, count, base):
        new = new.astype(jnp.bfloat16)
        if base:
            p_out_ref[at : at + count, :] = new
        else:
            for i, part in enumerate(e_out_refs):
                columns = slice(part.shape[1] - width, part.shape[1])
                part[:, columns] = new[i * part.shape[0] : (i + 1) * part.shape[0], :]
        if rims:
            final_ref[base + at : base + at + count, :] = new[:, width - ny :]

    def product(weight_ref, at, count):
        if not last:
            return jnp.dot(weight_ref[at : at + count, :], sp_ref[...], preferred_element_type=jnp.float32)
        total = 0.0
        for j in range(CORES):
            weight = weight_ref[at : at + count, rows_at(place_ref[1 + j], p)]
            total += jnp.dot(weight, sp_ref[j * p : (j + 1) * p, :], preferred_element_type=jnp.float32)
        return total

    for copy in early:
        copy.wait()
    if only != "p":
        gain = product(absorption_ref, 0, e)
        own, lower, higher = around(se_ref, rows_at(me, e), pl.ds(0, e))
        f_up = jnp.where(up_ref[...] == 1, lower, higher)
        new = own - as_column(speed_ref[...]) * (own - f_up) + 0.5 * gain
        if last:
            e_out_refs[0][...] = new
        else:
            store(new / (1.0 + as_column(e_rate_ref[...])), 0, e, 0)
    for copy in middle + late:
        copy.wait()

    for at in range(0, 0 if only == "e" else p, tile):
        source = product(dense_ref, at, tile) + jnp.dot(
            emission_ref[at : at + tile, :], se_ref[...], preferred_element_type=jnp.float32
        )
        rows = pl.ds(pl.multiple_of(me_p * p + at, tile), tile)
        own, lower, higher = around(sp_ref, rows, pl.ds(e + at, tile))
        column = lax.broadcasted_iota(jnp.int32, (tile, ny), 1)
        left, right = [], []
        for r in range(tall):
            row = own[:, r * ny : (r + 1) * ny]
            left.append(jnp.where(column == 0, 0.0, pltpu.roll(row, 1, 1)))
            right.append(jnp.where(column == ny - 1, 0.0, pltpu.roll(row, ny - 1, 1)))
        left, right = jnp.concatenate(left, axis=1), jnp.concatenate(right, axis=1)
        lap = lower + higher + left + right - 4.0 * own
        diffusion, rate = as_column(diffusion_ref[:, at : at + tile]), as_column(p_rate_ref[:, at : at + tile])
        new = own + diffusion * lap + 0.5 * source
        if last:
            p_out_ref[at : at + tile, :] = new
        else:
            store(new / (1.0 + rate), at, tile, e)

    if rims:
        for to_ref, is_final in ((to_refs[0], even), (to_refs[1], jnp.logical_not(even))):

            @pl.when(is_final)
            def _():
                to_ref[...] = final_ref[...]

            @pl.when(jnp.logical_not(is_final))
            def _():
                to_ref[...] = first_ref[...]


def on_device(
    electrons,
    phonons,
    emission,
    absorption,
    block_coupling,
    block_cols,
    upwind,
    speed,
    diffusion,
    electron_rate,
    phonon_rate,
):
    e, nx, ny = electrons.shape
    p = phonons.shape[0]
    n = lax.axis_size("mode")
    chips = n // CORES
    slots = block_coupling.shape[1]
    b_rows = p // BLK
    talls = [nx * share // sum(SHARES) for share in SHARES]
    starts = [sum(talls[:k]) for k in range(CHUNKS)]
    widths = [tall * ny for tall in talls]
    lanes = pltpu.VMEM((64 * nx, ny), jnp.float32)
    me, space = (lax.axis_index(a).astype(jnp.uint32) for a in ("mode", "space"))
    chip, core = me // CORES, me % CORES
    places = [space % 2] + [((chip + d) % chips) * CORES + (core ^ c) for d in range(chips) for c in range(CORES)]

    places = jnp.stack(places).astype(jnp.int32)

    near_e = swap_cores(electrons)
    far_e = [from_chip(electrons, d) for d in range(1, chips)]
    e_all, *flat, to_a, to_b = call(
        lambda *refs: flatten_own_kernel(nx, ny, PARTS, *refs),
        (bf16(e, nx * ny),) + tuple(bf16(p // count, width) for count, width in zip(PARTS, widths) for _ in range(count))
        + (bf16(e + p, ny),) * 2,
        [pltpu.VMEM((e * nx, ny), jnp.bfloat16), pltpu.VMEM((p * nx, ny), jnp.bfloat16), lanes],
        (places, electrons.reshape(e * nx, ny), phonons.reshape(p * nx, ny)), [SMEM, ANY, ANY], 8, "flatten", 2,
    )
    p_chunks = [flat[sum(PARTS[:k]) : sum(PARTS[: k + 1])] for k in range(CHUNKS)]
    block_coupling = after(block_coupling, flat[0])
    kernel = block_coupling.reshape(b_rows, BLK, slots, BLK)
    block_ids = jnp.arange(NM // BLK, dtype=jnp.int32)
    hits = (block_cols[:, :, None] == block_ids[None, None, :]).astype(jnp.bfloat16)
    dense = jnp.einsum(
        "bsk,bisj->bikj", hits, kernel, preferred_element_type=jnp.float32
    ).astype(jnp.bfloat16).reshape(p, NM)

    ups = [upwind[a : a + tall].reshape(1, tall * ny) for a, tall in zip(starts, talls)]
    weights = (emission, absorption, dense)
    rates = (speed[None], diffusion[None], electron_rate[None], phonon_rate[None])

    def step(k, es, ps, before, behind, last, border, only=None, nexts=()):
        edges, width = len(border), widths[k]
        e_parts = NEXT_E_PARTS if edges else 1
        counts = (
            len(ps[0]), len(before[1]), len(behind[1]), len(es[0][0]), len(before[0]), len(behind[0]),
            len(border[0]) if edges else 0, e_parts,
        )
        operands = (
            places, *(x for parts, _ in es for x in parts), *(x for parts in ps for x in parts), *before[0],
            *before[1], *behind[0], *behind[1], *weights, ups[k], *rates, *(x for parts in border for x in parts), *nexts,
        )
        large = n * counts[3] + len(ps) * counts[0] + sum(counts[1:3]) + sum(counts[4:6])
        specs = [SMEM] + [ANY] * large + [VMEM] * 8 + [ANY] * (sum(len(parts) for parts in border) + len(nexts))
        scratch = [
            pltpu.VMEM(shape, jnp.bfloat16)
            for shape in (
                (n * e, width), (len(ps) * p, width), (e + p, ny), (e + p, ny),
            )
        ]
        if last:
            out = tuple(jax.ShapeDtypeStruct((count, width), jnp.float32) for count in (e, p))
        else:
            out_e = (bf16(e // e_parts, nx * ny if edges else width),) * e_parts
            out_p = (bf16(p, width),) + (bf16(e + p, ny),) * edges
            out = out_e if only == "e" else out_p if only == "p" else out_e + out_p
            scratch += [pltpu.VMEM((e + p, ny), jnp.bfloat16)] * (0 if only == "e" else edges)
        out = call(
            lambda *refs: step_kernel(n, e, p, width, ny, nx, k, [c for _, c in es], counts, edges, last, only, *refs),
            out, scratch, operands, specs, 24, "step", large + counts[6] + 2 * e_parts + 2,
        )
        return out if only else (list(out[:e_parts]), *out[e_parts:])

    def add(far, which, rest):
        return call(
            lambda *refs: add_kernel(e, p, which, *refs),
            tuple(jax.ShapeDtypeStruct((count, widths[-1]), jnp.float32) for count in (e, p)),
            [pltpu.VMEM((p, widths[-1]), jnp.bfloat16) for _ in far], (places, *far, *rest, absorption, dense),
            [SMEM] + [ANY] * len(far) + [VMEM] * 4, 20, "add", len(far),
        )

    def finish(far, which, rest, done):
        operands = (
            places, *far, *rest, absorption, dense, rates[2], rates[3], *(d[0][0] for d in done), *(d[1] for d in done),
        )
        return call(
            lambda *refs: finish_kernel(e, p, ny, nx, which, *refs), (bf16(e * nx, ny), bf16(p * nx, ny)),
            [pltpu.VMEM((p, widths[-1]), jnp.bfloat16) for _ in far]
            + [pltpu.VMEM((count * nx, ny), jnp.bfloat16) for count in (e, p)]
            + [pltpu.VMEM((max(e, min(p, LAST_TILE)) * nx, ny), jnp.float32)],
            operands, [SMEM] + [ANY] * len(far) + [VMEM] * (4 + 2 * CHUNKS), 24, "finish",
            len(far) + 1 + p // min(p, LAST_TILE), ANY,
        )

    def gathered(own, far, wait_for):
        arrays = []
        for f in far:
            f = after(f, *wait_for)
            arrays += [f, swap_cores(f)]
        return [own, swap_cores(own)] + arrays

    halo = halos(to_a, to_b)
    far_p = [[[from_chip(x, d) for d in range(1, chips)] for x in parts] for parts in p_chunks]
    others = [near_e]
    for f in far_e:
        f = after(f, flat[0], *halo)
        others += [f, swap_cores(f)]
    others = call(
        lambda *refs: flatten_others_kernel(nx, ny, n - 1, *refs),
        (bf16(e, nx * ny),) * (n - 1),
        [pltpu.VMEM((e * nx, ny), jnp.bfloat16)] * (n - 1) + [lanes],
        [x.reshape(e * nx, ny) for x in others], [ANY] * (n - 1), 12, "flatten", n - 1,
    )
    everyone = [e_all, *others]
    waits = (dense, *halo)
    new = []
    for k in range(CHUNKS):
        ps = list(zip(*(gathered(x, far, waits) for x, far in zip(p_chunks[k], far_p[k]))))
        operands = (
            k, [([x], starts[k] * ny) for x in everyone], ps,
            ([e_all], p_chunks[k - 1]) if k else (halo[:1], halo[1:]),
            ([e_all], p_chunks[k + 1]) if k + 1 < CHUNKS else (halo[:1], halo[1:]), False,
        )
        if k + 1 < CHUNKS:
            new.append(step(*operands, ()))
        else:
            border = (new[0][0], new[0][1:2])
            e_new = step(*operands, border, "e")
            new.append((list(e_new), *step(*operands, border, "p", e_new)))
        waits = (new[-1][1],)
    halo = halos(new[-1][2], new[-1][3])
    e_next, p_next = new[-1][0], [c[1] for c in new]

    far_p = [[from_chip(x, d) for d in range(1, chips)] for x in p_next]
    first_p = gathered(p_next[0], far_p[0], (p_next[-1],))
    everyone = zip(*(gathered(x, [from_chip(x, d) for d in range(1, chips)], (first_p[-1], *halo)) for x in e_next))
    everyone = list(everyone)
    done = []
    for k in range(CHUNKS):
        last = k + 1 == CHUNKS
        es = [(parts, starts[k] * ny) for parts in everyone]
        ps = [p_next[k], swap_cores(p_next[k])] if last else first_p
        done.append(step(
            k, es, [[x] for x in ps], (e_next, p_next[k - 1 : k]) if k else (halo[:1], halo[1:]),
            (halo[:1], halo[1:]) if last else (e_next, p_next[k + 1 : k + 2]), last, (),
        ))
    rest = done.pop()
    far = [after(f, rest[1], done[-1][1]) for f in far_p[-1]]
    passed = [swap_cores(f) for f in far]
    direct = [CORES * (d + 1) for d in range(len(far))]
    rest = add(far, direct, (rest[0][0], rest[1]))
    e_out, p_out = finish(passed, [j + 1 for j in direct], rest, done)
    return e_out.reshape(e, nx, ny), p_out.reshape(p, nx, ny)


def solution(mesh):
    placed = (
        P("mode", ("grp", "space"), None),
        P("mode", ("grp", "space"), None),
        P("mode", None),
        P("mode", None),
        P("mode", None, None),
        P("mode", None),
        P(("grp", "space"), None),
        P("mode"),
        P("mode"),
        P("mode"),
        P("mode"),
    )
    return jax.shard_map(
        on_device,
        mesh=mesh,
        in_specs=placed,
        out_specs=(P("mode", ("grp", "space"), None), P("mode", ("grp", "space"), None)),
        check_vma=False,
    )
```
